32 devices in a mesh: dp: 8 (over z, y), tensor: 4 (over x, core).
Axes of the slice: x: 2, y: 2, z: 4, core: 2. Of those that a mesh axis runs over, the one named last changes fastest.
Arguments:
- hidden: bfloat16 [5120, 1152], P(('dp', 'tensor')), may hold values from -6 to 6
- in_gain: bfloat16 [1152], P('dp'), may hold values from 0.25 to 1.75
- w_query: bfloat16 [1152, 1024], P('dp', 'tensor'), may hold values from -0.1875 to 0.1875
- w_key: bfloat16 [1152, 256], P('dp'), may hold values from -0.1875 to 0.1875
- w_value: bfloat16 [1152, 256], P('dp'), may hold values from -0.1875 to 0.1875
- query_gain: bfloat16 [256], P('dp'), may hold values from 0.25 to 1.75
- key_gain: bfloat16 [256], P('dp'), may hold values from 0.25 to 1.75
- w_output: bfloat16 [1024, 1152], P('tensor', 'dp'), may hold values from -0.1875 to 0.1875
- attn_gain: bfloat16 [1152], P('dp'), may hold values from 0.25 to 1.75
- ffn_gain: bfloat16 [1152], P('dp'), may hold values from 0.25 to 1.75
- w_gate: bfloat16 [1152, 6912], P('dp', 'tensor'), may hold values from -0.1875 to 0.1875
- w_up: bfloat16 [1152, 6912], P('dp', 'tensor'), may hold values from -0.1875 to 0.1875
- w_down: bfloat16 [6912, 1152], P('tensor', 'dp'), may hold values from -0.078125 to 0.078125
- out_gain: bfloat16 [1152], P('dp'), may hold values from 0.25 to 1.75
- cotangent: bfloat16 [5120, 1152], P(('dp', 'tensor')), may hold values from -6 to 6
- segment_ids: int32 [5120], P('dp'), may hold values from 0 to 5119, as said below
- positions: int32 [5120], P('dp'), may hold values from 0 to 1999, as said below
Outputs:
- output: bfloat16 [5120, 1152], P(('dp', 'tensor'))
- grad_hidden: float32 [5120, 1152], P(('dp', 'tensor'))
- grad_in_gain: float32 [1152], P('dp')
- grad_w_query: float32 [1152, 1024], P('dp', 'tensor')
- grad_w_key: float32 [1152, 256], P('dp')
- grad_w_value: float32 [1152, 256], P('dp')
- grad_query_gain: float32 [256], P('dp')
- grad_key_gain: float32 [256], P('dp')
- grad_w_output: float32 [1024, 1152], P('tensor', 'dp')
- grad_attn_gain: float32 [1152], P('dp')
- grad_ffn_gain: float32 [1152], P('dp')
- grad_w_gate: float32 [1152, 6912], P('dp', 'tensor')
- grad_w_up: float32 [1152, 6912], P('dp', 'tensor')
- grad_w_down: float32 [6912, 1152], P('tensor', 'dp')
- grad_out_gain: float32 [1152], P('dp')
The draws below stay inside these ranges and needn't reach their ends.
Inputs may be any that keep to these rules, and one draw needn't show every extreme that they name: `segment_ids`: segment ids never fall along the tokens and are equal exactly within a document; a document's id is the index of its first token, except that the document holding the last token has id 5120 - 1; every document holds 200 to 2000 tokens, except that the last may be cut short by the end of the array, and one document holds exactly 2000; documents may run across the bounds of packed sequences. `positions`: the offset of each token from the first token of its document.
All inputs are finite; a program needn't handle non-finite values.
Results may differ from the reference program's by a relative error of at most 0.025.
Values may be sent and summed in bfloat16 or wider, within the bound.
A program may use at most 128 MiB of HBM per device.

```python
import jax
import jax.numpy as jnp
from jax import lax

D = 1152
FF = 6912
H = 4
HD = 256
WINDOW = 512
SEQ = 640
DOC_LEAST = 200
DOC_MOST = 2000
TOKENS = 5120
N_DP = 8
N_TENSOR = 4


def document_layout(key):
    doc_slots = TOKENS // DOC_LEAST + 1
    lengths = jax.random.randint(jax.random.fold_in(key, 11), (doc_slots,), DOC_LEAST, DOC_MOST + 1)
    chosen = jax.random.randint(jax.random.fold_in(key, 12), (), 0, max(TOKENS // DOC_MOST - 1, 1))
    slot_index = jnp.arange(doc_slots, dtype=jnp.int32)
    lengths = jnp.where(slot_index == chosen, DOC_MOST, lengths).astype(jnp.int32)
    ends = jnp.cumsum(lengths)
    starts = ends - lengths
    token_index = jnp.arange(TOKENS, dtype=jnp.int32)
    begin = jnp.max(jnp.where(starts[None, :] <= token_index[:, None], starts[None, :], 0), axis=1)
    finish = jnp.min(jnp.where(ends[None, :] > token_index[:, None], ends[None, :], 4 * TOKENS + 4 * DOC_MOST), axis=1)
    segment = jnp.where(finish >= TOKENS, TOKENS - 1, begin)
    return (segment.astype(jnp.int32), (token_index - begin).astype(jnp.int32))


def draw_segment_ids(key, part):
    return document_layout(key)[0]


def draw_positions(key, part):
    return document_layout(key)[1]


def strengthened(drawn, rng, source, target, shards_of, factor):
    def block_of(axis_at):
        return (jnp.arange(drawn.shape[axis_at]) // (drawn.shape[axis_at] // shards_of)).reshape((-1,) + (1,) * (drawn.ndim - 1 - axis_at))

    one_side = jax.random.permutation(rng, shards_of)[block_of(target)]
    second = (block_of(target) + shards_of // 2) % shards_of
    return jnp.where((block_of(source) == one_side) | (block_of(source) == second), factor * drawn, drawn)


def levels(own_key, dims, shards, smallest, top_value):
    gain = 1.0
    for dim, blocks in shards:
        heights = jax.random.uniform(jax.random.fold_in(jax.random.fold_in(own_key, 6), dim), (blocks,), jnp.float32, smallest / len(shards), top_value / len(shards))
        gain = gain * jnp.repeat(jnp.exp(heights), dims[dim] // blocks).reshape((-1,) + (1,) * (len(dims) - 1 - dim))
    return gain


def gaussian(stream_key, shape, scale, most, split=(), kind=jnp.bfloat16):
    drawn = jax.random.normal(stream_key, shape, jnp.float32) * scale
    if len(split) > 0:
        drawn = levels(stream_key, shape, split, -0.22, 0.18) * drawn
    return jnp.clip(drawn, min=-most, max=most).astype(kind)


def heavy_noise(key, shape, deviation, most, cuts, heavy, held_as=jnp.bfloat16):
    values = deviation * jax.random.normal(key, shape, jnp.float32)
    if cuts:
        values = values * levels(key, shape, cuts, -0.22, 0.18)
    return jnp.clip(strengthened(values, jax.random.fold_in(key, 3), *heavy), -most, most).astype(held_as)


def setup_inputs(seed: int = 0) -> dict:
    seeds = jax.random.split(jax.random.key(seed), 18)
    hidden = heavy_noise(seeds[0], (TOKENS, D), 1.0, 6.0, ((0, 32),), (0, 1, 32, 2.75))
    in_gain = jnp.clip(1.0 + 0.15 * jax.random.normal(seeds[1], (D,), jnp.float32), 0.25, 1.75).astype(jnp.bfloat16)
    w_query = gaussian(seeds[2], (D, H * HD), D ** -0.5, 0.1875, ((0, 8), (1, 4)))
    w_key = gaussian(seeds[3], (D, HD), D ** -0.5, 0.1875, ((0, 8),))
    w_value = gaussian(seeds[4], (D, HD), D ** -0.5, 0.1875, ((0, 8),))
    query_gain = jnp.clip(1.0 + 0.15 * jax.random.normal(seeds[5], (HD,), jnp.float32), 0.25, 1.75).astype(jnp.bfloat16)
    key_gain = jnp.clip(1.0 + 0.15 * jax.random.normal(seeds[6], (HD,), jnp.float32), 0.25, 1.75).astype(jnp.bfloat16)
    w_output = gaussian(seeds[7], (H * HD, D), (H * HD) ** -0.5, 0.1875, ((0, 4), (1, 8)))
    attn_gain = jnp.clip(1.0 + 0.15 * jax.random.normal(seeds[8], (D,), jnp.float32), 0.25, 1.75).astype(jnp.bfloat16)
    ffn_gain = jnp.clip(1.0 + 0.15 * jax.random.normal(seeds[9], (D,), jnp.float32), 0.25, 1.75).astype(jnp.bfloat16)
    w_gate = gaussian(seeds[10], (D, FF), D ** -0.5, 0.1875, ((0, 8), (1, 4)))
    w_up = gaussian(seeds[11], (D, FF), D ** -0.5, 0.1875, ((0, 8), (1, 4)))
    w_down = gaussian(seeds[12], (FF, D), FF ** -0.5, 0.078125, ((0, 4), (1, 8)))
    out_gain = jnp.clip(1.0 + 0.15 * jax.random.normal(seeds[13], (D,), jnp.float32), 0.25, 1.75).astype(jnp.bfloat16)
    cotangent = heavy_noise(seeds[14], (TOKENS, D), 1.0, 6.0, ((0, 32),), (0, 1, 32, 2.75))
    segment_ids = draw_segment_ids(jax.random.fold_in(seeds[17], 71), 0)
    positions = draw_positions(jax.random.fold_in(seeds[17], 71), 0)
    return {"hidden": hidden, "in_gain": in_gain, "w_query": w_query, "w_key": w_key, "w_value": w_value, "query_gain": query_gain, "key_gain": key_gain, "w_output": w_output, "attn_gain": attn_gain, "ffn_gain": ffn_gain, "w_gate": w_gate, "w_up": w_up, "w_down": w_down, "out_gain": out_gain, "cotangent": cotangent, "segment_ids": segment_ids, "positions": positions}


EPSILON = 1e-06
ROPE_BASE = 10000.0

def rms_scale(values):
    return lax.rsqrt(lax.optimization_barrier(jnp.mean(values * values, axis=-1, keepdims=True)) + EPSILON)

def apply_norm(values, gain_vec):
    return values * rms_scale(values) * gain_vec.astype(jnp.float32)

def norm_back(values, gain_vec, upstream):
    factor = rms_scale(values)
    unit_rows = values * factor
    scaled = upstream * gain_vec.astype(jnp.float32)
    grad_values = factor * (scaled - unit_rows * lax.optimization_barrier(jnp.mean(scaled * unit_rows, axis=-1, keepdims=True)))
    return (grad_values, upstream * unit_rows)

def rotary_tables(token_pos, width):
    steps_half = jnp.arange(width // 2, dtype=jnp.float32)
    frequency = ROPE_BASE ** (-2.0 * steps_half / width)
    angles = token_pos.astype(jnp.float32)[:, None] * frequency[None, :]
    return (jnp.cos(angles), jnp.sin(angles))

def rotate(values, cosine, sine_table):
    half_width = values.shape[-1] // 2
    first_half = values[..., :half_width]
    second = values[..., half_width:]
    return jnp.concatenate([first_half * cosine - second * sine_table, second * cosine + first_half * sine_table], axis=-1)

def window_mask(seq_ids):
    length_seq = seq_ids.shape[0]
    token_index = jnp.arange(length_seq, dtype=jnp.int32)
    behind = token_index[:, None] - token_index[None, :]
    return (seq_ids[:, None] == seq_ids[None, :]) & (behind >= 0) & (behind < WINDOW)

def gelu_tanh(values):
    return jax.nn.gelu(values, approximate=True)

def round_low(values):
    return lax.optimization_barrier(values.astype(jnp.bfloat16)).astype(jnp.float32)

def token_partials(term):
    blocks = term.reshape(N_TENSOR, SEQ // N_TENSOR, term.shape[-1])
    return lax.optimization_barrier(jnp.sum(round_low(lax.optimization_barrier(jnp.sum(blocks, axis=1))), axis=0))

def head_partials(term):
    groups = term.reshape(SEQ, N_TENSOR, H // N_TENSOR, HD)
    return lax.optimization_barrier(jnp.sum(round_low(lax.optimization_barrier(jnp.sum(groups, axis=(0, 2)))), axis=0))

def reference(hidden, in_gain, w_query, w_key, w_value, query_gain, key_gain, w_output, attn_gain, ffn_gain, w_gate, w_up, w_down, out_gain, cotangent, segment_ids, positions):
    factor = HD ** (-0.5)

    def one_sequence(totals, inputs):
        rows_in, rows_cot, seq_ids, seq_pos = inputs
        hidden_f = rows_in.astype(jnp.float32)
        normed_in = apply_norm(hidden_f, in_gain).astype(jnp.bfloat16)
        query_raw = jnp.dot(normed_in, w_query, preferred_element_type=jnp.float32).reshape(SEQ, H, HD)
        key_raw = jnp.dot(normed_in, w_key, preferred_element_type=jnp.float32)
        value_rows = jnp.dot(normed_in, w_value, preferred_element_type=jnp.float32).astype(jnp.bfloat16)
        cosine, sine_table = rotary_tables(seq_pos, HD)
        query_rot = rotate(apply_norm(query_raw, query_gain), cosine[:, None, :], sine_table[:, None, :]).astype(jnp.bfloat16)
        key_rot = rotate(apply_norm(key_raw, key_gain), cosine, sine_table).astype(jnp.bfloat16)
        allowed = window_mask(seq_ids)[None]
        scores = jnp.einsum('qhd,kd->hqk', query_rot.astype(jnp.float32), key_rot.astype(jnp.float32)) * factor
        log_total = jnp.log(lax.optimization_barrier(jnp.sum(jnp.where(allowed, jnp.exp(scores), 0.0), axis=-1, keepdims=True)))
        probs = jnp.where(allowed, jnp.exp(scores - log_total), 0.0)
        probs_low = probs.astype(jnp.bfloat16)
        context = jnp.einsum('hqk,kd->qhd', probs_low.astype(jnp.float32), value_rows.astype(jnp.float32))
        context = context.reshape(SEQ, H * HD).astype(jnp.bfloat16)
        attn_rows = jnp.dot(context, w_output, preferred_element_type=jnp.float32)
        residual = hidden_f + apply_norm(attn_rows, attn_gain)
        ffn_in = apply_norm(residual, ffn_gain).astype(jnp.bfloat16)
        gate_pre = jnp.dot(ffn_in, w_gate, preferred_element_type=jnp.float32)
        up_pre = jnp.dot(ffn_in, w_up, preferred_element_type=jnp.float32)
        gelu_values, gelu_back = jax.vjp(gelu_tanh, gate_pre)
        mixed = (gelu_values * up_pre).astype(jnp.bfloat16)
        down_rows = jnp.dot(mixed, w_down, preferred_element_type=jnp.float32)
        out_rows = (residual + apply_norm(down_rows, out_gain)).astype(jnp.bfloat16)
        cot_f = rows_cot.astype(jnp.float32)
        grad_down, term_out = norm_back(down_rows, out_gain, cot_f)
        down_low = grad_down.astype(jnp.bfloat16)
        grad_wd = jnp.dot(mixed.T, down_low, preferred_element_type=jnp.float32)
        grad_mixed = jnp.dot(down_low, w_down.T, preferred_element_type=jnp.float32)
        gate_low = gelu_back(grad_mixed * up_pre)[0].astype(jnp.bfloat16)
        up_low = (grad_mixed * gelu_values).astype(jnp.bfloat16)
        grad_wg = jnp.dot(ffn_in.T, gate_low, preferred_element_type=jnp.float32)
        grad_wu = jnp.dot(ffn_in.T, up_low, preferred_element_type=jnp.float32)
        ffn_back = jnp.dot(gate_low, w_gate.T, preferred_element_type=jnp.float32) + jnp.dot(up_low, w_up.T, preferred_element_type=jnp.float32)
        resid_norm, term_ffn = norm_back(residual, ffn_gain, ffn_back)
        grad_residual = cot_f + resid_norm
        grad_attn, term_attn = norm_back(attn_rows, attn_gain, grad_residual)
        attn_low = grad_attn.astype(jnp.bfloat16)
        grad_wo = jnp.dot(context.T, attn_low, preferred_element_type=jnp.float32)
        grad_context = jnp.dot(attn_low, w_output.T, preferred_element_type=jnp.float32).astype(jnp.bfloat16)
        grad_context = grad_context.reshape(SEQ, H, HD).astype(jnp.float32)
        grad_probs = jnp.einsum('qhd,kd->hqk', grad_context, value_rows.astype(jnp.float32))
        delta = lax.optimization_barrier(jnp.sum(probs * grad_probs, axis=-1, keepdims=True))
        grad_scores = (probs * (grad_probs - delta) * factor).astype(jnp.bfloat16).astype(jnp.float32)
        value_heads = jnp.einsum('hqk,qhd->khd', probs_low.astype(jnp.float32), grad_context).astype(jnp.bfloat16)
        grad_qrot = jnp.einsum('hqk,kd->qhd', grad_scores, key_rot.astype(jnp.float32))
        grad_kheads = jnp.einsum('hqk,qhd->khd', grad_scores, query_rot.astype(jnp.float32))
        grad_qraw, term_qgain = norm_back(query_raw, query_gain, rotate(grad_qrot, cosine[:, None, :], -sine_table[:, None, :]))
        grad_kraw, term_kgain = norm_back(key_raw[:, None, :], key_gain, rotate(grad_kheads, cosine[:, None, :], -sine_table[:, None, :]))
        query_low = grad_qraw.astype(jnp.bfloat16).reshape(SEQ, H * HD)
        key_low = grad_kraw.astype(jnp.bfloat16).astype(jnp.float32)
        value_low = value_heads.astype(jnp.float32)
        normed_f = normed_in.astype(jnp.float32)
        grad_wq = jnp.dot(normed_in.T, query_low, preferred_element_type=jnp.float32)
        key_groups = key_low.reshape(SEQ, N_TENSOR, H // N_TENSOR, HD)
        value_groups = value_low.reshape(SEQ, N_TENSOR, H // N_TENSOR, HD)
        grad_wk = lax.optimization_barrier(jnp.sum(round_low(jnp.einsum('sd,sghe->gde', normed_f, key_groups)), axis=0))
        grad_wv = lax.optimization_barrier(jnp.sum(round_low(jnp.einsum('sd,sghe->gde', normed_f, value_groups)), axis=0))
        attn_back = jnp.dot(query_low, w_query.T, preferred_element_type=jnp.float32)
        attn_back = attn_back + jnp.einsum('she,de->sd', key_low, w_key.astype(jnp.float32))
        attn_back = attn_back + jnp.einsum('she,de->sd', value_low, w_value.astype(jnp.float32))
        in_norm, term_in = norm_back(hidden_f, in_gain, attn_back)
        grad_rows = grad_residual + in_norm
        terms = (token_partials(term_in), round_low(grad_wq), grad_wk, grad_wv, head_partials(term_qgain), head_partials(term_kgain), round_low(grad_wo), token_partials(term_attn), token_partials(term_ffn), round_low(grad_wg), round_low(grad_wu), round_low(grad_wd), token_partials(term_out))
        updated = tuple((running + fresh for running, fresh in zip(totals, terms)))
        return (updated, (out_rows, grad_rows))
    shapes = ((D,), (D, H * HD), (D, HD), (D, HD), (HD,), (HD,), (H * HD, D), (D,), (D,), (D, FF), (D, FF), (FF, D), (D,))
    start_totals = tuple((jnp.zeros(shape_one, jnp.float32) for shape_one in shapes))
    inputs = (hidden.reshape(N_DP, SEQ, D), cotangent.reshape(N_DP, SEQ, D), segment_ids.reshape(N_DP, SEQ), positions.reshape(N_DP, SEQ))
    totals, stacked = lax.scan(one_sequence, start_totals, inputs)
    output = stacked[0].reshape(TOKENS, D)
    grad_hidden = stacked[1].reshape(TOKENS, D)
    return (output, grad_hidden, totals[0], totals[1], totals[2], totals[3], totals[4], totals[5], totals[6], totals[7], totals[8], totals[9], totals[10], totals[11], totals[12])
```

```python
import functools

import jax
import jax.numpy as jnp
from jax import lax
from jax.experimental import pallas as pl
from jax.experimental.pallas import tpu as pltpu
from jax.sharding import PartitionSpec as P

HD = 256
WINDOW = 512


EPSILON = 1e-06
ROPE_BASE = 10000.0


def rms_scale(values):
    return lax.rsqrt(jnp.mean(values * values, axis=-1, keepdims=True) + EPSILON)


def apply_norm(values, gain_vec):
    return values * rms_scale(values) * gain_vec.astype(jnp.float32)


def norm_back(values, gain_vec, upstream):
    factor = rms_scale(values)
    unit_rows = values * factor
    scaled = upstream * gain_vec.astype(jnp.float32)
    grad_values = factor * (
        scaled - unit_rows * jnp.mean(scaled * unit_rows, axis=-1, keepdims=True)
    )
    return (grad_values, upstream * unit_rows)


def rotary_tables(token_pos, width):
    steps_half = jnp.arange(width // 2, dtype=jnp.float32)
    frequency = ROPE_BASE ** (-2.0 * steps_half / width)
    angles = token_pos.astype(jnp.float32)[:, None] * frequency[None, :]
    return (jnp.cos(angles), jnp.sin(angles))


def rotate(values, cosine, sine_table):
    half_width = values.shape[-1] // 2
    first_half = values[..., :half_width]
    second = values[..., half_width:]
    return jnp.concatenate(
        [first_half * cosine - second * sine_table, second * cosine + first_half * sine_table],
        axis=-1,
    )


def window_mask(seq_ids):
    length_seq = seq_ids.shape[0]
    token_index = jnp.arange(length_seq, dtype=jnp.int32)
    behind = token_index[:, None] - token_index[None, :]
    return (seq_ids[:, None] == seq_ids[None, :]) & (behind >= 0) & (behind < WINDOW)


def gelu_tanh(values):
    return jax.nn.gelu(values, approximate=True)


def contract_rows(left, right):
    return lax.dot_general(
        left, right, (((0,), (0,)), ((), ())), preferred_element_type=jnp.float32
    )


def contract_cols(left, right):
    return lax.dot_general(
        left, right, (((1,), (1,)), ((), ())), preferred_element_type=jnp.float32
    )


MESH = pl.DeviceIdType.MESH
LANES = 128
SUBLANES = 16
MIB = 1024 * 1024


def send_to(where, src, dst, send, recv):
    return pltpu.make_async_remote_copy(
        src_ref=src,
        dst_ref=dst,
        send_sem=send,
        recv_sem=recv,
        device_id=where,
        device_id_type=MESH,
    )


def meet(partners):
    barrier = pltpu.get_barrier_semaphore()
    for where in partners:
        pl.semaphore_signal(barrier, inc=1, device_id=where, device_id_type=MESH)
    pl.semaphore_wait(barrier, len(partners))


class Spot:
    def __init__(self, n_dp):
        self.n_rest = n_dp // 4
        self.dp = lax.axis_index("dp")
        self.t = lax.axis_index("tensor")
        self.x = self.t // 2
        self.core = self.t - 2 * self.x
        self.line = self.dp // self.n_rest
        self.rest = self.dp - self.line * self.n_rest
        self.half = self.line % 2
        high = self.line // 2
        self.lines = [
            self.line,
            2 * high + 1 - self.half,
            2 * (1 - high) + self.half,
            2 * (1 - high) + 1 - self.half,
        ]
        self.line_dp = [line * self.n_rest + self.rest for line in self.lines]
        self.line_at = [{"dp": dp} for dp in self.line_dp]
        self.rests = [(self.rest + r) % self.n_rest for r in range(self.n_rest)]
        self.rest_at = [{"dp": self.line * self.n_rest + rest} for rest in self.rests]
        self.from_rest = [
            (self.rest + self.n_rest - r) % self.n_rest for r in range(self.n_rest)
        ]
        self.t_mate = 2 * self.x + 1 - self.core
        self.t_side = 2 * (1 - self.x) + self.core
        self.t_side_mate = 2 * (1 - self.x) + 1 - self.core
        self.mate = {"tensor": self.t_mate}
        self.side = {"tensor": self.t_side}
        self.pair = self.line_at[1]


def row_pieces(rows, wanted):
    cuts = wanted if rows % (wanted * SUBLANES) == 0 else 1
    size = rows // cuts
    return [(cut * size, size) for cut in range(cuts)]


def gather8_body(n_dp, pieces, mine, full, own_sem, xs, xr, zs, zr, ds, dr, ms, mr):
    at = Spot(n_dp)
    meet([at.mate, at.side, at.pair])
    half, other = at.half, 1 - at.half

    def cut(ref, p):
        return ref.at[pl.ds(*pieces[p])]

    def over_x(p):
        return send_to(at.side, cut(mine, p), cut(full.at[half, at.t], p), xs.at[p], xr.at[p])

    def over_z(p):
        return send_to(at.pair, cut(mine, p), cut(full.at[half, at.t], p), zs.at[p], zr.at[p])

    def onward(p):
        if p % 2 == 0:
            block = cut(full.at[half, at.t_side], p)
            return send_to(at.pair, block, block, ds.at[p], dr.at[p])
        block = cut(full.at[other, at.t], p)
        return send_to(at.side, block, block, ds.at[p], dr.at[p])

    def near(j, p):
        place = cut(full.at[(half, half, other, other)[j], (at.t, at.t_side, at.t, at.t_side)[j]], p)
        source = cut(mine, p) if j == 0 else place
        return send_to(at.mate, source, place, ms.at[j, p], mr.at[j, p])

    count = len(pieces)
    for p in range(count):
        over_x(p).start()
        over_z(p).start()
    own = pltpu.make_async_copy(mine, full.at[half, at.t], own_sem)
    own.start()
    for p in range(count):
        near(0, p).start()
    for p in range(count):
        over_x(p).wait_recv()
        if p % 2 == 0:
            onward(p).start()
        near(1, p).start()
        over_z(p).wait_recv()
        if p % 2 == 1:
            onward(p).start()
        near(2, p).start()
    for p in range(count):
        onward(p).wait_recv()
        near(3, p).start()
    own.wait()
    for p in range(count):
        over_x(p).wait_send()
        over_z(p).wait_send()
        onward(p).wait_send()
        for j in range(4):
            near(j, p).wait()


def gather8(n_dp, block, ident):
    pieces = row_pieces(block.shape[0], 10)
    count = len(pieces)
    one = pltpu.SemaphoreType.DMA((count,))
    four = pltpu.SemaphoreType.DMA((4, count))
    return pl.pallas_call(
        functools.partial(gather8_body, n_dp, pieces),
        out_shape=jax.ShapeDtypeStruct((2, 4, *block.shape), block.dtype),
        in_specs=[pl.BlockSpec(memory_space=pltpu.VMEM)],
        out_specs=pl.BlockSpec(memory_space=pl.ANY),
        scratch_shapes=[pltpu.SemaphoreType.DMA, one, one, one, one, one, one, four, four],
        compiler_params=pltpu.CompilerParams(collective_id=ident, has_side_effects=True),
        name=f"gather8_{ident}",
    )(block)


def gather4_body(n_dp, pieces, mine, full, own_sem, xs, xr, ms, mr):
    at = Spot(n_dp)
    meet([at.mate, at.side])

    def cut(ref, p):
        return ref.at[pl.ds(*pieces[p])]

    def over_x(p):
        return send_to(at.side, cut(mine, p), cut(full.at[at.t], p), xs.at[p], xr.at[p])

    def near(j, p):
        place = cut(full.at[(at.t, at.t_side)[j]], p)
        source = cut(mine, p) if j == 0 else place
        return send_to(at.mate, source, place, ms.at[j, p], mr.at[j, p])

    count = len(pieces)
    for p in range(count):
        over_x(p).start()
    own = pltpu.make_async_copy(mine, full.at[at.t], own_sem)
    own.start()
    for p in range(count):
        near(0, p).start()
    for p in range(count):
        over_x(p).wait_recv()
        near(1, p).start()
    own.wait()
    for p in range(count):
        over_x(p).wait_send()
        for j in range(2):
            near(j, p).wait()


def gather4(n_dp, block, ident):
    pieces = row_pieces(block.shape[0], 10)
    count = len(pieces)
    one = pltpu.SemaphoreType.DMA((count,))
    two = pltpu.SemaphoreType.DMA((2, count))
    return pl.pallas_call(
        functools.partial(gather4_body, n_dp, pieces),
        out_shape=jax.ShapeDtypeStruct((4, *block.shape), block.dtype),
        in_specs=[pl.BlockSpec(memory_space=pltpu.VMEM)],
        out_specs=pl.BlockSpec(memory_space=pl.ANY),
        scratch_shapes=[pltpu.SemaphoreType.DMA, one, one, two, two],
        compiler_params=pltpu.CompilerParams(collective_id=ident, has_side_effects=True),
        name=f"gather4_{ident}",
    )(block)


def add_up(left, right):
    return left.astype(jnp.float32) + right.astype(jnp.float32)


def scatter8_body(
    n_dp, pieces, parts, out, held, come, last, ms, mr, fs, fr, ls, lr
):
    at = Spot(n_dp)
    meet([at.mate, at.side, at.pair])
    half, other = at.half, 1 - at.half
    halves = (half, half, other, other)
    mine_t = (at.t, at.t_side, at.t, at.t_side)
    mate_t = (at.t_mate, at.t_side_mate, at.t_mate, at.t_side_mate)
    count = len(pieces)

    def near(k, p):
        rows = pl.ds(*pieces[p])
        return send_to(
            at.mate, parts.at[halves[k], mate_t[k], rows], held.at[k, rows], ms.at[k, p], mr.at[k, p]
        )

    def first(j, p):
        rows = pl.ds(*pieces[p])
        if p % 2 == 0:
            return send_to(at.side, held.at[(1, 3)[j], rows], come.at[j, rows], fs.at[j, p], fr.at[j, p])
        return send_to(at.pair, held.at[(2, 3)[j], rows], come.at[j, rows], fs.at[j, p], fr.at[j, p])

    def second(p):
        rows = pl.ds(*pieces[p])
        if p % 2 == 0:
            return send_to(at.pair, held.at[2, rows], last.at[rows], ls.at[p], lr.at[p])
        return send_to(at.side, held.at[1, rows], last.at[rows], ls.at[p], lr.at[p])

    for p in range(count):
        for k in (3, 1, 2, 0):
            near(k, p).start()
    for p in range(count):
        rows = pl.ds(*pieces[p])
        for k in (3, 1, 2, 0):
            near(k, p).wait_recv()
            held[k, rows] = add_up(parts[halves[k], mine_t[k], rows], held[k, rows]).astype(jnp.bfloat16)
        first(1, p).start()
        first(0, p).start()
    for p in range(count):
        rows = pl.ds(*pieces[p])
        keep = 2 if p % 2 == 0 else 1
        first(1, p).wait_recv()
        held[keep, rows] = add_up(held[keep, rows], come[1, rows]).astype(jnp.bfloat16)
        second(p).start()
        first(0, p).wait_recv()
        out[rows] = add_up(held[0, rows], come[0, rows])
    for p in range(count):
        rows = pl.ds(*pieces[p])
        second(p).wait_recv()
        out[rows] = out[rows] + last[rows].astype(jnp.float32)
    for p in range(count):
        for k in range(4):
            near(k, p).wait_send()
        for j in range(2):
            first(j, p).wait_send()
        second(p).wait_send()


def scatter8(n_dp, parts, ident):
    rows, width = parts.shape[2:]
    pieces = row_pieces(rows, 10)
    count = len(pieces)

    def sems(*shape):
        return pltpu.SemaphoreType.DMA((*shape, count))

    return pl.pallas_call(
        functools.partial(scatter8_body, n_dp, pieces),
        out_shape=jax.ShapeDtypeStruct((rows, width), jnp.float32),
        in_specs=[pl.BlockSpec(memory_space=pltpu.VMEM)],
        out_specs=pl.BlockSpec(memory_space=pltpu.VMEM),
        scratch_shapes=[
            pltpu.VMEM((4, rows, width), jnp.bfloat16),
            pltpu.VMEM((2, rows, width), jnp.bfloat16),
            pltpu.VMEM((rows, width), jnp.bfloat16),
            sems(4), sems(4), sems(2), sems(2), sems(), sems(),
        ],
        compiler_params=pltpu.CompilerParams(
            collective_id=ident, has_side_effects=True, vmem_limit_bytes=40 * MIB
        ),
        name=f"scatter8_{ident}",
    )(parts)


def scatter4_body(n_dp, pieces, parts, out, held, come, ms, mr, fs, fr):
    at = Spot(n_dp)
    meet([at.mate, at.side])
    mine_t = (at.t, at.t_side)
    mate_t = (at.t_mate, at.t_side_mate)
    count = len(pieces)

    def near(k, p):
        rows = pl.ds(*pieces[p])
        return send_to(at.mate, parts.at[mate_t[k], rows], held.at[k, rows], ms.at[k, p], mr.at[k, p])

    def first(p):
        rows = pl.ds(*pieces[p])
        return send_to(at.side, held.at[1, rows], come.at[rows], fs.at[p], fr.at[p])

    for p in range(count):
        for k in (1, 0):
            near(k, p).start()
    for p in range(count):
        rows = pl.ds(*pieces[p])
        near(1, p).wait_recv()
        held[1, rows] = add_up(parts[mine_t[1], rows], held[1, rows]).astype(jnp.bfloat16)
        first(p).start()
        near(0, p).wait_recv()
        out[rows] = add_up(parts[mine_t[0], rows], held[0, rows])
    for p in range(count):
        rows = pl.ds(*pieces[p])
        first(p).wait_recv()
        out[rows] = out[rows] + come[rows].astype(jnp.float32)
    for p in range(count):
        for k in range(2):
            near(k, p).wait_send()
        first(p).wait_send()


def scatter4(n_dp, parts, ident):
    rows, width = parts.shape[1:]
    pieces = row_pieces(rows, 10)
    count = len(pieces)

    def sems(*shape):
        return pltpu.SemaphoreType.DMA((*shape, count))

    return pl.pallas_call(
        functools.partial(scatter4_body, n_dp, pieces),
        out_shape=jax.ShapeDtypeStruct((rows, width), jnp.float32),
        in_specs=[pl.BlockSpec(memory_space=pltpu.VMEM)],
        out_specs=pl.BlockSpec(memory_space=pltpu.VMEM),
        scratch_shapes=[
            pltpu.VMEM((2, rows, width), jnp.bfloat16),
            pltpu.VMEM((rows, width), jnp.bfloat16),
            sems(2), sems(2), sems(), sems(),
        ],
        compiler_params=pltpu.CompilerParams(
            collective_id=ident, has_side_effects=True, vmem_limit_bytes=40 * MIB
        ),
        name=f"scatter4_{ident}",
    )(parts)


def weights_body(
    n_dp, gains, wq, wo, kv, ffn, gains_all, wq_all, wo_all, kv_all, ffn_all,
    own_sem, zs, zr, rs, rr, ks, kr
):
    at = Spot(n_dp)
    meet([at.mate] + at.line_at[1:] + at.rest_at[1:])
    parts = ffn.shape[1]
    halves = (at.half, 1 - at.half, at.half, 1 - at.half)

    def source(c, k):
        if c < 3:
            return (gains, wq, wo)[c]
        if c == 3:
            return kv.at[at.core]
        return ffn.at[halves[k], c - 4]

    def place(c, dp):
        if c < 3:
            return (gains_all, wq_all, wo_all)[c].at[dp]
        if c == 3:
            return kv_all.at[at.core, dp]
        return ffn_all.at[c - 4, dp]

    def along(c, k):
        return send_to(at.line_at[k], source(c, k), place(c, at.dp), zs.at[c, k], zr.at[c, k])

    def across(c, k, r):
        spot = place(c, at.line_dp[k])
        return send_to(
            at.rest_at[r], source(c, 0) if k == 0 else spot, spot, rs.at[c, k, r], rr.at[c, k, r]
        )

    everything = range(4 + parts)
    for c in everything:
        for k in (1, 2, 3):
            along(c, k).start()
        for r in range(1, at.n_rest):
            across(c, 0, r).start()
    own = [pltpu.make_async_copy(source(c, 0), place(c, at.dp), own_sem.at[c]) for c in everything]
    for copy in own:
        copy.start()
    for c in everything:
        for k in (1, 2, 3):
            along(c, k).wait_recv()
            for r in range(1, at.n_rest):
                across(c, k, r).start()
    for copy in own:
        copy.wait()
    for c in everything:
        for k in range(4):
            for r in range(1, at.n_rest):
                across(c, k, r).wait()
            if k:
                along(c, k).wait_send()
    share = send_to(at.mate, kv_all.at[at.core], kv_all.at[at.core], ks, kr)
    share.start()
    share.wait()


def all_weights(n_dp, gains, wq, wo, kv, ffn, ident):
    count = 4 + ffn.shape[1]
    line = pltpu.SemaphoreType.DMA((count, 4))
    rest = pltpu.SemaphoreType.DMA((count, 4, n_dp // 4))
    any_space = pl.BlockSpec(memory_space=pl.ANY)

    def shape(*dims):
        return jax.ShapeDtypeStruct(dims, jnp.bfloat16)

    return pl.pallas_call(
        functools.partial(weights_body, n_dp),
        out_shape=[
            shape(n_dp, *gains.shape), shape(n_dp, *wq.shape), shape(n_dp, *wo.shape),
            shape(2, n_dp, *kv.shape[1:]), shape(ffn.shape[1], n_dp, *ffn.shape[2:]),
        ],
        in_specs=[any_space] * 5,
        out_specs=[any_space] * 5,
        scratch_shapes=[
            pltpu.SemaphoreType.DMA((count,)), line, line, rest, rest,
            pltpu.SemaphoreType.DMA, pltpu.SemaphoreType.DMA,
        ],
        compiler_params=pltpu.CompilerParams(collective_id=ident, has_side_effects=True),
        name="all_weights",
    )(gains, wq, wo, kv, ffn)


def by_rows(rows, body):
    step = SUBLANES if rows % SUBLANES == 0 else rows
    if step == rows:
        body(slice(None))
        return

    def one(i, carry):
        body(pl.ds(pl.multiple_of(i * step, step), step))
        return carry

    lax.fori_loop(0, rows // step, one, 0)


def grads_body(
    n_dp, gains, wq, wo, kv, ffn, gains_out, wq_out, wo_out, kv_out, ffn_out,
    kv_held, gains_in, wq_in, wo_in, kv_in, ffn_in, gains_far, wq_far, wo_far, kv_far, ffn_far,
    gains_pool, kv_pool, rs, rr, zs, zr, ks, kr, gs, gr
):
    at = Spot(n_dp)
    meet([at.mate, at.side, {"tensor": at.t_side_mate}] + at.line_at[1:] + at.rest_at[1:])
    count = 4 + ffn.shape[0]
    order = list(range(4, count)) + [1, 2, 3, 0]
    turns = (1, 2, 3, 0)

    def block(c, dp):
        if c < 3:
            return (gains, wq, wo)[c].at[dp]
        if c == 3:
            return kv_held.at[dp]
        return ffn.at[c - 4, dp]

    def landed(c):
        if c < 4:
            return (gains_in, wq_in, wo_in, kv_in)[c]
        return ffn_in.at[c - 4]

    def distant(c):
        if c < 4:
            return (gains_far, wq_far, wo_far, kv_far)[c]
        return ffn_far.at[c - 4]

    def across(c, k, r):
        target = at.lines[k] * at.n_rest + at.rests[r]
        return send_to(
            at.rest_at[r], block(c, target), landed(c).at[k, r - 1], rs.at[c, k, r], rr.at[c, k, r]
        )

    def along(c, k):
        return send_to(
            at.line_at[k], landed(c).at[k, 0], distant(c).at[k - 1], zs.at[c, k], zr.at[c, k]
        )

    mate_kv = send_to(at.mate, kv.at[1 - at.core], kv_held, ks.at[0], kr.at[0])
    mate_kv.start()
    for c in order:
        if c == 3:
            mate_kv.wait()

            def pair_up(dp, carry):
                def add(rows):
                    kv_held[dp, rows] = add_up(kv[at.core, dp, rows], kv_held[dp, rows]).astype(
                        jnp.bfloat16
                    )

                by_rows(kv.shape[2], add)
                return carry

            lax.fori_loop(0, n_dp, pair_up, 0)
        for k in turns:
            for r in range(1, at.n_rest):
                across(c, k, r).start()
    for c in order:
        for k in turns:
            spot = block(c, at.line_dp[k])
            for r in range(1, at.n_rest):
                across(c, k, r).wait_recv()
            come = landed(c)

            def add(rows, spot=spot, come=come, k=k):
                total = spot[rows].astype(jnp.float32)
                for r in range(1, at.n_rest):
                    total = total + come[k, r - 1, rows].astype(jnp.float32)
                come[k, 0, rows] = total.astype(jnp.bfloat16)

            by_rows(spot.shape[0], add)
            if k:
                along(c, k).start()
    width = ffn.shape[-1]
    for c in order:
        spot = landed(c).at[0, 0]
        far = distant(c)
        for k in (1, 2, 3):
            along(c, k).wait_recv()
        if c >= 4:
            target = ffn_out.at[c - 4]

            def finish(first, spot=spot, far=far, target=target):
                def put(rows):
                    same = add_up(spot[rows], far[1, rows])
                    cross = add_up(far[0, rows], far[2, rows])
                    low, high = (same, cross) if first else (cross, same)
                    target[rows, :width] = low
                    target[rows, width:] = high[:, : target.shape[-1] - width]

                by_rows(spot.shape[0], put)

            @pl.when(at.half == 0)
            def _(finish=finish):
                finish(True)

            @pl.when(at.half == 1)
            def _(finish=finish):
                finish(False)
        else:

            def total_of(rows, spot=spot, far=far):
                return add_up(spot[rows], far[0, rows]) + add_up(far[1, rows], far[2, rows])

            if c in (1, 2):
                target = (wq_out, wo_out)[c - 1]

                def put(rows, target=target, total_of=total_of):
                    target[rows] = total_of(rows)

                by_rows(spot.shape[0], put)
            elif c == 3:

                def put(rows, total_of=total_of):
                    kv_pool[0, rows] = total_of(rows).astype(jnp.bfloat16)

                by_rows(spot.shape[0], put)
            else:
                gains_pool[at.t] = total_of(slice(None)).astype(jnp.bfloat16)
    kv_side = send_to(at.side, kv_pool.at[0], kv_pool.at[1], ks.at[1], kr.at[1])
    kv_side.start()
    others = [at.mate, at.side, {"tensor": at.t_side_mate}]
    spread = [
        send_to(where, gains_pool.at[at.t], gains_pool.at[at.t], gs.at[j], gr.at[j])
        for j, where in enumerate(others)
    ]
    for copy in spread:
        copy.start()
    kv_side.wait()

    def put(rows):
        kv_out[at.core, rows] = add_up(kv_pool[0, rows], kv_pool[1, rows])

    by_rows(kv_pool.shape[1], put)
    give = send_to(at.mate, kv_out.at[at.core], kv_out.at[at.core], ks.at[2], kr.at[2])
    give.start()
    for copy in spread:
        copy.wait()
    gains_out[...] = add_up(gains_pool[0], gains_pool[1]) + add_up(gains_pool[2], gains_pool[3])
    give.wait()
    for c in order:
        for k in turns:
            for r in range(1, at.n_rest):
                across(c, k, r).wait_send()
            if k:
                along(c, k).wait_send()


def all_grads(n_dp, gains, wq, wo, kv, ffn, columns, ident):
    count = 4 + ffn.shape[0]
    n_rest = n_dp // 4
    blocks = [gains.shape[1:], wq.shape[1:], wo.shape[1:], kv.shape[2:]]
    vmem = pl.BlockSpec(memory_space=pltpu.VMEM)
    rest = pltpu.SemaphoreType.DMA((count, 4, n_rest))
    line = pltpu.SemaphoreType.DMA((count, 4))
    three = pltpu.SemaphoreType.DMA((3,))

    def shape(*dims):
        return jax.ShapeDtypeStruct(dims, jnp.float32)

    def low(*dims):
        return pltpu.VMEM(dims, jnp.bfloat16)

    parts, _, rows, width = ffn.shape
    return pl.pallas_call(
        functools.partial(grads_body, n_dp),
        out_shape=[
            shape(*blocks[0]), shape(*blocks[1]), shape(*blocks[2]), shape(2, *blocks[3]),
            shape(parts, rows, columns),
        ],
        in_specs=[vmem] * 5,
        out_specs=[vmem] * 5,
        scratch_shapes=[low(n_dp, *blocks[3])]
        + [low(4, n_rest - 1, *block) for block in blocks]
        + [low(parts, 4, n_rest - 1, rows, width)]
        + [low(3, *block) for block in blocks]
        + [low(parts, 3, rows, width)]
        + [low(4, *blocks[0]), low(2, *blocks[3])]
        + [rest, rest, line, line, three, three, three, three],
        compiler_params=pltpu.CompilerParams(
            collective_id=ident, has_side_effects=True, vmem_limit_bytes=60 * MIB
        ),
        name="all_grads",
    )(gains, wq, wo, kv, ffn)


def pack_gains(blocks, width):
    n = blocks[0].shape[0]
    rows = [jnp.pad(block, ((0, 0), (0, width - block.shape[1]))) for block in blocks]
    packed = jnp.stack(rows, axis=1)
    return jnp.pad(packed, ((0, 0), (0, SUBLANES - len(blocks)), (0, 0)))


def local(
    n_dp,
    n_tensor,
    hidden,
    in_gain,
    w_query,
    w_key,
    w_value,
    query_gain,
    key_gain,
    w_output,
    attn_gain,
    ffn_gain,
    w_gate,
    w_up,
    w_down,
    out_gain,
    cotangent,
    segment_ids,
    positions,
):
    factor = HD ** (-0.5)
    gains = (in_gain, attn_gain, ffn_gain, out_gain, query_gain, key_gain)
    width = -(-max(gain.shape[0] for gain in gains) // LANES) * LANES
    gain_rows = pack_gains([gain[None] for gain in gains], width)[0]
    columns = w_gate.shape[1]
    wide = -(-columns // (2 * LANES)) * LANES
    ffn = jnp.stack([w_gate, w_up, w_down.T])
    ffn = jnp.pad(ffn, ((0, 0), (0, 0), (0, 2 * wide - columns)))
    ffn = jnp.stack([ffn[:, :, :wide], ffn[:, :, wide:]])
    gains_all, wq_all, wo_all, kv_all, ffn_all = all_weights(
        n_dp, gain_rows, w_query, w_output.T, jnp.stack([w_key, w_value]), ffn, 0
    )
    full_in_gain, full_attn_gain, full_ffn_gain, full_out_gain, full_qgain, full_kgain = (
        gains_all[:, row, : gain.shape[0]].reshape(-1) for row, gain in enumerate(gains)
    )
    full_query, full_output = (block.reshape(-1, block.shape[-1]) for block in (wq_all, wo_all))
    full_key, full_value = (kv_all[i].reshape(-1, kv_all.shape[-1]) for i in range(2))
    full_gate, full_up, full_down = (ffn_all[i].reshape(-1, wide) for i in range(3))
    heads_local = full_query.shape[1] // HD
    hidden_f = hidden.astype(jnp.float32)
    normed_local = apply_norm(hidden_f, full_in_gain).astype(jnp.bfloat16)
    normed_in = gather4(n_dp, normed_local, 1).reshape(-1, normed_local.shape[-1])
    seq_len = normed_in.shape[0]
    query_raw = jnp.dot(normed_in, full_query, preferred_element_type=jnp.float32).reshape(
        seq_len, heads_local, HD
    )
    key_raw = jnp.dot(normed_in, full_key, preferred_element_type=jnp.float32)
    value_rows = jnp.dot(normed_in, full_value, preferred_element_type=jnp.float32).astype(
        jnp.bfloat16
    )
    cosine, sine_table = rotary_tables(positions, HD)
    query_rot = rotate(
        apply_norm(query_raw, full_qgain), cosine[:, None, :], sine_table[:, None, :]
    ).astype(jnp.bfloat16)
    key_rot = rotate(apply_norm(key_raw, full_kgain), cosine, sine_table).astype(jnp.bfloat16)
    allowed = window_mask(segment_ids)[None]
    scores = (
        jnp.einsum("qhd,kd->hqk", query_rot, key_rot, preferred_element_type=jnp.float32) * factor
    )
    log_total = jnp.log(jnp.sum(jnp.where(allowed, jnp.exp(scores), 0.0), axis=-1, keepdims=True))
    probs_low = jnp.where(allowed, jnp.exp(scores - log_total), 0.0).astype(jnp.bfloat16)
    context = jnp.einsum("hqk,kd->qhd", probs_low, value_rows, preferred_element_type=jnp.float32)
    context = context.reshape(seq_len, heads_local * HD).astype(jnp.bfloat16)
    attn_part = contract_cols(context, full_output)
    attn_rows = scatter4(
        n_dp, attn_part.astype(jnp.bfloat16).reshape(n_tensor, -1, attn_part.shape[-1]), 2
    )
    residual = hidden_f + apply_norm(attn_rows, full_attn_gain)
    ffn_local = apply_norm(residual, full_ffn_gain).astype(jnp.bfloat16)
    ffn_in = gather8(n_dp, ffn_local, 3).reshape(-1, ffn_local.shape[-1])
    gate_pre = jnp.dot(ffn_in, full_gate, preferred_element_type=jnp.float32)
    up_pre = jnp.dot(ffn_in, full_up, preferred_element_type=jnp.float32)
    gelu_values, gelu_back = jax.vjp(gelu_tanh, gate_pre)
    mixed = (gelu_values * up_pre).astype(jnp.bfloat16)
    down_part = contract_cols(mixed, full_down)
    down_rows = scatter8(
        n_dp, down_part.astype(jnp.bfloat16).reshape(2, n_tensor, -1, down_part.shape[-1]), 4
    )
    output = (residual + apply_norm(down_rows, full_out_gain)).astype(jnp.bfloat16)
    cot_f = cotangent.astype(jnp.float32)
    grad_down, term_out = norm_back(down_rows, full_out_gain, cot_f)
    down_all = gather8(n_dp, grad_down.astype(jnp.bfloat16), 5).reshape(-1, grad_down.shape[-1])
    grad_wd = contract_rows(down_all, mixed)
    grad_mixed = jnp.dot(down_all, full_down, preferred_element_type=jnp.float32)
    gate_low = gelu_back(grad_mixed * up_pre)[0].astype(jnp.bfloat16)
    up_low = (grad_mixed * gelu_values).astype(jnp.bfloat16)
    grad_wg = contract_rows(ffn_in, gate_low)
    grad_wu = contract_rows(ffn_in, up_low)
    ffn_part = contract_cols(gate_low, full_gate) + contract_cols(up_low, full_up)
    ffn_back = scatter8(
        n_dp, ffn_part.astype(jnp.bfloat16).reshape(2, n_tensor, -1, ffn_part.shape[-1]), 6
    )
    resid_norm, term_ffn = norm_back(residual, full_ffn_gain, ffn_back)
    grad_residual = cot_f + resid_norm
    grad_attn, term_attn = norm_back(attn_rows, full_attn_gain, grad_residual)
    attn_all = gather4(n_dp, grad_attn.astype(jnp.bfloat16), 7).reshape(-1, grad_attn.shape[-1])
    grad_wo = contract_rows(attn_all, context)
    grad_context = (
        jnp.dot(attn_all, full_output, preferred_element_type=jnp.float32)
        .astype(jnp.bfloat16)
        .reshape(seq_len, heads_local, HD)
    )
    scores_again = (
        jnp.einsum("qhd,kd->hqk", query_rot, key_rot, preferred_element_type=jnp.float32) * factor
    )
    probs = jnp.where(allowed, jnp.exp(scores_again - log_total), 0.0)
    grad_probs = jnp.einsum(
        "qhd,kd->hqk", grad_context, value_rows, preferred_element_type=jnp.float32
    )
    delta = jnp.sum(probs * grad_probs, axis=-1, keepdims=True)
    grad_scores = (probs * (grad_probs - delta) * factor).astype(jnp.bfloat16)
    value_heads = jnp.einsum(
        "hqk,qhd->khd", probs.astype(jnp.bfloat16), grad_context, preferred_element_type=jnp.float32
    ).astype(jnp.bfloat16)
    grad_qrot = jnp.einsum("hqk,kd->qhd", grad_scores, key_rot, preferred_element_type=jnp.float32)
    grad_kheads = jnp.einsum(
        "hqk,qhd->khd", grad_scores, query_rot, preferred_element_type=jnp.float32
    )
    grad_qraw, term_qgain = norm_back(
        query_raw, full_qgain, rotate(grad_qrot, cosine[:, None, :], -sine_table[:, None, :])
    )
    grad_kraw, term_kgain = norm_back(
        key_raw[:, None, :],
        full_kgain,
        rotate(grad_kheads, cosine[:, None, :], -sine_table[:, None, :]),
    )
    query_low = grad_qraw.astype(jnp.bfloat16).reshape(seq_len, heads_local * HD)
    key_low = grad_kraw.astype(jnp.bfloat16)
    grad_wq = contract_rows(normed_in, query_low)
    grad_wk = jnp.einsum("sd,she->de", normed_in, key_low, preferred_element_type=jnp.float32)
    grad_wv = jnp.einsum("sd,she->de", normed_in, value_heads, preferred_element_type=jnp.float32)
    attn_in_part = contract_cols(query_low, full_query)
    attn_in_part = attn_in_part + jnp.einsum(
        "she,de->sd", key_low, full_key, preferred_element_type=jnp.float32
    )
    attn_in_part = attn_in_part + jnp.einsum(
        "she,de->sd", value_heads, full_value, preferred_element_type=jnp.float32
    )
    attn_back = scatter4(
        n_dp, attn_in_part.astype(jnp.bfloat16).reshape(n_tensor, -1, attn_in_part.shape[-1]), 8
    )
    in_norm, term_in = norm_back(hidden_f, full_in_gain, attn_back)
    grad_hidden = grad_residual + in_norm
    def blocks(values):
        return values.astype(jnp.bfloat16).reshape(n_dp, -1, values.shape[-1])

    gain_grads = [
        jnp.sum(term, axis=tuple(range(term.ndim - 1))).astype(jnp.bfloat16).reshape(n_dp, -1)
        for term in (term_in, term_attn, term_ffn, term_out, term_qgain, term_kgain)
    ]
    own_gains, own_query, own_output, own_kv, own_ffn_weights = all_grads(
        n_dp,
        pack_gains(gain_grads, width),
        blocks(grad_wq),
        blocks(grad_wo),
        jnp.stack([blocks(grad_wk), blocks(grad_wv)]),
        jnp.stack([blocks(grad_wg), blocks(grad_wu), blocks(grad_wd)]),
        columns,
        9,
    )
    own_in, own_attn, own_ffn, own_out, own_q, own_k = (
        own_gains[row, : gain.shape[0]] for row, gain in enumerate(gains)
    )
    return (
        output,
        grad_hidden,
        own_in,
        own_query,
        own_kv[0],
        own_kv[1],
        own_q,
        own_k,
        own_output.T,
        own_attn,
        own_ffn,
        own_ffn_weights[0],
        own_ffn_weights[1],
        own_ffn_weights[2].T,
        own_out,
    )


def solution(mesh):
    placed = (
        P(("dp", "tensor"), None),
        P("dp"),
        P("dp", "tensor"),
        P("dp", None),
        P("dp", None),
        P("dp"),
        P("dp"),
        P("tensor", "dp"),
        P("dp"),
        P("dp"),
        P("dp", "tensor"),
        P("dp", "tensor"),
        P("tensor", "dp"),
        P("dp"),
        P(("dp", "tensor"), None),
        P("dp"),
        P("dp"),
    )
    return jax.shard_map(
        functools.partial(local, mesh.shape["dp"], mesh.shape["tensor"]),
        mesh=mesh,
        in_specs=placed,
        out_specs=(
            P(("dp", "tensor"), None),
            P(("dp", "tensor"), None),
            P("dp"),
            P("dp", "tensor"),
            P("dp", None),
            P("dp", None),
            P("dp"),
            P("dp"),
            P("tensor", "dp"),
            P("dp"),
            P("dp"),
            P("dp", "tensor"),
            P("dp", "tensor"),
            P("tensor", "dp"),
            P("dp"),
        ),
        check_vma=False,
    )
```

```python
import functools

import jax
import jax.numpy as jnp
from jax import lax
from jax.experimental import pallas as pl
from jax.experimental.pallas import tpu as pltpu
from jax.sharding import PartitionSpec as P

HD = 256
WINDOW = 512


EPSILON = 1e-06
ROPE_BASE = 10000.0


def rms_scale(values):
    return lax.rsqrt(jnp.mean(values * values, axis=-1, keepdims=True) + EPSILON)


def apply_norm(values, gain_vec):
    return values * rms_scale(values) * gain_vec.astype(jnp.float32)


def norm_back(values, gain_vec, upstream):
    factor = rms_scale(values)
    unit_rows = values * factor
    scaled = upstream * gain_vec.astype(jnp.float32)
    grad_values = factor * (
        scaled - unit_rows * jnp.mean(scaled * unit_rows, axis=-1, keepdims=True)
    )
    return (grad_values, upstream * unit_rows)


def rotary_tables(token_pos, width):
    steps_half = jnp.arange(width // 2, dtype=jnp.float32)
    frequency = ROPE_BASE ** (-2.0 * steps_half / width)
    angles = token_pos.astype(jnp.float32)[:, None] * frequency[None, :]
    return (jnp.cos(angles), jnp.sin(angles))


def gelu_tanh(values):
    return jax.nn.gelu(values, approximate=True)


def contract_rows(left, right):
    return lax.dot_general(
        left, right, (((0,), (0,)), ((), ())), preferred_element_type=jnp.float32
    )


def contract_cols(left, right):
    return lax.dot_general(
        left, right, (((1,), (1,)), ((), ())), preferred_element_type=jnp.float32
    )


MESH = pl.DeviceIdType.MESH
LANES = 128
SUBLANES = 16
MIB = 1024 * 1024


def send_to(where, src, dst, send, recv):
    return pltpu.make_async_remote_copy(
        src_ref=src,
        dst_ref=dst,
        send_sem=send,
        recv_sem=recv,
        device_id=where,
        device_id_type=MESH,
    )


def meet(partners):
    barrier = pltpu.get_barrier_semaphore()
    for where in partners:
        pl.semaphore_signal(barrier, inc=1, device_id=where, device_id_type=MESH)
    pl.semaphore_wait(barrier, len(partners))


class Spot:
    def __init__(self, n_dp):
        self.n_rest = n_dp // 4
        self.dp = lax.axis_index("dp")
        self.t = lax.axis_index("tensor")
        self.x = self.t // 2
        self.core = self.t - 2 * self.x
        self.line = self.dp // self.n_rest
        self.rest = self.dp - self.line * self.n_rest
        self.half = self.line % 2
        high = self.line // 2
        self.lines = [
            self.line,
            2 * high + 1 - self.half,
            2 * (1 - high) + self.half,
            2 * (1 - high) + 1 - self.half,
        ]
        self.line_dp = [line * self.n_rest + self.rest for line in self.lines]
        self.line_at = [{"dp": dp} for dp in self.line_dp]
        self.rests = [(self.rest + r) % self.n_rest for r in range(self.n_rest)]
        self.rest_at = [{"dp": self.line * self.n_rest + rest} for rest in self.rests]
        self.from_rest = [
            (self.rest + self.n_rest - r) % self.n_rest for r in range(self.n_rest)
        ]
        self.t_mate = 2 * self.x + 1 - self.core
        self.t_side = 2 * (1 - self.x) + self.core
        self.t_side_mate = 2 * (1 - self.x) + 1 - self.core
        self.mate = {"tensor": self.t_mate}
        self.side = {"tensor": self.t_side}
        self.pair = self.line_at[1]


def row_pieces(rows, wanted):
    cuts = wanted if rows % (wanted * SUBLANES) == 0 else 1
    size = rows // cuts
    return [(cut * size, size) for cut in range(cuts)]


def gather8_body(n_dp, pieces, mine, full, own_sem, xs, xr, zs, zr, ds, dr, ms, mr):
    at = Spot(n_dp)
    meet([at.mate, at.side, at.pair])
    half, other = at.half, 1 - at.half

    def cut(ref, p):
        return ref.at[pl.ds(*pieces[p])]

    def over_x(p):
        return send_to(at.side, cut(mine, p), cut(full.at[half, at.t], p), xs.at[p], xr.at[p])

    def over_z(p):
        return send_to(at.pair, cut(mine, p), cut(full.at[half, at.t], p), zs.at[p], zr.at[p])

    def onward(p):
        if p % 2 == 0:
            block = cut(full.at[half, at.t_side], p)
            return send_to(at.pair, block, block, ds.at[p], dr.at[p])
        block = cut(full.at[other, at.t], p)
        return send_to(at.side, block, block, ds.at[p], dr.at[p])

    def near(j, p):
        place = cut(full.at[(half, half, other, other)[j], (at.t, at.t_side, at.t, at.t_side)[j]], p)
        source = cut(mine, p) if j == 0 else place
        return send_to(at.mate, source, place, ms.at[j, p], mr.at[j, p])

    count = len(pieces)
    for p in range(count):
        over_x(p).start()
        over_z(p).start()
    own = pltpu.make_async_copy(mine, full.at[half, at.t], own_sem)
    own.start()
    for p in range(count):
        near(0, p).start()
    for p in range(count):
        over_x(p).wait_recv()
        if p % 2 == 0:
            onward(p).start()
        near(1, p).start()
        over_z(p).wait_recv()
        if p % 2 == 1:
            onward(p).start()
        near(2, p).start()
    for p in range(count):
        onward(p).wait_recv()
        near(3, p).start()
    own.wait()
    for p in range(count):
        over_x(p).wait_send()
        over_z(p).wait_send()
        onward(p).wait_send()
        for j in range(4):
            near(j, p).wait()


def gather8(n_dp, block, ident):
    pieces = row_pieces(block.shape[0], 10)
    count = len(pieces)
    one = pltpu.SemaphoreType.DMA((count,))
    four = pltpu.SemaphoreType.DMA((4, count))
    return pl.pallas_call(
        functools.partial(gather8_body, n_dp, pieces),
        out_shape=jax.ShapeDtypeStruct((2, 4, *block.shape), block.dtype),
        in_specs=[pl.BlockSpec(memory_space=pltpu.VMEM)],
        out_specs=pl.BlockSpec(memory_space=pl.ANY),
        scratch_shapes=[pltpu.SemaphoreType.DMA, one, one, one, one, one, one, four, four],
        compiler_params=pltpu.CompilerParams(collective_id=ident, has_side_effects=True),
        name=f"gather8_{ident}",
    )(block)


def add_up(left, right):
    return left.astype(jnp.float32) + right.astype(jnp.float32)


def scatter8_body(
    n_dp, pieces, parts, out, held, come, last, ms, mr, fs, fr, ls, lr
):
    at = Spot(n_dp)
    meet([at.mate, at.side, at.pair])
    half, other = at.half, 1 - at.half
    halves = (half, half, other, other)
    mine_t = (at.t, at.t_side, at.t, at.t_side)
    mate_t = (at.t_mate, at.t_side_mate, at.t_mate, at.t_side_mate)
    count = len(pieces)

    def near(k, p):
        rows = pl.ds(*pieces[p])
        return send_to(
            at.mate, parts.at[halves[k], mate_t[k], rows], held.at[k, rows], ms.at[k, p], mr.at[k, p]
        )

    def first(j, p):
        rows = pl.ds(*pieces[p])
        if p % 2 == 0:
            return send_to(at.side, held.at[(1, 3)[j], rows], come.at[j, rows], fs.at[j, p], fr.at[j, p])
        return send_to(at.pair, held.at[(2, 3)[j], rows], come.at[j, rows], fs.at[j, p], fr.at[j, p])

    def second(p):
        rows = pl.ds(*pieces[p])
        if p % 2 == 0:
            return send_to(at.pair, held.at[2, rows], last.at[rows], ls.at[p], lr.at[p])
        return send_to(at.side, held.at[1, rows], last.at[rows], ls.at[p], lr.at[p])

    for p in range(count):
        for k in (3, 1, 2, 0):
            near(k, p).start()
    for p in range(count):
        rows = pl.ds(*pieces[p])
        for k in (3, 1, 2, 0):
            near(k, p).wait_recv()
            held[k, rows] = add_up(parts[halves[k], mine_t[k], rows], held[k, rows]).astype(jnp.bfloat16)
        first(1, p).start()
        first(0, p).start()
    for p in range(count):
        rows = pl.ds(*pieces[p])
        keep = 2 if p % 2 == 0 else 1
        first(1, p).wait_recv()
        held[keep, rows] = add_up(held[keep, rows], come[1, rows]).astype(jnp.bfloat16)
        second(p).start()
        first(0, p).wait_recv()
        out[rows] = add_up(held[0, rows], come[0, rows])
    for p in range(count):
        rows = pl.ds(*pieces[p])
        second(p).wait_recv()
        out[rows] = out[rows] + last[rows].astype(jnp.float32)
    for p in range(count):
        for k in range(4):
            near(k, p).wait_send()
        for j in range(2):
            first(j, p).wait_send()
        second(p).wait_send()


def scatter8(n_dp, parts, ident):
    rows, width = parts.shape[2:]
    pieces = row_pieces(rows, 10)
    count = len(pieces)

    def sems(*shape):
        return pltpu.SemaphoreType.DMA((*shape, count))

    return pl.pallas_call(
        functools.partial(scatter8_body, n_dp, pieces),
        out_shape=jax.ShapeDtypeStruct((rows, width), jnp.float32),
        in_specs=[pl.BlockSpec(memory_space=pltpu.VMEM)],
        out_specs=pl.BlockSpec(memory_space=pltpu.VMEM),
        scratch_shapes=[
            pltpu.VMEM((4, rows, width), jnp.bfloat16),
            pltpu.VMEM((2, rows, width), jnp.bfloat16),
            pltpu.VMEM((rows, width), jnp.bfloat16),
            sems(4), sems(4), sems(2), sems(2), sems(), sems(),
        ],
        compiler_params=pltpu.CompilerParams(
            collective_id=ident, has_side_effects=True, vmem_limit_bytes=40 * MIB
        ),
        name=f"scatter8_{ident}",
    )(parts)


def weights_body(
    n_dp, gains, wq, wo, kv, gains_all, wq_all, wo_all, kv_all, own_sem, zs, zr, rs, rr, ks, kr
):
    at = Spot(n_dp)
    meet([at.mate] + at.line_at[1:] + at.rest_at[1:])

    def source(c):
        return kv.at[at.core] if c == 3 else (gains, wq, wo)[c]

    def place(c, dp):
        return kv_all.at[at.core, dp] if c == 3 else (gains_all, wq_all, wo_all)[c].at[dp]

    def along(c, k):
        return send_to(at.line_at[k], source(c), place(c, at.dp), zs.at[c, k], zr.at[c, k])

    def across(c, k, r):
        spot = place(c, at.line_dp[k])
        return send_to(
            at.rest_at[r], source(c) if k == 0 else spot, spot, rs.at[c, k, r], rr.at[c, k, r]
        )

    order = (0, 3, 1, 2)
    for c in order:
        for k in (1, 2, 3):
            along(c, k).start()
        for r in range(1, at.n_rest):
            across(c, 0, r).start()
    own = [pltpu.make_async_copy(source(c), place(c, at.dp), own_sem.at[c]) for c in order]
    for copy in own:
        copy.start()
    for c in order:
        for k in (1, 2, 3):
            along(c, k).wait_recv()
            for r in range(1, at.n_rest):
                across(c, k, r).start()
    for copy in own:
        copy.wait()
    share = send_to(at.mate, kv_all.at[at.core], kv_all.at[at.core], ks, kr)
    for c in (3, 0, 1, 2):
        for k in range(4):
            for r in range(1, at.n_rest):
                across(c, k, r).wait()
            if k:
                along(c, k).wait_send()
        if c == 3:
            share.start()
    share.wait()


def attention_weights(n_dp, gains, wq, wo, kv, ident):
    line = pltpu.SemaphoreType.DMA((4, 4))
    rest = pltpu.SemaphoreType.DMA((4, 4, n_dp // 4))
    any_space = pl.BlockSpec(memory_space=pl.ANY)

    def shape(*dims):
        return jax.ShapeDtypeStruct(dims, jnp.bfloat16)

    return pl.pallas_call(
        functools.partial(weights_body, n_dp),
        out_shape=[
            shape(n_dp, *gains.shape), shape(n_dp, *wq.shape), shape(n_dp, *wo.shape),
            shape(2, n_dp, *kv.shape[1:]),
        ],
        in_specs=[pl.BlockSpec(memory_space=pltpu.VMEM)] * 4,
        out_specs=[any_space] * 4,
        scratch_shapes=[
            pltpu.SemaphoreType.DMA((4,)), line, line, rest, rest,
            pltpu.SemaphoreType.DMA, pltpu.SemaphoreType.DMA,
        ],
        compiler_params=pltpu.CompilerParams(collective_id=ident, has_side_effects=True),
        name="attention_weights",
    )(gains, wq, wo, kv)


class Background:
    def __init__(self, at, ffn, ffn_all, own_sem, zs, zr, rs, rr):
        self.at, self.ffn, self.ffn_all = at, ffn, ffn_all
        self.own_sem, self.zs, self.zr, self.rs, self.rr = own_sem, zs, zr, rs, rr
        self.halves = (at.half, 1 - at.half, at.half, 1 - at.half)

    def along(self, c, k):
        at = self.at
        return send_to(
            at.line_at[k], self.ffn.at[self.halves[k], c], self.ffn_all.at[c, at.dp],
            self.zs.at[c, k], self.zr.at[c, k],
        )

    def across(self, c, k, r):
        at = self.at
        spot = self.ffn_all.at[c, at.line_dp[k]]
        source = self.ffn.at[at.half, c] if k == 0 else spot
        return send_to(at.rest_at[r], source, spot, self.rs.at[c, k, r], self.rr.at[c, k, r])

    def own(self, c):
        at = self.at
        return pltpu.make_async_copy(
            self.ffn.at[at.half, c], self.ffn_all.at[c, at.dp], self.own_sem.at[c]
        )

    def launch(self, c):
        for k in (2, 3, 1):
            self.along(c, k).start()
        for r in range(1, self.at.n_rest):
            self.across(c, 0, r).start()
        self.own(c).start()

    def forward(self, c, ks=(2, 3, 1)):
        for k in ks:
            self.along(c, k).wait_recv()
            for r in range(1, self.at.n_rest):
                self.across(c, k, r).start()

    def finish(self, c):
        self.own(c).wait()
        for k in range(4):
            for r in range(1, self.at.n_rest):
                self.across(c, k, r).wait()
            if k:
                self.along(c, k).wait_send()


def dot(left, right):
    return jnp.dot(left, right, preferred_element_type=jnp.float32)


def turn(values, cosine, sine_table):
    half_width = values.shape[-1] // 2
    first_half = values[:, :half_width]
    second = values[:, half_width:]
    return jnp.concatenate(
        [first_half * cosine - second * sine_table, second * cosine + first_half * sine_table],
        axis=-1,
    )


class Gather4:
    def __init__(self, at, pieces, mine, full, xs, xr, ms, mr):
        self.at, self.pieces, self.mine, self.full = at, pieces, mine, full
        self.xs, self.xr, self.ms, self.mr = xs, xr, ms, mr

    def over_x(self, p):
        rows, at = pl.ds(*self.pieces[p]), self.at
        return send_to(
            at.side, self.mine.at[rows], self.full.at[at.t, rows], self.xs.at[p], self.xr.at[p]
        )

    def near(self, p):
        rows, at = pl.ds(*self.pieces[p]), self.at
        block = self.full.at[at.t_side, rows]
        return send_to(at.mate, block, block, self.ms.at[p], self.mr.at[p])

    def near_own(self):
        at, p = self.at, len(self.pieces)
        return send_to(at.mate, self.mine, self.full.at[at.t], self.ms.at[p], self.mr.at[p])

    def start(self):
        for p in range(len(self.pieces)):
            self.over_x(p).start()
        self.near_own().start()

    def pass_on(self):
        for p in range(len(self.pieces)):
            self.over_x(p).wait_recv()
            self.near(p).start()

    def all_here(self):
        for p in range(len(self.pieces)):
            self.near(p).wait_recv()

    def finish(self):
        self.near_own().wait_send()
        for p in range(len(self.pieces)):
            self.over_x(p).wait_send()
            self.near(p).wait_send()


class Scatter4:
    def __init__(self, at, pieces, parts, held, come, ms, mr, fs, fr):
        self.at, self.pieces, self.parts, self.held, self.come = at, pieces, parts, held, come
        self.ms, self.mr, self.fs, self.fr = ms, mr, fs, fr
        self.mate_t = (at.t_mate, at.t_side_mate)

    def near(self, k):
        return send_to(
            self.at.mate, self.parts.at[self.mate_t[k]], self.held.at[k], self.ms.at[k], self.mr.at[k]
        )

    def far(self, p):
        rows = pl.ds(*self.pieces[p])
        return send_to(
            self.at.side, self.held.at[1, rows], self.come.at[rows], self.fs.at[p], self.fr.at[p]
        )

    def send_side(self):
        self.near(1).wait_recv()
        for p, piece in enumerate(self.pieces):
            rows = pl.ds(*piece)
            self.held[1, rows] = add_up(self.parts[self.at.t_side, rows], self.held[1, rows]).astype(
                jnp.bfloat16
            )
            self.far(p).start()

    def result(self, out):
        self.near(0).wait_recv()
        for p, piece in enumerate(self.pieces):
            rows = pl.ds(*piece)
            self.far(p).wait_recv()
            out[rows] = add_up(self.parts[self.at.t, rows], self.held[0, rows]) + self.come[
                rows
            ].astype(jnp.float32)

    def finish(self):
        for k in range(2):
            self.near(k).wait_send()
        for p in range(len(self.pieces)):
            self.far(p).wait_send()


class Gather8:
    def __init__(self, at, pieces, mine, full, xs, xr, zs, zr, ds, dr, ms, mr):
        self.at, self.pieces, self.mine, self.full = at, pieces, mine, full
        self.xs, self.xr, self.zs, self.zr = xs, xr, zs, zr
        self.ds, self.dr, self.ms, self.mr = ds, dr, ms, mr

    def spot(self, z, t, p):
        return self.full.at[z, t, pl.ds(*self.pieces[p])]

    def over_x(self, p):
        at = self.at
        return send_to(
            at.side, self.mine.at[pl.ds(*self.pieces[p])], self.spot(at.half, at.t, p),
            self.xs.at[p], self.xr.at[p],
        )

    def over_z(self, p):
        at = self.at
        return send_to(
            at.pair, self.mine.at[pl.ds(*self.pieces[p])], self.spot(at.half, at.t, p),
            self.zs.at[p], self.zr.at[p],
        )

    def onward(self, p):
        at = self.at
        if p % 2 == 0:
            block = self.spot(at.half, at.t_side, p)
            return send_to(at.pair, block, block, self.ds.at[p], self.dr.at[p])
        block = self.spot(1 - at.half, at.t, p)
        return send_to(at.side, block, block, self.ds.at[p], self.dr.at[p])

    def near(self, j, p):
        at = self.at
        z = (at.half, at.half, 1 - at.half, 1 - at.half)[j]
        place = self.spot(z, (at.t, at.t_side, at.t, at.t_side)[j], p)
        source = self.mine.at[pl.ds(*self.pieces[p])] if j == 0 else place
        return send_to(at.mate, source, place, self.ms.at[j, p], self.mr.at[j, p])

    def start(self, p):
        self.over_x(p).start()
        self.over_z(p).start()
        self.near(0, p).start()

    def pass_on(self):
        for p in range(len(self.pieces)):
            self.over_x(p).wait_recv()
            if p % 2 == 0:
                self.onward(p).start()
            self.near(1, p).start()
            self.over_z(p).wait_recv()
            if p % 2 == 1:
                self.onward(p).start()
            self.near(2, p).start()

    def pass_last(self):
        for p in range(len(self.pieces)):
            self.onward(p).wait_recv()
            self.near(3, p).start()

    def finish(self):
        for p in range(len(self.pieces)):
            self.over_x(p).wait_send()
            self.over_z(p).wait_send()
            self.onward(p).wait_send()
            for j in range(4):
                self.near(j, p).wait()


def forward_body(
    n_dp, pieces,
    hidden, gains, head_gains, wq, wk, wv, wo, cosine, sine, seg_col, seg_row, ffn,
    a_all, q_raw, k_raw, q_rot, k_rot, v_all, lse, ctx, u_out, h_out, c_all, ffn_all,
    a_own, c_own, parts, held, come,
    own_sem, bzs, bzr, brs, brr, gxs, gxr, gms, gmr, sms, smr, sfs, sfr,
    xs, xr, zs, zr, ds, dr, ms, mr,
):
    at = Spot(n_dp)
    meet([at.mate, at.side] + at.line_at[1:] + at.rest_at[1:])
    load = Background(at, ffn, ffn_all, own_sem, bzs, bzr, brs, brr)
    count = ffn.shape[1]
    size = hidden.shape[0]
    load.launch(0)
    if count > 1:
        load.launch(1)

    def gain(row):
        return gains[row : row + 1, :]

    bring = Gather4(at, pieces, a_own, a_all, gxs, gxr, gms, gmr)
    for piece in pieces:
        rows = pl.ds(*piece)
        a_own[rows] = apply_norm(hidden[rows].astype(jnp.float32), gain(0)).astype(jnp.bfloat16)
    bring.start()
    a_all[at.t] = a_own[...]

    def project(t):
        rows = pl.ds(pl.multiple_of(t * size, SUBLANES), size)
        a = a_all[t]
        q = dot(a, wq[...])
        q_raw[t] = q
        q_rot[t] = turn(apply_norm(q, head_gains[0:1, :]), cosine[t], sine[t]).astype(jnp.bfloat16)
        k = dot(a, wk[...])
        k_raw[t] = k
        k_rot[rows] = turn(apply_norm(k, head_gains[1:2, :]), cosine[t], sine[t]).astype(
            jnp.bfloat16
        )
        v_all[rows] = dot(a, wv[...]).astype(jnp.bfloat16)

    project(at.t)
    bring.near_own().wait_recv()
    project(at.t_mate)
    bring.pass_on()
    project(at.t_side)
    bring.all_here()
    project(at.t_side_mate)

    def attend(t):
        scores = contract_cols(q_rot[t], k_rot[...]) * HD ** (-0.5)
        row = lax.broadcasted_iota(jnp.int32, scores.shape, 0) + t * size
        behind = row - lax.broadcasted_iota(jnp.int32, scores.shape, 1)
        allowed = (seg_col[t] == seg_row[...]) & (behind >= 0) & (behind < WINDOW)
        weights = jnp.where(allowed, jnp.exp(scores), 0.0)
        total = jnp.sum(weights, axis=-1, keepdims=True)
        lse[t] = jnp.log(total)
        mixed = dot((weights / total).astype(jnp.bfloat16), v_all[...]).astype(jnp.bfloat16)
        ctx[t] = mixed
        parts[t] = contract_cols(mixed, wo[...]).astype(jnp.bfloat16)

    back = Scatter4(at, pieces, parts, held, come, sms, smr, sfs, sfr)
    attend(at.t_side_mate)
    back.near(1).start()
    attend(at.t_side)
    back.send_side()
    attend(at.t_mate)
    back.near(0).start()
    attend(at.t)
    load.forward(0)
    back.result(u_out)
    spread = Gather8(at, pieces, c_own, c_all, xs, xr, zs, zr, ds, dr, ms, mr)
    for p, piece in enumerate(pieces):
        rows = pl.ds(*piece)
        total = hidden[rows].astype(jnp.float32) + apply_norm(u_out[rows], gain(1))
        h_out[rows] = total
        c_own[rows] = apply_norm(total, gain(2)).astype(jnp.bfloat16)
        spread.start(p)
    for c in range(2, count):
        load.launch(c)
    c_all[at.half, at.t] = c_own[...]
    if count > 1:
        load.forward(1)
    spread.pass_on()
    spread.pass_last()
    for c in range(2, count):
        load.forward(c)
    bring.finish()
    back.finish()
    spread.finish()
    for c in range(count):
        load.finish(c)


def forward(n_dp, hidden, gains, head_gains, wq, wk, wv, wo, cosine, sine, seg_ids, ffn, ident):
    size, width = hidden.shape
    n_tensor = seg_ids.shape[0] // size
    parts = ffn.shape[1]
    pieces = row_pieces(size, 10)
    count = len(pieces)
    head = wq.shape[1]
    vmem = pl.BlockSpec(memory_space=pltpu.VMEM)
    any_space = pl.BlockSpec(memory_space=pl.ANY)

    def low(*dims):
        return jax.ShapeDtypeStruct(dims, jnp.bfloat16)

    def full(*dims):
        return jax.ShapeDtypeStruct(dims, jnp.float32)

    def dma(*dims):
        return pltpu.SemaphoreType.DMA(dims)

    line, rest = dma(parts, 4), dma(parts, 4, n_dp // 4)
    blocked = (n_tensor, size)
    return pl.pallas_call(
        functools.partial(forward_body, n_dp, pieces),
        out_shape=[
            low(*blocked, width), full(*blocked, head), full(*blocked, wk.shape[1]),
            low(*blocked, head), low(n_tensor * size, wk.shape[1]), low(n_tensor * size, wv.shape[1]),
            full(*blocked, 1), low(*blocked, head), full(size, width), full(size, width),
            low(2, *blocked, width), low(parts, n_dp, *ffn.shape[2:]),
        ],
        in_specs=[vmem] * 11 + [any_space],
        out_specs=[vmem] * 11 + [any_space],
        scratch_shapes=[
            pltpu.VMEM((size, width), jnp.bfloat16), pltpu.VMEM((size, width), jnp.bfloat16),
            pltpu.VMEM((*blocked, width), jnp.bfloat16), pltpu.VMEM((2, size, width), jnp.bfloat16),
            pltpu.VMEM((size, width), jnp.bfloat16),
            dma(parts), line, line, rest, rest,
            dma(count), dma(count), dma(count + 1), dma(count + 1),
            dma(2), dma(2), dma(count), dma(count),
            dma(count), dma(count), dma(count), dma(count), dma(count), dma(count),
            dma(4, count), dma(4, count),
        ],
        compiler_params=pltpu.CompilerParams(
            collective_id=ident, has_side_effects=True, vmem_limit_bytes=56 * MIB
        ),
        name="forward",
    )(
        hidden, gains, head_gains, wq, wk, wv, wo,
        cosine.reshape(*blocked, -1), sine.reshape(*blocked, -1),
        seg_ids.reshape(*blocked, 1), seg_ids.reshape(1, -1), ffn,
    )


def by_rows(rows, body):
    step = SUBLANES if rows % SUBLANES == 0 else rows
    if step == rows:
        body(slice(None))
        return

    def one(i, carry):
        body(pl.ds(pl.multiple_of(i * step, step), step))
        return carry

    lax.fori_loop(0, rows // step, one, 0)


class Sums:
    def __init__(self, at, blocks, owns, landed, distant, rs, rr, zs, zr):
        self.at, self.blocks, self.owns, self.landed, self.distant = at, blocks, owns, landed, distant
        self.rs, self.rr, self.zs, self.zr = rs, rr, zs, zr
        self.turns = (2, 3, 1, 0)

    def across(self, c, k, r):
        at = self.at
        target = at.lines[k] * at.n_rest + at.rests[r]
        return send_to(
            at.rest_at[r], self.blocks[c](target), self.landed[c].at[k, r - 1],
            self.rs.at[c, k, r], self.rr.at[c, k, r],
        )

    def along(self, c, k):
        return send_to(
            self.at.line_at[k], self.landed[c].at[k, 0], self.distant[c].at[k - 1],
            self.zs.at[c, k], self.zr.at[c, k],
        )

    def start(self, c):
        for k in self.turns:
            for r in range(1, self.at.n_rest):
                self.across(c, k, r).start()

    def add(self, c, k):
        at, come = self.at, self.landed[c]
        for r in range(1, at.n_rest):
            self.across(c, k, r).wait_recv()
        own = self.owns[c](k)

        def one(rows):
            total = own[rows].astype(jnp.float32)
            for r in range(1, at.n_rest):
                total = total + come[k, r - 1, rows].astype(jnp.float32)
            come[k, 0, rows] = total.astype(jnp.bfloat16)

        by_rows(come.shape[2], one)
        if k:
            self.along(c, k).start()

    def arrive(self, c):
        for k in (1, 2, 3):
            self.along(c, k).wait_recv()

    def finish(self, c):
        for k in self.turns:
            for r in range(1, self.at.n_rest):
                self.across(c, k, r).wait_send()
            if k:
                self.along(c, k).wait_send()


def backward_body(
    n_dp, pieces,
    hidden, cot, back_rows, h_rows, u_rows, term_out, gains, head_gains, wq, wk, wv, wo,
    cosine, sine, seg_col, seg_row, a_all, q_raw, k_raw, q_rot, k_rot, v_all, lse, ctx, ffn,
    hidden_out, gains_out, wq_out, wo_out, kv_out, ffn_out,
    dh, du_own, du_all, parts, held, come, dctx, dv, dk, dq_low, dk_low, dv_low, wide,
    wq_part, wo_part, kv_part, kv_held, ffn_own, wq_in, wo_in, kv_in, ffn_in,
    wq_far, wo_far, kv_far, ffn_far, kv_pool, terms, pool_t, pool_r, pool_z,
    own_sem, rs, rr, zs, zr, ks, kr, gxs, gxr, gms, gmr, sms, smr, sfs, sfr, ts, tr, us, ur, vs, vr,
):
    at = Spot(n_dp)
    others = [at.mate, at.side, {"tensor": at.t_side_mate}]
    meet(others + at.line_at[1:] + at.rest_at[1:])
    n_ffn = ffn.shape[0]
    size = hidden.shape[0]
    c_wo, c_wq, c_kv = n_ffn, n_ffn + 1, n_ffn + 2
    factor = HD ** (-0.5)

    def of_ffn(c):
        return lambda dp: ffn.at[c, dp]

    def own_ffn(c):
        return lambda k: ffn_own.at[c, k]

    def of(ref):
        return lambda dp: ref.at[dp]

    def own(ref):
        return lambda k: ref.at[at.line_dp[k]]

    sums = Sums(
        at,
        [of_ffn(c) for c in range(n_ffn)] + [of(wo_part), of(wq_part), of(kv_held)],
        [own_ffn(c) for c in range(n_ffn)] + [own(wo_part), own(wq_part), own(kv_held)],
        [ffn_in.at[c] for c in range(n_ffn)] + [wo_in, wq_in, kv_in],
        [ffn_far.at[c] for c in range(n_ffn)] + [wo_far, wq_far, kv_far],
        rs, rr, zs, zr,
    )
    for c in range(n_ffn):
        sums.start(c)
    keep = [
        pltpu.make_async_copy(ffn.at[c, at.line_dp[k]], ffn_own.at[c, k], own_sem.at[c, k])
        for c in range(n_ffn)
        for k in range(4)
    ]
    for copy in keep:
        copy.start()
    steps = [(c, k) for c in range(n_ffn) for k in sums.turns]

    def pump(count):
        for _ in range(count):
            if steps:
                sums.add(*steps.pop(0))

    def gain(row):
        return gains[row : row + 1, :]

    def column_sum(values):
        return jnp.sum(values, axis=0, keepdims=True)

    width = hidden.shape[1]
    head = q_raw.shape[-1]
    terms[...] = jnp.zeros_like(terms)
    terms[3:4, :] = term_out[...]
    bring = Gather4(at, pieces, du_own, du_all, gxs, gxr, gms, gmr)
    sum_ffn = jnp.zeros((1, width), jnp.float32)
    sum_attn = jnp.zeros((1, width), jnp.float32)
    for p, piece in enumerate(pieces):
        rows = pl.ds(*piece)
        grad_norm, term = norm_back(h_rows[rows], gain(2), back_rows[rows])
        sum_ffn += column_sum(term)
        total = cot[rows].astype(jnp.float32) + grad_norm
        dh[rows] = total
        grad_u, term = norm_back(u_rows[rows], gain(1), total)
        sum_attn += column_sum(term)
        du_own[rows] = grad_u.astype(jnp.bfloat16)
        bring.over_x(p).start()
    terms[1:2, :] = sum_attn
    terms[2:3, :] = sum_ffn
    bring.near_own().start()
    du_all[at.t] = du_own[...]
    for copy in keep:
        copy.wait()

    def back_ctx(t):
        dctx[t] = dot(du_all[t], wo[...]).astype(jnp.bfloat16)

    back_ctx(at.t)
    bring.near_own().wait_recv()
    back_ctx(at.t_mate)
    bring.pass_on()
    back_ctx(at.t_side)
    bring.all_here()
    back_ctx(at.t_side_mate)
    n_tensor = du_all.shape[0]
    dr = wo_part.shape[1]

    def weight_grad(out, left, right):
        total = contract_rows(left[0], right[0])
        for t in range(1, n_tensor):
            total = total + contract_rows(left[t], right[t])
        wide[...] = total
        for i in range(n_dp):
            out[i] = wide[i * dr : (i + 1) * dr].astype(jnp.bfloat16)

    weight_grad(wo_part, du_all, ctx)
    sums.start(c_wo)
    pump(3)

    def attend_back(t):
        scores = contract_cols(q_rot[t], k_rot[...]) * factor
        row = lax.broadcasted_iota(jnp.int32, scores.shape, 0) + t * size
        behind = row - lax.broadcasted_iota(jnp.int32, scores.shape, 1)
        allowed = (seg_col[t] == seg_row[...]) & (behind >= 0) & (behind < WINDOW)
        probs = jnp.where(allowed, jnp.exp(scores - lse[t]), 0.0)
        grad_probs = contract_cols(dctx[t], v_all[...])
        delta = jnp.sum(probs * grad_probs, axis=-1, keepdims=True)
        grad_scores = (probs * (grad_probs - delta) * factor).astype(jnp.bfloat16)
        grad_q = dot(grad_scores, k_rot[...])
        low, term = norm_back(q_raw[t], head_gains[0:1, :], turn(grad_q, cosine[t], -sine[t]))
        dq_low[t] = low.astype(jnp.bfloat16)
        return (
            contract_rows(probs.astype(jnp.bfloat16), dctx[t]),
            contract_rows(grad_scores, q_rot[t]),
            column_sum(term),
        )

    add_v, add_k, sum_q = attend_back(0)
    dv[...] = add_v
    dk[...] = add_k
    for t in range(1, n_tensor):
        add_v, add_k, more = attend_back(t)
        dv[...] += add_v
        dk[...] += add_k
        sum_q += more
    sum_k = jnp.zeros((1, head), jnp.float32)
    for t in range(n_tensor):
        rows = pl.ds(t * size, size)
        low, term = norm_back(k_raw[t], head_gains[1:2, :], turn(dk[rows], cosine[t], -sine[t]))
        dk_low[t] = low.astype(jnp.bfloat16)
        sum_k += column_sum(term)
        dv_low[t] = dv[rows].astype(jnp.bfloat16)
    terms[4:5, :head] = sum_q
    terms[5:6, :head] = sum_k
    pump(2)

    def back_in(t):
        parts[t] = (
            contract_cols(dq_low[t], wq[...])
            + contract_cols(dk_low[t], wk[...])
            + contract_cols(dv_low[t], wv[...])
        ).astype(jnp.bfloat16)

    back = Scatter4(at, pieces, parts, held, come, sms, smr, sfs, sfr)
    back_in(at.t_side_mate)
    back.near(1).start()
    back_in(at.t_side)
    back.send_side()
    back_in(at.t_mate)
    back.near(0).start()
    back_in(at.t)
    weight_grad(kv_part.at[0], a_all, dk_low)
    weight_grad(kv_part.at[1], a_all, dv_low)
    mate_kv = send_to(at.mate, kv_part.at[1 - at.core], kv_held, ks.at[0], kr.at[0])
    mate_kv.start()
    weight_grad(wq_part, a_all, dq_low)
    sums.start(c_wq)
    mate_kv.wait()

    def pair_up(dp, carry):
        def add(rows):
            kv_held[dp, rows] = add_up(kv_part[at.core, dp, rows], kv_held[dp, rows]).astype(
                jnp.bfloat16
            )

        by_rows(kv_held.shape[1], add)
        return carry

    lax.fori_loop(0, n_dp, pair_up, 0)
    sums.start(c_kv)
    pump(1)
    back.near(0).wait_recv()
    sum_in = jnp.zeros((1, width), jnp.float32)
    for p, piece in enumerate(pieces):
        rows = pl.ds(*piece)
        back.far(p).wait_recv()
        total = add_up(parts[at.t, rows], held[0, rows]) + come[rows].astype(jnp.float32)
        grad_norm, term = norm_back(hidden[rows].astype(jnp.float32), gain(0), total)
        hidden_out[rows] = dh[rows] + grad_norm
        sum_in += column_sum(term)
    terms[0:1, :] = sum_in

    pool_t[at.t] = terms[...].astype(jnp.bfloat16)
    over_t = [
        send_to(where, pool_t.at[at.t], pool_t.at[at.t], ts.at[j], tr.at[j])
        for j, where in enumerate(others)
    ]
    for copy in over_t:
        copy.start()
    pump(2)
    for copy in over_t:
        copy.wait()
    total = pool_t[0].astype(jnp.float32)
    for t in range(1, n_tensor):
        total = total + pool_t[t].astype(jnp.float32)
    pool_r[at.rest] = total.astype(jnp.bfloat16)
    over_r = [
        send_to(at.rest_at[r], pool_r.at[at.rest], pool_r.at[at.rest], us.at[r], ur.at[r])
        for r in range(1, at.n_rest)
    ]
    for copy in over_r:
        copy.start()
    pump(len(steps))
    for copy in over_r:
        copy.wait()
    total = pool_r[0].astype(jnp.float32)
    for r in range(1, at.n_rest):
        total = total + pool_r[r].astype(jnp.float32)
    pool_z[at.line] = total.astype(jnp.bfloat16)
    over_z = [
        send_to(at.line_at[k], pool_z.at[at.line], pool_z.at[at.line], vs.at[k], vr.at[k])
        for k in (1, 2, 3)
    ]
    for copy in over_z:
        copy.start()
    for c in (c_wo, c_wq, c_kv):
        for k in sums.turns:
            sums.add(c, k)
    half_width = ffn.shape[-1]
    for c in range(n_ffn):
        sums.arrive(c)

        def finish(first, own=ffn_in.at[c, 0, 0], far=ffn_far.at[c], target=ffn_out.at[c]):
            def put(rows):
                same = add_up(own[rows], far[1, rows])
                cross = add_up(far[0, rows], far[2, rows])
                low, high = (same, cross) if first else (cross, same)
                target[rows, :half_width] = low
                target[rows, half_width:] = high[:, : target.shape[-1] - half_width]

            by_rows(own.shape[0], put)

        @pl.when(at.half == 0)
        def _(finish=finish):
            finish(True)

        @pl.when(at.half == 1)
        def _(finish=finish):
            finish(False)

    for copy in over_z:
        copy.wait()
    gains_out[...] = add_up(pool_z[0], pool_z[1]) + add_up(pool_z[2], pool_z[3])
    sums.arrive(c_wo)
    wo_out[...] = add_up(wo_in[0, 0], wo_far[0]) + add_up(wo_far[1], wo_far[2])
    sums.arrive(c_wq)
    wq_out[...] = add_up(wq_in[0, 0], wq_far[0]) + add_up(wq_far[1], wq_far[2])
    sums.arrive(c_kv)
    kv_pool[0] = (add_up(kv_in[0, 0], kv_far[0]) + add_up(kv_far[1], kv_far[2])).astype(jnp.bfloat16)
    kv_side = send_to(at.side, kv_pool.at[0], kv_pool.at[1], ks.at[1], kr.at[1])
    kv_side.start()
    kv_side.wait()
    kv_out[at.core] = add_up(kv_pool[0], kv_pool[1])
    give = send_to(at.mate, kv_out.at[at.core], kv_out.at[at.core], ks.at[2], kr.at[2])
    give.start()
    give.wait()
    for c in range(n_ffn + 3):
        sums.finish(c)
    bring.finish()
    back.finish()


def backward(
    n_dp, hidden, cot, back_rows, h_rows, u_rows, term_out, gains, head_gains, wq, wk, wv, wo,
    cosine, sine, seg_ids, a_all, q_raw, k_raw, q_rot, k_rot, v_all, lse, ctx, ffn, columns, ident,
):
    size, width = hidden.shape
    n_tensor = seg_ids.shape[0] // size
    n_ffn, _, dr, half_width = ffn.shape
    n_rest = n_dp // 4
    head = wq.shape[1]
    pieces = row_pieces(size, 10)
    count = len(pieces)
    vmem = pl.BlockSpec(memory_space=pltpu.VMEM)
    blocked = (n_tensor, size)

    def out(*dims):
        return jax.ShapeDtypeStruct(dims, jnp.float32)

    def low(*dims):
        return pltpu.VMEM(dims, jnp.bfloat16)

    def full(*dims):
        return pltpu.VMEM(dims, jnp.float32)

    def dma(*dims):
        return pltpu.SemaphoreType.DMA(dims)

    total = n_ffn + 3
    rows16 = -(-6 // SUBLANES) * SUBLANES
    return pl.pallas_call(
        functools.partial(backward_body, n_dp, pieces),
        out_shape=[
            out(size, width), out(rows16, width), out(dr, head), out(dr, head), out(2, dr, head),
            out(n_ffn, dr, columns),
        ],
        in_specs=[vmem] * 24 + [pl.BlockSpec(memory_space=pl.ANY)],
        out_specs=[vmem] * 6,
        scratch_shapes=[
            full(size, width), low(size, width), low(*blocked, width), low(*blocked, width),
            low(2, size, width), low(size, width), low(*blocked, head),
            full(n_tensor * size, head), full(n_tensor * size, head),
            low(*blocked, head), low(*blocked, head), low(*blocked, head), full(width, head),
            low(n_dp, dr, head), low(n_dp, dr, head), low(2, n_dp, dr, head), low(n_dp, dr, head),
            low(n_ffn, 4, dr, half_width),
            low(4, n_rest - 1, dr, head), low(4, n_rest - 1, dr, head), low(4, n_rest - 1, dr, head),
            low(n_ffn, 4, n_rest - 1, dr, half_width),
            low(3, dr, head), low(3, dr, head), low(3, dr, head), low(n_ffn, 3, dr, half_width),
            low(2, dr, head), full(rows16, width), low(n_tensor, rows16, width),
            low(n_rest, rows16, width), low(4, rows16, width),
            dma(n_ffn, 4), dma(total, 4, n_rest), dma(total, 4, n_rest), dma(total, 4), dma(total, 4),
            dma(3), dma(3), dma(count), dma(count), dma(count + 1), dma(count + 1),
            dma(2), dma(2), dma(count), dma(count),
            dma(3), dma(3), dma(n_rest), dma(n_rest), dma(4), dma(4),
        ],
        compiler_params=pltpu.CompilerParams(
            collective_id=ident, has_side_effects=True, vmem_limit_bytes=60 * MIB
        ),
        name="backward",
    )(
        hidden, cot, back_rows, h_rows, u_rows, term_out, gains, head_gains, wq, wk, wv, wo,
        cosine.reshape(*blocked, -1), sine.reshape(*blocked, -1),
        seg_ids.reshape(*blocked, 1), seg_ids.reshape(1, -1),
        a_all, q_raw, k_raw, q_rot, k_rot, v_all, lse, ctx, ffn,
    )


def pack_gains(blocks, width):
    n = blocks[0].shape[0]
    rows = [jnp.pad(block, ((0, 0), (0, width - block.shape[1]))) for block in blocks]
    packed = jnp.stack(rows, axis=1)
    return jnp.pad(packed, ((0, 0), (0, SUBLANES - len(blocks)), (0, 0)))


def local(
    n_dp,
    n_tensor,
    hidden,
    in_gain,
    w_query,
    w_key,
    w_value,
    query_gain,
    key_gain,
    w_output,
    attn_gain,
    ffn_gain,
    w_gate,
    w_up,
    w_down,
    out_gain,
    cotangent,
    segment_ids,
    positions,
):
    gains = (in_gain, attn_gain, ffn_gain, out_gain, query_gain, key_gain)
    width = -(-max(gain.shape[0] for gain in gains) // LANES) * LANES
    gain_rows = pack_gains([gain[None] for gain in gains], width)[0]
    columns = w_gate.shape[1]
    wide = -(-columns // (2 * LANES)) * LANES
    ffn = jnp.stack([w_gate, w_up, w_down.T])
    ffn = jnp.pad(ffn, ((0, 0), (0, 0), (0, 2 * wide - columns)))
    ffn = jnp.stack([ffn[:, :, :wide], ffn[:, :, wide:]])
    gains_all, wq_all, wo_all, kv_all = attention_weights(
        n_dp, gain_rows, w_query, w_output.T, jnp.stack([w_key, w_value]), 0
    )
    full_in_gain, full_attn_gain, full_ffn_gain, full_out_gain, full_qgain, full_kgain = (
        gains_all[:, row, : gain.shape[0]].reshape(-1).astype(jnp.float32)
        for row, gain in enumerate(gains)
    )
    full_query, full_output = (block.reshape(-1, block.shape[-1]) for block in (wq_all, wo_all))
    full_key, full_value = (kv_all[i].reshape(-1, kv_all.shape[-1]) for i in range(2))
    cosine, sine_table = rotary_tables(positions, HD)
    wide_gains = jnp.stack([full_in_gain, full_attn_gain, full_ffn_gain, full_out_gain])
    head_gains = jnp.stack([full_qgain, full_kgain])
    (
        normed_in, query_raw, key_raw, query_rot, key_rot, value_rows, log_total, context,
        attn_rows, residual, ffn_in, ffn_all,
    ) = forward(
        n_dp,
        hidden,
        wide_gains,
        head_gains,
        full_query, full_key, full_value, full_output, cosine, sine_table, segment_ids, ffn, 1,
    )
    ffn_in = ffn_in.reshape(-1, ffn_in.shape[-1])
    full_gate, full_up, full_down = (ffn_all[i].reshape(-1, wide) for i in range(3))
    gate_pre = jnp.dot(ffn_in, full_gate, preferred_element_type=jnp.float32)
    up_pre = jnp.dot(ffn_in, full_up, preferred_element_type=jnp.float32)
    gelu_values, gelu_back = jax.vjp(gelu_tanh, gate_pre)
    mixed = (gelu_values * up_pre).astype(jnp.bfloat16)
    down_part = contract_cols(mixed, full_down)
    down_rows = scatter8(
        n_dp, down_part.astype(jnp.bfloat16).reshape(2, n_tensor, -1, down_part.shape[-1]), 4
    )
    output = (residual + apply_norm(down_rows, full_out_gain)).astype(jnp.bfloat16)
    cot_f = cotangent.astype(jnp.float32)
    grad_down, term_out = norm_back(down_rows, full_out_gain, cot_f)
    down_all = gather8(n_dp, grad_down.astype(jnp.bfloat16), 5).reshape(-1, grad_down.shape[-1])
    grad_wd = contract_rows(down_all, mixed)
    grad_mixed = jnp.dot(down_all, full_down, preferred_element_type=jnp.float32)
    gate_low = gelu_back(grad_mixed * up_pre)[0].astype(jnp.bfloat16)
    up_low = (grad_mixed * gelu_values).astype(jnp.bfloat16)
    grad_wg = contract_rows(ffn_in, gate_low)
    grad_wu = contract_rows(ffn_in, up_low)
    ffn_part = contract_cols(gate_low, full_gate) + contract_cols(up_low, full_up)
    ffn_back = scatter8(
        n_dp, ffn_part.astype(jnp.bfloat16).reshape(2, n_tensor, -1, ffn_part.shape[-1]), 6
    )
    grad_hidden, gain_sums, own_query, own_output, own_kv, own_ffn_weights = backward(
        n_dp, hidden, cotangent, ffn_back, residual, attn_rows,
        jnp.sum(term_out, axis=0, keepdims=True), wide_gains, head_gains,
        full_query, full_key, full_value, full_output, cosine, sine_table, segment_ids,
        normed_in, query_raw, key_raw, query_rot, key_rot, value_rows, log_total, context,
        jnp.stack(
            [
                grad.astype(jnp.bfloat16).reshape(n_dp, -1, grad.shape[-1])
                for grad in (grad_wd, grad_wg, grad_wu)
            ]
        ),
        columns,
        9,
    )
    place = lax.axis_index("dp")
    own_in, own_attn, own_ffn, own_out, own_q, own_k = (
        lax.dynamic_slice(gain_sums[row], (place * gain.shape[0],), gain.shape)
        for row, gain in enumerate(gains)
    )
    return (
        output,
        grad_hidden,
        own_in,
        own_query,
        own_kv[0],
        own_kv[1],
        own_q,
        own_k,
        own_output.T,
        own_attn,
        own_ffn,
        own_ffn_weights[1],
        own_ffn_weights[2],
        own_ffn_weights[0].T,
        own_out,
    )


def solution(mesh):
    placed = (
        P(("dp", "tensor"), None),
        P("dp"),
        P("dp", "tensor"),
        P("dp", None),
        P("dp", None),
        P("dp"),
        P("dp"),
        P("tensor", "dp"),
        P("dp"),
        P("dp"),
        P("dp", "tensor"),
        P("dp", "tensor"),
        P("tensor", "dp"),
        P("dp"),
        P(("dp", "tensor"), None),
        P("dp"),
        P("dp"),
    )
    return jax.shard_map(
        functools.partial(local, mesh.shape["dp"], mesh.shape["tensor"]),
        mesh=mesh,
        in_specs=placed,
        out_specs=(
            P(("dp", "tensor"), None),
            P(("dp", "tensor"), None),
            P("dp"),
            P("dp", "tensor"),
            P("dp", None),
            P("dp", None),
            P("dp"),
            P("dp"),
            P("tensor", "dp"),
            P("dp"),
            P("dp"),
            P("dp", "tensor"),
            P("dp", "tensor"),
            P("tensor", "dp"),
            P("dp"),
        ),
        check_vma=False,
    )
```

```python
import functools
import math

import jax
import jax.numpy as jnp
from jax import lax
from jax.experimental import pallas as pl
from jax.experimental.pallas import tpu as pltpu
from jax.sharding import PartitionSpec as P

HD = 256
WINDOW = 512


EPSILON = 1e-06
ROPE_BASE = 10000.0


def rms_scale(values):
    return lax.rsqrt(jnp.mean(values * values, axis=-1, keepdims=True) + EPSILON)


def apply_norm(values, gain_vec):
    return values * rms_scale(values) * gain_vec.astype(jnp.float32)


def norm_back(values, gain_vec, upstream):
    factor = rms_scale(values)
    unit_rows = values * factor
    scaled = upstream * gain_vec.astype(jnp.float32)
    grad_values = factor * (
        scaled - unit_rows * jnp.mean(scaled * unit_rows, axis=-1, keepdims=True)
    )
    return (grad_values, upstream * unit_rows)


def rotary_tables(token_pos, width):
    steps_half = jnp.arange(width // 2, dtype=jnp.float32)
    frequency = ROPE_BASE ** (-2.0 * steps_half / width)
    angles = token_pos.astype(jnp.float32)[:, None] * frequency[None, :]
    return (jnp.cos(angles), jnp.sin(angles))


def gelu_tanh(values):
    return jax.nn.gelu(values, approximate=True)


def contract_rows(left, right):
    return lax.dot_general(
        left, right, (((0,), (0,)), ((), ())), preferred_element_type=jnp.float32
    )


def contract_cols(left, right):
    return lax.dot_general(
        left, right, (((1,), (1,)), ((), ())), preferred_element_type=jnp.float32
    )


MESH = pl.DeviceIdType.MESH
LANES = 128
SUBLANES = 16
MIB = 1024 * 1024
LAYER_VMEM = 63 * MIB
GELU_SCALE = (2.0 / math.pi) ** 0.5
GELU_CUBE = 0.044715


def send_to(where, src, dst, send, recv):
    return pltpu.make_async_remote_copy(
        src_ref=src,
        dst_ref=dst,
        send_sem=send,
        recv_sem=recv,
        device_id=where,
        device_id_type=MESH,
    )


def meet(partners):
    barrier = pltpu.get_barrier_semaphore()
    for where in partners:
        pl.semaphore_signal(barrier, inc=1, device_id=where, device_id_type=MESH)
    pl.semaphore_wait(barrier, len(partners))


class Spot:
    def __init__(self, n_dp):
        self.n_rest = n_dp // 4
        self.dp = lax.axis_index("dp")
        self.t = lax.axis_index("tensor")
        self.x = self.t // 2
        self.core = self.t - 2 * self.x
        self.line = self.dp // self.n_rest
        self.rest = self.dp - self.line * self.n_rest
        self.half = self.line % 2
        high = self.line // 2
        self.lines = [
            self.line,
            2 * high + 1 - self.half,
            2 * (1 - high) + self.half,
            2 * (1 - high) + 1 - self.half,
        ]
        self.line_dp = [line * self.n_rest + self.rest for line in self.lines]
        self.line_at = [{"dp": dp} for dp in self.line_dp]
        self.rests = [(self.rest + r) % self.n_rest for r in range(self.n_rest)]
        self.rest_at = [{"dp": self.line * self.n_rest + rest} for rest in self.rests]
        self.from_rest = [
            (self.rest + self.n_rest - r) % self.n_rest for r in range(self.n_rest)
        ]
        self.t_mate = 2 * self.x + 1 - self.core
        self.t_side = 2 * (1 - self.x) + self.core
        self.t_side_mate = 2 * (1 - self.x) + 1 - self.core
        self.mate = {"tensor": self.t_mate}
        self.side = {"tensor": self.t_side}
        self.pair = self.line_at[1]


def row_pieces(rows, wanted):
    cuts = wanted if rows % (wanted * SUBLANES) == 0 else 1
    size = rows // cuts
    return [(cut * size, size) for cut in range(cuts)]


def gather8_body(n_dp, pieces, mine, full, own_sem, xs, xr, zs, zr, ds, dr, ms, mr):
    at = Spot(n_dp)
    meet([at.mate, at.side, at.pair])
    half, other = at.half, 1 - at.half

    def cut(ref, p):
        return ref.at[pl.ds(*pieces[p])]

    def over_x(p):
        return send_to(at.side, cut(mine, p), cut(full.at[half, at.t], p), xs.at[p], xr.at[p])

    def over_z(p):
        return send_to(at.pair, cut(mine, p), cut(full.at[half, at.t], p), zs.at[p], zr.at[p])

    def onward(p):
        if p % 2 == 0:
            block = cut(full.at[half, at.t_side], p)
            return send_to(at.pair, block, block, ds.at[p], dr.at[p])
        block = cut(full.at[other, at.t], p)
        return send_to(at.side, block, block, ds.at[p], dr.at[p])

    def near(j, p):
        place = cut(full.at[(half, half, other, other)[j], (at.t, at.t_side, at.t, at.t_side)[j]], p)
        source = cut(mine, p) if j == 0 else place
        return send_to(at.mate, source, place, ms.at[j, p], mr.at[j, p])

    count = len(pieces)
    for p in range(count):
        over_x(p).start()
        over_z(p).start()
    own = pltpu.make_async_copy(mine, full.at[half, at.t], own_sem)
    own.start()
    for p in range(count):
        near(0, p).start()
    for p in range(count):
        over_x(p).wait_recv()
        if p % 2 == 0:
            onward(p).start()
        near(1, p).start()
        over_z(p).wait_recv()
        if p % 2 == 1:
            onward(p).start()
        near(2, p).start()
    for p in range(count):
        onward(p).wait_recv()
        near(3, p).start()
    own.wait()
    for p in range(count):
        over_x(p).wait_send()
        over_z(p).wait_send()
        onward(p).wait_send()
        for j in range(4):
            near(j, p).wait()


def gather8(n_dp, block, ident):
    pieces = row_pieces(block.shape[0], 10)
    count = len(pieces)
    one = pltpu.SemaphoreType.DMA((count,))
    four = pltpu.SemaphoreType.DMA((4, count))
    return pl.pallas_call(
        functools.partial(gather8_body, n_dp, pieces),
        out_shape=jax.ShapeDtypeStruct((2, 4, *block.shape), block.dtype),
        in_specs=[pl.BlockSpec(memory_space=pltpu.VMEM)],
        out_specs=pl.BlockSpec(memory_space=pl.ANY),
        scratch_shapes=[pltpu.SemaphoreType.DMA, one, one, one, one, one, one, four, four],
        compiler_params=pltpu.CompilerParams(collective_id=ident, has_side_effects=True),
        name=f"gather8_{ident}",
    )(block)


def add_up(left, right):
    return left.astype(jnp.float32) + right.astype(jnp.float32)


def scatter8_body(
    n_dp, pieces, parts, out, held, come, last, ms, mr, fs, fr, ls, lr
):
    at = Spot(n_dp)
    meet([at.mate, at.side, at.pair])
    half, other = at.half, 1 - at.half
    halves = (half, half, other, other)
    mine_t = (at.t, at.t_side, at.t, at.t_side)
    mate_t = (at.t_mate, at.t_side_mate, at.t_mate, at.t_side_mate)
    count = len(pieces)

    def near(k, p):
        rows = pl.ds(*pieces[p])
        return send_to(
            at.mate, parts.at[halves[k], mate_t[k], rows], held.at[k, rows], ms.at[k, p], mr.at[k, p]
        )

    def first(j, p):
        rows = pl.ds(*pieces[p])
        if p % 2 == 0:
            return send_to(at.side, held.at[(1, 3)[j], rows], come.at[j, rows], fs.at[j, p], fr.at[j, p])
        return send_to(at.pair, held.at[(2, 3)[j], rows], come.at[j, rows], fs.at[j, p], fr.at[j, p])

    def second(p):
        rows = pl.ds(*pieces[p])
        if p % 2 == 0:
            return send_to(at.pair, held.at[2, rows], last.at[rows], ls.at[p], lr.at[p])
        return send_to(at.side, held.at[1, rows], last.at[rows], ls.at[p], lr.at[p])

    for p in range(count):
        for k in (3, 1, 2, 0):
            near(k, p).start()
    for p in range(count):
        rows = pl.ds(*pieces[p])
        for k in (3, 1, 2, 0):
            near(k, p).wait_recv()
            held[k, rows] = add_up(parts[halves[k], mine_t[k], rows], held[k, rows]).astype(jnp.bfloat16)
        first(1, p).start()
        first(0, p).start()
    for p in range(count):
        rows = pl.ds(*pieces[p])
        keep = 2 if p % 2 == 0 else 1
        first(1, p).wait_recv()
        held[keep, rows] = add_up(held[keep, rows], come[1, rows]).astype(jnp.bfloat16)
        second(p).start()
        first(0, p).wait_recv()
        out[rows] = add_up(held[0, rows], come[0, rows])
    for p in range(count):
        rows = pl.ds(*pieces[p])
        second(p).wait_recv()
        out[rows] = out[rows] + last[rows].astype(jnp.float32)
    for p in range(count):
        for k in range(4):
            near(k, p).wait_send()
        for j in range(2):
            first(j, p).wait_send()
        second(p).wait_send()


def scatter8(n_dp, parts, ident):
    rows, width = parts.shape[2:]
    pieces = row_pieces(rows, 10)
    count = len(pieces)

    def sems(*shape):
        return pltpu.SemaphoreType.DMA((*shape, count))

    return pl.pallas_call(
        functools.partial(scatter8_body, n_dp, pieces),
        out_shape=jax.ShapeDtypeStruct((rows, width), jnp.float32),
        in_specs=[pl.BlockSpec(memory_space=pltpu.VMEM)],
        out_specs=pl.BlockSpec(memory_space=pltpu.VMEM),
        scratch_shapes=[
            pltpu.VMEM((4, rows, width), jnp.bfloat16),
            pltpu.VMEM((2, rows, width), jnp.bfloat16),
            pltpu.VMEM((rows, width), jnp.bfloat16),
            sems(4), sems(4), sems(2), sems(2), sems(), sems(),
        ],
        compiler_params=pltpu.CompilerParams(
            collective_id=ident, has_side_effects=True, vmem_limit_bytes=40 * MIB
        ),
        name=f"scatter8_{ident}",
    )(parts)


def weights_body(
    n_dp, gains, wq, wo, kv, gains_all, wq_all, wo_all, kv_all, own_sem, zs, zr, rs, rr, ks, kr
):
    at = Spot(n_dp)
    meet([at.mate] + at.line_at[1:] + at.rest_at[1:])

    def source(c):
        return kv.at[at.core] if c == 3 else (gains, wq, wo)[c]

    def place(c, dp):
        return kv_all.at[at.core, dp] if c == 3 else (gains_all, wq_all, wo_all)[c].at[dp]

    def along(c, k):
        return send_to(at.line_at[k], source(c), place(c, at.dp), zs.at[c, k], zr.at[c, k])

    def across(c, k, r):
        spot = place(c, at.line_dp[k])
        return send_to(
            at.rest_at[r], source(c) if k == 0 else spot, spot, rs.at[c, k, r], rr.at[c, k, r]
        )

    order = (0, 3, 1, 2)
    for c in order:
        for k in (1, 2, 3):
            along(c, k).start()
        for r in range(1, at.n_rest):
            across(c, 0, r).start()
    own = [pltpu.make_async_copy(source(c), place(c, at.dp), own_sem.at[c]) for c in order]
    for copy in own:
        copy.start()
    for c in order:
        for k in (1, 2, 3):
            along(c, k).wait_recv()
            for r in range(1, at.n_rest):
                across(c, k, r).start()
    for copy in own:
        copy.wait()
    share = send_to(at.mate, kv_all.at[at.core], kv_all.at[at.core], ks, kr)
    for c in (3, 0, 1, 2):
        for k in range(4):
            for r in range(1, at.n_rest):
                across(c, k, r).wait()
            if k:
                along(c, k).wait_send()
        if c == 3:
            share.start()
    share.wait()


def attention_weights(n_dp, gains, wq, wo, kv, ident):
    line = pltpu.SemaphoreType.DMA((4, 4))
    rest = pltpu.SemaphoreType.DMA((4, 4, n_dp // 4))
    any_space = pl.BlockSpec(memory_space=pl.ANY)

    def shape(*dims):
        return jax.ShapeDtypeStruct(dims, jnp.bfloat16)

    return pl.pallas_call(
        functools.partial(weights_body, n_dp),
        out_shape=[
            shape(n_dp, *gains.shape), shape(n_dp, *wq.shape), shape(n_dp, *wo.shape),
            shape(2, n_dp, *kv.shape[1:]),
        ],
        in_specs=[pl.BlockSpec(memory_space=pltpu.VMEM)] * 4,
        out_specs=[any_space] * 4,
        scratch_shapes=[
            pltpu.SemaphoreType.DMA((4,)), line, line, rest, rest,
            pltpu.SemaphoreType.DMA, pltpu.SemaphoreType.DMA,
        ],
        compiler_params=pltpu.CompilerParams(collective_id=ident, has_side_effects=True),
        name="attention_weights",
    )(gains, wq, wo, kv)


class Background:
    def __init__(self, at, ffn, ffn_all, own_sem, zs, zr, rs, rr):
        self.at, self.ffn, self.ffn_all = at, ffn, ffn_all
        self.own_sem, self.zs, self.zr, self.rs, self.rr = own_sem, zs, zr, rs, rr
        self.halves = (at.half, 1 - at.half, at.half, 1 - at.half)

    def along(self, c, k):
        at = self.at
        return send_to(
            at.line_at[k], self.ffn.at[self.halves[k], c], self.ffn_all.at[c, at.dp],
            self.zs.at[c, k], self.zr.at[c, k],
        )

    def across(self, c, k, r):
        at = self.at
        spot = self.ffn_all.at[c, at.line_dp[k]]
        source = self.ffn.at[at.half, c] if k == 0 else spot
        return send_to(at.rest_at[r], source, spot, self.rs.at[c, k, r], self.rr.at[c, k, r])

    def own(self, c):
        at = self.at
        return pltpu.make_async_copy(
            self.ffn.at[at.half, c], self.ffn_all.at[c, at.dp], self.own_sem.at[c]
        )

    def launch(self, c):
        for k in (2, 3, 1):
            self.along(c, k).start()
        for r in range(1, self.at.n_rest):
            self.across(c, 0, r).start()
        self.own(c).start()

    def forward(self, c, ks=(2, 3, 1)):
        for k in ks:
            self.along(c, k).wait_recv()
            for r in range(1, self.at.n_rest):
                self.across(c, k, r).start()

    def finish(self, c):
        self.own(c).wait()
        for k in range(4):
            for r in range(1, self.at.n_rest):
                self.across(c, k, r).wait()
            if k:
                self.along(c, k).wait_send()


def dot(left, right):
    return jnp.dot(left, right, preferred_element_type=jnp.float32)


def turn(values, cosine, sine_table):
    half_width = values.shape[-1] // 2
    first_half = values[:, :half_width]
    second = values[:, half_width:]
    return jnp.concatenate(
        [first_half * cosine - second * sine_table, second * cosine + first_half * sine_table],
        axis=-1,
    )


class Gather4:
    def __init__(self, at, pieces, mine, full, xs, xr, ms, mr):
        self.at, self.pieces, self.mine, self.full = at, pieces, mine, full
        self.xs, self.xr, self.ms, self.mr = xs, xr, ms, mr

    def over_x(self, p):
        rows, at = pl.ds(*self.pieces[p]), self.at
        return send_to(
            at.side, self.mine.at[rows], self.full.at[at.t, rows], self.xs.at[p], self.xr.at[p]
        )

    def near(self, p):
        rows, at = pl.ds(*self.pieces[p]), self.at
        block = self.full.at[at.t_side, rows]
        return send_to(at.mate, block, block, self.ms.at[p], self.mr.at[p])

    def near_own(self):
        at, p = self.at, len(self.pieces)
        return send_to(at.mate, self.mine, self.full.at[at.t], self.ms.at[p], self.mr.at[p])

    def start(self):
        for p in range(len(self.pieces)):
            self.over_x(p).start()
        self.near_own().start()

    def pass_on(self):
        for p in range(len(self.pieces)):
            self.over_x(p).wait_recv()
            self.near(p).start()

    def all_here(self):
        for p in range(len(self.pieces)):
            self.near(p).wait_recv()

    def finish(self):
        self.near_own().wait_send()
        for p in range(len(self.pieces)):
            self.over_x(p).wait_send()
            self.near(p).wait_send()


class Scatter4:
    def __init__(self, at, pieces, parts, held, come, ms, mr, fs, fr):
        self.at, self.pieces, self.parts, self.held, self.come = at, pieces, parts, held, come
        self.ms, self.mr, self.fs, self.fr = ms, mr, fs, fr
        self.mate_t = (at.t_mate, at.t_side_mate)

    def near(self, k):
        return send_to(
            self.at.mate, self.parts.at[self.mate_t[k]], self.held.at[k], self.ms.at[k], self.mr.at[k]
        )

    def far(self, p):
        rows = pl.ds(*self.pieces[p])
        return send_to(
            self.at.side, self.held.at[1, rows], self.come.at[rows], self.fs.at[p], self.fr.at[p]
        )

    def send_side(self):
        self.near(1).wait_recv()
        for p, piece in enumerate(self.pieces):
            rows = pl.ds(*piece)
            self.held[1, rows] = add_up(self.parts[self.at.t_side, rows], self.held[1, rows]).astype(
                jnp.bfloat16
            )
            self.far(p).start()

    def result(self, out):
        self.near(0).wait_recv()
        for p, piece in enumerate(self.pieces):
            rows = pl.ds(*piece)
            self.far(p).wait_recv()
            out[rows] = add_up(self.parts[self.at.t, rows], self.held[0, rows]) + self.come[
                rows
            ].astype(jnp.float32)

    def finish(self):
        for k in range(2):
            self.near(k).wait_send()
        for p in range(len(self.pieces)):
            self.far(p).wait_send()


class Gather8:
    def __init__(self, at, pieces, mine, full, xs, xr, zs, zr, ds, dr, ms, mr):
        self.at, self.pieces, self.mine, self.full = at, pieces, mine, full
        self.xs, self.xr, self.zs, self.zr = xs, xr, zs, zr
        self.ds, self.dr, self.ms, self.mr = ds, dr, ms, mr

    def spot(self, z, t, p):
        return self.full.at[z, t, pl.ds(*self.pieces[p])]

    def over_x(self, p):
        at = self.at
        return send_to(
            at.side, self.mine.at[pl.ds(*self.pieces[p])], self.spot(at.half, at.t, p),
            self.xs.at[p], self.xr.at[p],
        )

    def over_z(self, p):
        at = self.at
        return send_to(
            at.pair, self.mine.at[pl.ds(*self.pieces[p])], self.spot(at.half, at.t, p),
            self.zs.at[p], self.zr.at[p],
        )

    def onward(self, p):
        at = self.at
        if p % 2 == 0:
            block = self.spot(at.half, at.t_side, p)
            return send_to(at.pair, block, block, self.ds.at[p], self.dr.at[p])
        block = self.spot(1 - at.half, at.t, p)
        return send_to(at.side, block, block, self.ds.at[p], self.dr.at[p])

    def near(self, j, p):
        at = self.at
        z = (at.half, at.half, 1 - at.half, 1 - at.half)[j]
        place = self.spot(z, (at.t, at.t_side, at.t, at.t_side)[j], p)
        source = self.mine.at[pl.ds(*self.pieces[p])] if j == 0 else place
        return send_to(at.mate, source, place, self.ms.at[j, p], self.mr.at[j, p])

    def start(self, p):
        self.over_x(p).start()
        self.over_z(p).start()
        self.near(0, p).start()

    def pass_on(self):
        for p in range(len(self.pieces)):
            self.over_x(p).wait_recv()
            if p % 2 == 0:
                self.onward(p).start()
            self.near(1, p).start()
            self.over_z(p).wait_recv()
            if p % 2 == 1:
                self.onward(p).start()
            self.near(2, p).start()

    def pass_last(self):
        for p in range(len(self.pieces)):
            self.onward(p).wait_recv()
            self.near(3, p).start()

    def here(self, j):
        for p in range(len(self.pieces)):
            self.near(j, p).wait_recv()

    def finish(self):
        for p in range(len(self.pieces)):
            self.over_x(p).wait_send()
            self.over_z(p).wait_send()
            self.onward(p).wait_send()
            for j in range(4):
                self.near(j, p).wait_send()


def forward_body(
    n_dp, pieces,
    hidden, gains, head_gains, wq, wk, wv, wo, cosine, sine, seg_col, seg_row, ffn,
    a_all, q_raw, k_raw, q_rot, k_rot, v_all, lse, ctx, u_out, h_out, c_all, ffn_all,
    a_own, c_own, parts, held, come,
    own_sem, bzs, bzr, brs, brr, gxs, gxr, gms, gmr, sms, smr, sfs, sfr,
    xs, xr, zs, zr, ds, dr, ms, mr,
):
    at = Spot(n_dp)
    meet([at.mate, at.side] + at.line_at[1:] + at.rest_at[1:])
    load = Background(at, ffn, ffn_all, own_sem, bzs, bzr, brs, brr)
    count = ffn.shape[1]
    size = hidden.shape[0]
    load.launch(0)
    if count > 1:
        load.launch(1)

    def gain(row):
        return gains[row : row + 1, :]

    bring = Gather4(at, pieces, a_own, a_all, gxs, gxr, gms, gmr)
    for piece in pieces:
        rows = pl.ds(*piece)
        a_own[rows] = apply_norm(hidden[rows].astype(jnp.float32), gain(0)).astype(jnp.bfloat16)
    bring.start()
    a_all[at.t] = a_own[...]

    def project(t):
        rows = pl.ds(pl.multiple_of(t * size, SUBLANES), size)
        a = a_all[t]
        q = dot(a, wq[...])
        q_raw[t] = q
        q_rot[t] = turn(apply_norm(q, head_gains[0:1, :]), cosine[t], sine[t]).astype(jnp.bfloat16)
        k = dot(a, wk[...])
        k_raw[t] = k
        k_rot[rows] = turn(apply_norm(k, head_gains[1:2, :]), cosine[t], sine[t]).astype(
            jnp.bfloat16
        )
        v_all[rows] = dot(a, wv[...]).astype(jnp.bfloat16)

    project(at.t)
    bring.near_own().wait_recv()
    project(at.t_mate)
    bring.pass_on()
    project(at.t_side)
    bring.all_here()
    project(at.t_side_mate)

    def attend(t):
        scores = contract_cols(q_rot[t], k_rot[...]) * HD ** (-0.5)
        row = lax.broadcasted_iota(jnp.int32, scores.shape, 0) + t * size
        behind = row - lax.broadcasted_iota(jnp.int32, scores.shape, 1)
        allowed = (seg_col[t] == seg_row[...]) & (behind >= 0) & (behind < WINDOW)
        weights = jnp.where(allowed, jnp.exp(scores), 0.0)
        total = jnp.sum(weights, axis=-1, keepdims=True)
        lse[t] = jnp.log(total)
        mixed = dot((weights / total).astype(jnp.bfloat16), v_all[...]).astype(jnp.bfloat16)
        ctx[t] = mixed
        parts[t] = contract_cols(mixed, wo[...]).astype(jnp.bfloat16)

    back = Scatter4(at, pieces, parts, held, come, sms, smr, sfs, sfr)
    attend(at.t_side_mate)
    back.near(1).start()
    attend(at.t_side)
    back.send_side()
    attend(at.t_mate)
    back.near(0).start()
    attend(at.t)
    load.forward(0)
    back.result(u_out)
    spread = Gather8(at, pieces, c_own, c_all, xs, xr, zs, zr, ds, dr, ms, mr)
    for p, piece in enumerate(pieces):
        rows = pl.ds(*piece)
        total = hidden[rows].astype(jnp.float32) + apply_norm(u_out[rows], gain(1))
        h_out[rows] = total
        c_own[rows] = apply_norm(total, gain(2)).astype(jnp.bfloat16)
        spread.start(p)
    for c in range(2, count):
        load.launch(c)
    c_all[at.half, at.t] = c_own[...]
    if count > 1:
        load.forward(1)
    spread.pass_on()
    spread.pass_last()
    for c in range(2, count):
        load.forward(c)
    for k in range(4):
        spread.here(k)
    bring.finish()
    back.finish()
    spread.finish()
    for c in range(count):
        load.finish(c)


def forward(n_dp, hidden, gains, head_gains, wq, wk, wv, wo, cosine, sine, seg_ids, ffn, ident):
    size, width = hidden.shape
    n_tensor = seg_ids.shape[0] // size
    parts = ffn.shape[1]
    pieces = row_pieces(size, 10)
    count = len(pieces)
    head = wq.shape[1]
    vmem = pl.BlockSpec(memory_space=pltpu.VMEM)
    any_space = pl.BlockSpec(memory_space=pl.ANY)

    def low(*dims):
        return jax.ShapeDtypeStruct(dims, jnp.bfloat16)

    def full(*dims):
        return jax.ShapeDtypeStruct(dims, jnp.float32)

    def dma(*dims):
        return pltpu.SemaphoreType.DMA(dims)

    line, rest = dma(parts, 4), dma(parts, 4, n_dp // 4)
    blocked = (n_tensor, size)
    return pl.pallas_call(
        functools.partial(forward_body, n_dp, pieces),
        out_shape=[
            low(*blocked, width), full(*blocked, head), full(*blocked, wk.shape[1]),
            low(*blocked, head), low(n_tensor * size, wk.shape[1]), low(n_tensor * size, wv.shape[1]),
            full(*blocked, 1), low(*blocked, head), full(size, width), full(size, width),
            low(2, *blocked, width), low(parts, n_dp, *ffn.shape[2:]),
        ],
        in_specs=[vmem] * 11 + [any_space],
        out_specs=[vmem] * 11 + [any_space],
        scratch_shapes=[
            pltpu.VMEM((size, width), jnp.bfloat16), pltpu.VMEM((size, width), jnp.bfloat16),
            pltpu.VMEM((*blocked, width), jnp.bfloat16), pltpu.VMEM((2, size, width), jnp.bfloat16),
            pltpu.VMEM((size, width), jnp.bfloat16),
            dma(parts), line, line, rest, rest,
            dma(count), dma(count), dma(count + 1), dma(count + 1),
            dma(2), dma(2), dma(count), dma(count),
            dma(count), dma(count), dma(count), dma(count), dma(count), dma(count),
            dma(4, count), dma(4, count),
        ],
        compiler_params=pltpu.CompilerParams(
            collective_id=ident, has_side_effects=True, vmem_limit_bytes=56 * MIB
        ),
        name="forward",
    )(
        hidden, gains, head_gains, wq, wk, wv, wo,
        cosine.reshape(*blocked, -1), sine.reshape(*blocked, -1),
        seg_ids.reshape(*blocked, 1), seg_ids.reshape(1, -1), ffn,
    )


def by_rows(rows, body):
    step = SUBLANES if rows % SUBLANES == 0 else rows
    if step == rows:
        body(slice(None))
        return

    def one(i, carry):
        body(pl.ds(pl.multiple_of(i * step, step), step))
        return carry

    lax.fori_loop(0, rows // step, one, 0)


class Sums:
    def __init__(self, at, blocks, owns, landed, distant, rs, rr, zs, zr):
        self.at, self.blocks, self.owns, self.landed, self.distant = at, blocks, owns, landed, distant
        self.rs, self.rr, self.zs, self.zr = rs, rr, zs, zr
        self.turns = (2, 3, 1, 0)

    def across(self, c, k, r):
        at = self.at
        target = at.lines[k] * at.n_rest + at.rests[r]
        return send_to(
            at.rest_at[r], self.blocks[c](target), self.landed[c].at[k, r - 1],
            self.rs.at[c, k, r], self.rr.at[c, k, r],
        )

    def along(self, c, k):
        return send_to(
            self.at.line_at[k], self.landed[c].at[k, 0], self.distant[c].at[k - 1],
            self.zs.at[c, k], self.zr.at[c, k],
        )

    def start(self, c):
        for k in self.turns:
            for r in range(1, self.at.n_rest):
                self.across(c, k, r).start()

    def add(self, c, k):
        at, come = self.at, self.landed[c]
        for r in range(1, at.n_rest):
            self.across(c, k, r).wait_recv()
        own = self.owns[c](k)

        def one(rows):
            total = own[rows].astype(jnp.float32)
            for r in range(1, at.n_rest):
                total = total + come[k, r - 1, rows].astype(jnp.float32)
            come[k, 0, rows] = total.astype(jnp.bfloat16)

        by_rows(come.shape[2], one)
        if k:
            self.along(c, k).start()

    def arrive(self, c):
        for k in (1, 2, 3):
            self.along(c, k).wait_recv()

    def finish(self, c):
        for k in self.turns:
            for r in range(1, self.at.n_rest):
                self.across(c, k, r).wait_send()
            if k:
                self.along(c, k).wait_send()


def backward_body(
    n_dp, pieces,
    hidden, cot, back_rows, h_rows, u_rows, term_out, gains, head_gains, wq, wk, wv, wo,
    cosine, sine, seg_col, seg_row, a_all, q_raw, k_raw, q_rot, k_rot, v_all, lse, ctx, ffn,
    hidden_out, gains_out, wq_out, wo_out, kv_out, ffn_out,
    dh, du_own, du_all, parts, held, come, dctx, dv, dk, dq_low, dk_low, dv_low, wide,
    wq_part, wo_part, kv_part, kv_held, ffn_own, wq_in, wo_in, kv_in, ffn_in,
    wq_far, wo_far, kv_far, ffn_far, kv_pool, terms, pool_t, pool_r, pool_z,
    own_sem, rs, rr, zs, zr, ks, kr, gxs, gxr, gms, gmr, sms, smr, sfs, sfr, ts, tr, us, ur, vs, vr,
):
    at = Spot(n_dp)
    others = [at.mate, at.side, {"tensor": at.t_side_mate}]
    meet(others + at.line_at[1:] + at.rest_at[1:])
    n_ffn = ffn.shape[0]
    size = hidden.shape[0]
    c_wo, c_wq, c_kv = n_ffn, n_ffn + 1, n_ffn + 2
    factor = HD ** (-0.5)

    def of_ffn(c):
        return lambda dp: ffn.at[c, dp]

    def own_ffn(c):
        return lambda k: ffn_own.at[c, k]

    def of(ref):
        return lambda dp: ref.at[dp]

    def own(ref):
        return lambda k: ref.at[at.line_dp[k]]

    sums = Sums(
        at,
        [of_ffn(c) for c in range(n_ffn)] + [of(wo_part), of(wq_part), of(kv_held)],
        [own_ffn(c) for c in range(n_ffn)] + [own(wo_part), own(wq_part), own(kv_held)],
        [ffn_in.at[c] for c in range(n_ffn)] + [wo_in, wq_in, kv_in],
        [ffn_far.at[c] for c in range(n_ffn)] + [wo_far, wq_far, kv_far],
        rs, rr, zs, zr,
    )
    for c in range(n_ffn):
        sums.start(c)
    keep = [
        pltpu.make_async_copy(ffn.at[c, at.line_dp[k]], ffn_own.at[c, k], own_sem.at[c, k])
        for c in range(n_ffn)
        for k in range(4)
    ]
    for copy in keep:
        copy.start()
    steps = [(c, k) for c in range(n_ffn) for k in sums.turns]

    def pump(count):
        for _ in range(count):
            if steps:
                sums.add(*steps.pop(0))

    def gain(row):
        return gains[row : row + 1, :]

    def column_sum(values):
        return jnp.sum(values, axis=0, keepdims=True)

    width = hidden.shape[1]
    head = q_raw.shape[-1]
    terms[...] = jnp.zeros_like(terms)
    terms[3:4, :] = term_out[...]
    bring = Gather4(at, pieces, du_own, du_all, gxs, gxr, gms, gmr)
    sum_ffn = jnp.zeros((1, width), jnp.float32)
    sum_attn = jnp.zeros((1, width), jnp.float32)
    for p, piece in enumerate(pieces):
        rows = pl.ds(*piece)
        grad_norm, term = norm_back(h_rows[rows], gain(2), back_rows[rows])
        sum_ffn += column_sum(term)
        total = cot[rows].astype(jnp.float32) + grad_norm
        dh[rows] = total
        grad_u, term = norm_back(u_rows[rows], gain(1), total)
        sum_attn += column_sum(term)
        du_own[rows] = grad_u.astype(jnp.bfloat16)
        bring.over_x(p).start()
    terms[1:2, :] = sum_attn
    terms[2:3, :] = sum_ffn
    bring.near_own().start()
    du_all[at.t] = du_own[...]
    for copy in keep:
        copy.wait()

    def back_ctx(t):
        dctx[t] = dot(du_all[t], wo[...]).astype(jnp.bfloat16)

    back_ctx(at.t)
    bring.near_own().wait_recv()
    back_ctx(at.t_mate)
    bring.pass_on()
    back_ctx(at.t_side)
    bring.all_here()
    back_ctx(at.t_side_mate)
    n_tensor = du_all.shape[0]
    dr = wo_part.shape[1]

    def weight_grad(out, left, right):
        total = contract_rows(left[0], right[0])
        for t in range(1, n_tensor):
            total = total + contract_rows(left[t], right[t])
        wide[...] = total
        for i in range(n_dp):
            out[i] = wide[i * dr : (i + 1) * dr].astype(jnp.bfloat16)

    weight_grad(wo_part, du_all, ctx)
    sums.start(c_wo)
    pump(3)

    def attend_back(t):
        scores = contract_cols(q_rot[t], k_rot[...]) * factor
        row = lax.broadcasted_iota(jnp.int32, scores.shape, 0) + t * size
        behind = row - lax.broadcasted_iota(jnp.int32, scores.shape, 1)
        allowed = (seg_col[t] == seg_row[...]) & (behind >= 0) & (behind < WINDOW)
        probs = jnp.where(allowed, jnp.exp(scores - lse[t]), 0.0)
        grad_probs = contract_cols(dctx[t], v_all[...])
        delta = jnp.sum(probs * grad_probs, axis=-1, keepdims=True)
        grad_scores = (probs * (grad_probs - delta) * factor).astype(jnp.bfloat16)
        grad_q = dot(grad_scores, k_rot[...])
        low, term = norm_back(q_raw[t], head_gains[0:1, :], turn(grad_q, cosine[t], -sine[t]))
        dq_low[t] = low.astype(jnp.bfloat16)
        return (
            contract_rows(probs.astype(jnp.bfloat16), dctx[t]),
            contract_rows(grad_scores, q_rot[t]),
            column_sum(term),
        )

    add_v, add_k, sum_q = attend_back(0)
    dv[...] = add_v
    dk[...] = add_k
    for t in range(1, n_tensor):
        add_v, add_k, more = attend_back(t)
        dv[...] += add_v
        dk[...] += add_k
        sum_q += more
    sum_k = jnp.zeros((1, head), jnp.float32)
    for t in range(n_tensor):
        rows = pl.ds(t * size, size)
        low, term = norm_back(k_raw[t], head_gains[1:2, :], turn(dk[rows], cosine[t], -sine[t]))
        dk_low[t] = low.astype(jnp.bfloat16)
        sum_k += column_sum(term)
        dv_low[t] = dv[rows].astype(jnp.bfloat16)
    terms[4:5, :head] = sum_q
    terms[5:6, :head] = sum_k
    pump(2)

    def back_in(t):
        parts[t] = (
            contract_cols(dq_low[t], wq[...])
            + contract_cols(dk_low[t], wk[...])
            + contract_cols(dv_low[t], wv[...])
        ).astype(jnp.bfloat16)

    back = Scatter4(at, pieces, parts, held, come, sms, smr, sfs, sfr)
    back_in(at.t_side_mate)
    back.near(1).start()
    back_in(at.t_side)
    back.send_side()
    back_in(at.t_mate)
    back.near(0).start()
    back_in(at.t)
    weight_grad(kv_part.at[0], a_all, dk_low)
    weight_grad(kv_part.at[1], a_all, dv_low)
    mate_kv = send_to(at.mate, kv_part.at[1 - at.core], kv_held, ks.at[0], kr.at[0])
    mate_kv.start()
    weight_grad(wq_part, a_all, dq_low)
    sums.start(c_wq)
    mate_kv.wait()

    def pair_up(dp, carry):
        def add(rows):
            kv_held[dp, rows] = add_up(kv_part[at.core, dp, rows], kv_held[dp, rows]).astype(
                jnp.bfloat16
            )

        by_rows(kv_held.shape[1], add)
        return carry

    lax.fori_loop(0, n_dp, pair_up, 0)
    sums.start(c_kv)
    pump(1)
    back.near(0).wait_recv()
    sum_in = jnp.zeros((1, width), jnp.float32)
    for p, piece in enumerate(pieces):
        rows = pl.ds(*piece)
        back.far(p).wait_recv()
        total = add_up(parts[at.t, rows], held[0, rows]) + come[rows].astype(jnp.float32)
        grad_norm, term = norm_back(hidden[rows].astype(jnp.float32), gain(0), total)
        hidden_out[rows] = dh[rows] + grad_norm
        sum_in += column_sum(term)
    terms[0:1, :] = sum_in

    pool_t[at.t] = terms[...].astype(jnp.bfloat16)
    over_t = [
        send_to(where, pool_t.at[at.t], pool_t.at[at.t], ts.at[j], tr.at[j])
        for j, where in enumerate(others)
    ]
    for copy in over_t:
        copy.start()
    pump(2)
    for copy in over_t:
        copy.wait()
    total = pool_t[0].astype(jnp.float32)
    for t in range(1, n_tensor):
        total = total + pool_t[t].astype(jnp.float32)
    pool_r[at.rest] = total.astype(jnp.bfloat16)
    over_r = [
        send_to(at.rest_at[r], pool_r.at[at.rest], pool_r.at[at.rest], us.at[r], ur.at[r])
        for r in range(1, at.n_rest)
    ]
    for copy in over_r:
        copy.start()
    pump(len(steps))
    for copy in over_r:
        copy.wait()
    total = pool_r[0].astype(jnp.float32)
    for r in range(1, at.n_rest):
        total = total + pool_r[r].astype(jnp.float32)
    pool_z[at.line] = total.astype(jnp.bfloat16)
    over_z = [
        send_to(at.line_at[k], pool_z.at[at.line], pool_z.at[at.line], vs.at[k], vr.at[k])
        for k in (1, 2, 3)
    ]
    for copy in over_z:
        copy.start()
    for c in (c_wo, c_wq, c_kv):
        for k in sums.turns:
            sums.add(c, k)
    half_width = ffn.shape[-1]
    for c in range(n_ffn):
        sums.arrive(c)

        def finish(first, own=ffn_in.at[c, 0, 0], far=ffn_far.at[c], target=ffn_out.at[c]):
            def put(rows):
                same = add_up(own[rows], far[1, rows])
                cross = add_up(far[0, rows], far[2, rows])
                low, high = (same, cross) if first else (cross, same)
                target[rows, :half_width] = low
                target[rows, half_width:] = high[:, : target.shape[-1] - half_width]

            by_rows(own.shape[0], put)

        @pl.when(at.half == 0)
        def _(finish=finish):
            finish(True)

        @pl.when(at.half == 1)
        def _(finish=finish):
            finish(False)

    for copy in over_z:
        copy.wait()
    gains_out[...] = add_up(pool_z[0], pool_z[1]) + add_up(pool_z[2], pool_z[3])
    sums.arrive(c_wo)
    wo_out[...] = add_up(wo_in[0, 0], wo_far[0]) + add_up(wo_far[1], wo_far[2])
    sums.arrive(c_wq)
    wq_out[...] = add_up(wq_in[0, 0], wq_far[0]) + add_up(wq_far[1], wq_far[2])
    sums.arrive(c_kv)
    kv_pool[0] = (add_up(kv_in[0, 0], kv_far[0]) + add_up(kv_far[1], kv_far[2])).astype(jnp.bfloat16)
    kv_side = send_to(at.side, kv_pool.at[0], kv_pool.at[1], ks.at[1], kr.at[1])
    kv_side.start()
    kv_side.wait()
    kv_out[at.core] = add_up(kv_pool[0], kv_pool[1])
    give = send_to(at.mate, kv_out.at[at.core], kv_out.at[at.core], ks.at[2], kr.at[2])
    give.start()
    give.wait()
    for c in range(n_ffn + 3):
        sums.finish(c)
    bring.finish()
    back.finish()


def backward(
    n_dp, hidden, cot, back_rows, h_rows, u_rows, term_out, gains, head_gains, wq, wk, wv, wo,
    cosine, sine, seg_ids, a_all, q_raw, k_raw, q_rot, k_rot, v_all, lse, ctx, ffn, columns, ident,
):
    size, width = hidden.shape
    n_tensor = seg_ids.shape[0] // size
    n_ffn, _, dr, half_width = ffn.shape
    n_rest = n_dp // 4
    head = wq.shape[1]
    pieces = row_pieces(size, 10)
    count = len(pieces)
    vmem = pl.BlockSpec(memory_space=pltpu.VMEM)
    blocked = (n_tensor, size)

    def out(*dims):
        return jax.ShapeDtypeStruct(dims, jnp.float32)

    def low(*dims):
        return pltpu.VMEM(dims, jnp.bfloat16)

    def full(*dims):
        return pltpu.VMEM(dims, jnp.float32)

    def dma(*dims):
        return pltpu.SemaphoreType.DMA(dims)

    total = n_ffn + 3
    rows16 = -(-6 // SUBLANES) * SUBLANES
    return pl.pallas_call(
        functools.partial(backward_body, n_dp, pieces),
        out_shape=[
            out(size, width), out(rows16, width), out(dr, head), out(dr, head), out(2, dr, head),
            out(n_ffn, dr, columns),
        ],
        in_specs=[vmem] * 24 + [pl.BlockSpec(memory_space=pl.ANY)],
        out_specs=[vmem] * 6,
        scratch_shapes=[
            full(size, width), low(size, width), low(*blocked, width), low(*blocked, width),
            low(2, size, width), low(size, width), low(*blocked, head),
            full(n_tensor * size, head), full(n_tensor * size, head),
            low(*blocked, head), low(*blocked, head), low(*blocked, head), full(width, head),
            low(n_dp, dr, head), low(n_dp, dr, head), low(2, n_dp, dr, head), low(n_dp, dr, head),
            low(n_ffn, 4, dr, half_width),
            low(4, n_rest - 1, dr, head), low(4, n_rest - 1, dr, head), low(4, n_rest - 1, dr, head),
            low(n_ffn, 4, n_rest - 1, dr, half_width),
            low(3, dr, head), low(3, dr, head), low(3, dr, head), low(n_ffn, 3, dr, half_width),
            low(2, dr, head), full(rows16, width), low(n_tensor, rows16, width),
            low(n_rest, rows16, width), low(4, rows16, width),
            dma(n_ffn, 4), dma(total, 4, n_rest), dma(total, 4, n_rest), dma(total, 4), dma(total, 4),
            dma(3), dma(3), dma(count), dma(count), dma(count + 1), dma(count + 1),
            dma(2), dma(2), dma(count), dma(count),
            dma(3), dma(3), dma(n_rest), dma(n_rest), dma(4), dma(4),
        ],
        compiler_params=pltpu.CompilerParams(
            collective_id=ident, has_side_effects=True, vmem_limit_bytes=60 * MIB
        ),
        name="backward",
    )(
        hidden, cot, back_rows, h_rows, u_rows, term_out, gains, head_gains, wq, wk, wv, wo,
        cosine.reshape(*blocked, -1), sine.reshape(*blocked, -1),
        seg_ids.reshape(*blocked, 1), seg_ids.reshape(1, -1),
        a_all, q_raw, k_raw, q_rot, k_rot, v_all, lse, ctx, ffn,
    )


class Spread:
    def __init__(self, at, source, place, own_sem, zs, zr, rs, rr):
        self.at, self.source, self.place = at, source, place
        self.own_sem, self.zs, self.zr, self.rs, self.rr = own_sem, zs, zr, rs, rr

    def along(self, c, k):
        at = self.at
        return send_to(
            at.line_at[k], self.source(c, k), self.place(c, at.dp), self.zs.at[c, k], self.zr.at[c, k]
        )

    def across(self, c, k, r):
        at = self.at
        spot = self.place(c, at.line_dp[k])
        source = self.source(c, 0) if k == 0 else spot
        return send_to(at.rest_at[r], source, spot, self.rs.at[c, k, r], self.rr.at[c, k, r])

    def own(self, c):
        return pltpu.make_async_copy(
            self.source(c, 0), self.place(c, self.at.dp), self.own_sem.at[c]
        )

    def launch(self, c):
        for k in (2, 3, 1):
            self.along(c, k).start()
        for r in range(1, self.at.n_rest):
            self.across(c, 0, r).start()
        self.own(c).start()

    def forward(self, c):
        for k in (2, 3, 1):
            self.along(c, k).wait_recv()
            for r in range(1, self.at.n_rest):
                self.across(c, k, r).start()

    def arrived(self, c):
        self.own(c).wait()
        for k in range(4):
            for r in range(1, self.at.n_rest):
                self.across(c, k, r).wait_recv()

    def finish(self, c):
        for k in range(4):
            for r in range(1, self.at.n_rest):
                self.across(c, k, r).wait_send()
            if k:
                self.along(c, k).wait_send()


class Scatter8:
    def __init__(self, at, pieces, parts, held, come, last, ms, mr, fs, fr, ls, lr):
        self.at, self.pieces, self.parts, self.held = at, pieces, parts, held
        self.come, self.last = come, last
        self.ms, self.mr, self.fs, self.fr, self.ls, self.lr = ms, mr, fs, fr, ls, lr
        half, other = at.half, 1 - at.half
        self.z = (half, half, other, other)
        self.x = (at.x, 1 - at.x, at.x, 1 - at.x)
        self.mine_t = (at.t, at.t_side, at.t, at.t_side)
        self.mate_t = (at.t_mate, at.t_side_mate, at.t_mate, at.t_side_mate)

    def near(self, k):
        return send_to(
            self.at.mate, self.parts.at[self.z[k], self.mate_t[k]], self.held.at[k],
            self.ms.at[k], self.mr.at[k],
        )

    def first(self, j, p):
        rows = pl.ds(*self.pieces[p])
        where, blocks = (self.at.side, (1, 3)) if p % 2 == 0 else (self.at.pair, (2, 3))
        return send_to(
            where, self.held.at[blocks[j], rows], self.come.at[j, rows],
            self.fs.at[j, p], self.fr.at[j, p],
        )

    def second(self, p):
        rows = pl.ds(*self.pieces[p])
        where, block = (self.at.pair, 2) if p % 2 == 0 else (self.at.side, 1)
        return send_to(
            where, self.held.at[block, rows], self.last.at[rows], self.ls.at[p], self.lr.at[p]
        )

    def combine(self, k):
        self.near(k).wait_recv()
        for p, piece in enumerate(self.pieces):
            rows = pl.ds(*piece)
            self.held[k, rows] = add_up(
                self.parts[self.z[k], self.mine_t[k], rows], self.held[k, rows]
            ).astype(jnp.bfloat16)
            if k == 3:
                self.first(1, p).start()
            elif k == 1 and p % 2 == 0 or k == 2 and p % 2 == 1:
                self.first(0, p).start()

    def relay(self):
        for p, piece in enumerate(self.pieces):
            rows = pl.ds(*piece)
            keep = 2 if p % 2 == 0 else 1
            self.first(1, p).wait_recv()
            self.held[keep, rows] = add_up(self.held[keep, rows], self.come[1, rows]).astype(
                jnp.bfloat16
            )
            self.second(p).start()

    def result(self, p):
        rows = pl.ds(*self.pieces[p])
        self.first(0, p).wait_recv()
        self.second(p).wait_recv()
        return add_up(self.held[0, rows], self.come[0, rows]) + self.last[rows].astype(jnp.float32)

    def finish(self):
        for k in range(4):
            self.near(k).wait_send()
        for p in range(len(self.pieces)):
            self.first(0, p).wait_send()
            self.first(1, p).wait_send()
            self.second(p).wait_send()


GAINS, KV, WQ, WO, GATE, UP, DOWN = range(7)


def layer_body(n_dp, pieces, names, *refs):
    s = dict(zip(names, refs, strict=True))
    hidden, cot, ffn = s["hidden"], s["cot"], s["ffn"]
    cosine, sine, seg_col, seg_row = s["cosine"], s["sine"], s["seg_col"], s["seg_row"]
    at = Spot(n_dp)
    others = [at.mate, at.side, {"tensor": at.t_side_mate}]
    meet(others + at.line_at[1:] + at.rest_at[1:])
    halves = (at.half, 1 - at.half, at.half, 1 - at.half)
    size, width = hidden.shape
    dr, wide = ffn.shape[2:]
    n_tensor, _, head = s["q_raw"].shape
    factor = HD ** (-0.5)
    a_all, q_raw, k_raw, q_rot, k_rot = (s[n] for n in ("a_all", "q_raw", "k_raw", "q_rot", "k_rot"))
    v_all, lse, ctx, u_rows, h_rows = (s[n] for n in ("v_all", "lse", "ctx", "u_rows", "h_rows"))
    kv_all, wq, wo, ffn_all = s["kv_all"], s["wq_all"], s["wo_all"], s["ffn_all"]

    def rows_of(dp):
        return pl.ds(pl.multiple_of(dp * dr, SUBLANES), dr)

    def source(c, k):
        if c == KV:
            return s["kv"].at[at.core]
        if c < GATE:
            return s[{GAINS: "gains", WQ: "wq", WO: "wo"}[c]]
        return ffn.at[halves[k], c - GATE]

    def place(c, dp):
        if c == GAINS:
            return s["gains_all"].at[dp]
        if c == KV:
            return kv_all.at[at.core, rows_of(dp)]
        if c < GATE:
            return (wq if c == WQ else wo).at[rows_of(dp)]
        return ffn_all.at[c - GATE, rows_of(dp)]

    load = Spread(at, source, place, s["own_sem"], s["lzs"], s["lzr"], s["lrs"], s["lrr"])
    for c in (GAINS, KV, WQ, WO, GATE, UP):
        load.launch(c)

    load.forward(GAINS)
    load.arrived(GAINS)
    gains, head_gains = s["wide_gains"], s["head_gains"]
    g_width, g_head = width // n_dp, head // n_dp
    for i in range(n_dp):
        block = s["gains_all"][i].astype(jnp.float32)
        gains[:, i * g_width : (i + 1) * g_width] = block[:, :g_width]
        head_gains[:, i * g_head : (i + 1) * g_head] = block[:, :g_head]

    def gain(row):
        return gains[row : row + 1, :]

    q_gain, k_gain = head_gains[4:5, :], head_gains[5:6, :]

    def column_sum(values):
        return jnp.sum(values, axis=0, keepdims=True)

    bring = Gather4(at, pieces, s["a_own"], a_all, s["g1xs"], s["g1xr"], s["g1ms"], s["g1mr"])
    for piece in pieces:
        rows = pl.ds(*piece)
        s["a_own"][rows] = apply_norm(hidden[rows].astype(jnp.float32), gain(0)).astype(jnp.bfloat16)
    bring.start()
    a_all[at.t] = s["a_own"][...]
    bring.pass_on()
    load.forward(KV)
    load.forward(WQ)
    bring.near_own().wait_recv()
    bring.all_here()
    load.arrived(KV)
    share = send_to(at.mate, kv_all.at[at.core], kv_all.at[at.core], s["ks"].at[3], s["kr"].at[3])
    share.start()
    load.forward(WO)
    load.arrived(WQ)

    def project_q(t):
        q = dot(a_all[t], wq[...])
        q_raw[t] = q
        q_rot[t] = turn(apply_norm(q, q_gain), cosine[t], sine[t]).astype(jnp.bfloat16)

    def project_kv(t):
        rows = pl.ds(t * size, size)
        k = dot(a_all[t], kv_all[0])
        k_raw[t] = k
        k_rot[rows] = turn(apply_norm(k, k_gain), cosine[t], sine[t]).astype(jnp.bfloat16)
        v_all[rows] = dot(a_all[t], kv_all[1]).astype(jnp.bfloat16)

    for t in range(n_tensor):
        project_q(t)
    share.wait()
    for t in range(n_tensor):
        project_kv(t)
    load.arrived(WO)

    def allowed_pairs(t, shape):
        row = lax.broadcasted_iota(jnp.int32, shape, 0) + t * size
        behind = row - lax.broadcasted_iota(jnp.int32, shape, 1)
        return (seg_col[t] == seg_row[...]) & (behind >= 0) & (behind < WINDOW)

    parts8 = s["parts8"]
    parts4 = parts8.at[0]

    def attend(t):
        scores = contract_cols(q_rot[t], k_rot[...]) * factor
        weights = jnp.where(allowed_pairs(t, scores.shape), jnp.exp(scores), 0.0)
        total = jnp.sum(weights, axis=-1, keepdims=True)
        lse[t] = jnp.log(total)
        mixed = dot((weights / total).astype(jnp.bfloat16), v_all[...]).astype(jnp.bfloat16)
        ctx[t] = mixed
        parts4[t] = contract_cols(mixed, wo[...]).astype(jnp.bfloat16)

    back = Scatter4(
        at, pieces, parts4, s["held4"], s["come4"], s["s1ms"], s["s1mr"], s["s1fs"], s["s1fr"]
    )
    attend(at.t_side_mate)
    back.near(1).start()
    attend(at.t_side)
    back.send_side()
    attend(at.t_mate)
    back.near(0).start()
    attend(at.t)
    load.forward(GATE)
    back.result(u_rows)
    spread = Gather8(
        at, pieces, s["c_own"], s["c_all"],
        *(s[n] for n in ("x1s", "x1r", "z1s", "z1r", "d1s", "d1r", "m1s", "m1r")),
    )
    for p, piece in enumerate(pieces):
        rows = pl.ds(*piece)
        total = hidden[rows].astype(jnp.float32) + apply_norm(u_rows[rows], gain(1))
        h_rows[rows] = total
        s["c_own"][rows] = apply_norm(total, gain(2)).astype(jnp.bfloat16)
        spread.start(p)
    load.launch(DOWN)
    c_all = s["c_all"]
    c_all[at.half, at.t] = s["c_own"][...]
    load.forward(UP)
    spread.pass_on()
    spread.pass_last()
    for k in range(4):
        spread.here(k)
    back.finish()
    bring.finish()
    load.arrived(GATE)
    load.arrived(UP)
    for c in (GAINS, KV, WQ, WO):
        load.finish(c)
    spread.finish()

    fm, fa, fb = s["fm"], s["fa"], s["fb"]
    double = 2 * size
    cuts = [(0, 4 * LANES), (4 * LANES, wide)] if wide > 4 * LANES else [(0, wide)]

    def hidden_units(j, carry):
        z = j // 2
        x = j - 2 * z
        rows = pl.ds(pl.multiple_of(j * double, SUBLANES), double)
        block = c_all[z, pl.ds(2 * x, 2)].reshape(double, width)
        for low, high in cuts:
            g = dot(block, ffn_all[0, :, low:high])
            r = dot(block, ffn_all[1, :, low:high])
            square = g * g
            bend = jnp.tanh(GELU_SCALE * g * (1.0 + GELU_CUBE * square))
            rise = 0.5 * (1.0 + bend)
            value = g * rise
            slope = rise + 0.5 * g * (1.0 - bend * bend) * (
                GELU_SCALE * (1.0 + 3.0 * GELU_CUBE * square)
            )
            fm[rows, low:high] = (value * r).astype(jnp.bfloat16)
            fa[rows, low:high] = (r * slope).astype(jnp.bfloat16)
            fb[rows, low:high] = value.astype(jnp.bfloat16)
        return carry

    lax.fori_loop(0, 4, hidden_units, 0)
    load.forward(DOWN)
    load.arrived(DOWN)

    held8, come8, last8 = s["held8"], s["come8"], s["last8"]
    order = (3, 1, 2, 0)

    def block_rows(scatter, k):
        first = (2 * scatter.z[k] + scatter.x[k]) * double
        return pl.ds(pl.multiple_of(first, SUBLANES), double)

    def sum8(scatter, part):
        before = None
        for k in order:
            value = part(block_rows(scatter, k)).astype(jnp.bfloat16)
            parts8[scatter.z[k], pl.ds(2 * scatter.x[k], 2)] = value.reshape(2, size, width)
            scatter.near(k).start()
            if before is not None:
                scatter.combine(before)
            before = k
        scatter.combine(before)

    first = Scatter8(
        at, pieces, parts8, held8, come8, last8,
        *(s[n] for n in ("e1ms", "e1mr", "e1fs", "e1fr", "e1ls", "e1lr")),
    )
    sum8(first, lambda rows: contract_cols(fm[rows], ffn_all[2]))
    first.relay()
    df_own, df_all = s["df_own"], s["df_all"]
    spread = Gather8(
        at, pieces, df_own, df_all,
        *(s[n] for n in ("x2s", "x2r", "z2s", "z2r", "d2s", "d2r", "m2s", "m2r")),
    )
    terms = s["terms"]
    terms[...] = jnp.zeros_like(terms)
    sum_out = jnp.zeros((1, width), jnp.float32)
    for p, piece in enumerate(pieces):
        rows = pl.ds(*piece)
        down = first.result(p)
        s["out_rows"][rows] = (h_rows[rows] + apply_norm(down, gain(3))).astype(jnp.bfloat16)
        grad, term = norm_back(down, gain(3), cot[rows].astype(jnp.float32))
        sum_out += column_sum(term)
        df_own[rows] = grad.astype(jnp.bfloat16)
        spread.start(p)
    terms[3:4, :] = sum_out
    df_all[at.half, at.t] = df_own[...]
    first.finish()
    load.finish(GATE)
    load.finish(UP)
    load.finish(DOWN)

    def units_back(k):
        rows = block_rows(first, k)
        block = df_all[first.z[k], pl.ds(2 * first.x[k], 2)].reshape(double, width)
        for low, high in cuts:
            dm = dot(block, ffn_all[2, :, low:high])
            fa[rows, low:high] = (dm * fa[rows, low:high].astype(jnp.float32)).astype(jnp.bfloat16)
            fb[rows, low:high] = (dm * fb[rows, low:high].astype(jnp.float32)).astype(jnp.bfloat16)

    spread.here(0)
    units_back(0)
    spread.pass_on()
    spread.here(1)
    units_back(1)
    spread.here(2)
    units_back(2)
    spread.pass_last()
    spread.here(3)
    units_back(3)

    dwd = s["dwd"]
    tile = width // 3 if width % (3 * LANES) == 0 else width

    def ffn_grad(target, left, right):
        def one(i, carry):
            cols = pl.ds(pl.multiple_of(i * tile, LANES), tile)
            block = left[:, :, :, cols].reshape(4 * double, tile)
            value = contract_rows(block, right[...]).astype(jnp.bfloat16)
            target[pl.ds(pl.multiple_of(i * tile, SUBLANES), tile)] = value
            return carry

        lax.fori_loop(0, width // tile, one, 0)

    def flat(ref):
        return lambda dp: ref.at[rows_of(dp)]

    def own_flat(ref):
        return lambda k: ref.at[rows_of(at.line_dp[k])]

    dwg, dwu = fm, ffn_all.at[2]
    wo_part, wq_part, kv_part, kv_held = (s[n] for n in ("wo_part", "wq_part", "kv_part", "kv_held"))
    ffn_in, ffn_far = s["ffn_in"], s["ffn_far"]
    moved = (dwd, dwg, dwu, wo_part, wq_part, kv_held)
    n_ffn = 3
    c_wo, c_wq, c_kv = 3, 4, 5
    sums = Sums(
        at, [flat(ref) for ref in moved], [own_flat(ref) for ref in moved],
        [ffn_in.at[c] for c in range(n_ffn)] + [s["wo_in"], s["wq_in"], s["kv_in"]],
        [ffn_far.at[c] for c in range(n_ffn)] + [s["wo_far"], s["wq_far"], s["kv_far"]],
        s["rs"], s["rr"], s["zs"], s["zr"],
    )
    steps = [(c, k) for c in range(n_ffn) for k in sums.turns]

    def pump(count):
        for _ in range(count):
            if steps:
                sums.add(*steps.pop(0))

    ffn_grad(dwd, df_all, fm)
    sums.start(0)
    second = Scatter8(
        at, pieces, parts8, held8, come8, last8,
        *(s[n] for n in ("e2ms", "e2mr", "e2fs", "e2fr", "e2ls", "e2lr")),
    )
    sum8(
        second,
        lambda rows: contract_cols(fa[rows], ffn_all[0]) + contract_cols(fb[rows], ffn_all[1]),
    )
    ffn_grad(dwg, c_all, fa)
    sums.start(1)
    second.relay()
    ffn_grad(dwu, c_all, fb)
    sums.start(2)
    spread.finish()

    dh, du_own, du_all = s["dh"], s["du_own"], s["du_all"]
    bring = Gather4(at, pieces, du_own, du_all, s["g2xs"], s["g2xr"], s["g2ms"], s["g2mr"])
    sum_ffn = jnp.zeros((1, width), jnp.float32)
    sum_attn = jnp.zeros((1, width), jnp.float32)
    for p, piece in enumerate(pieces):
        rows = pl.ds(*piece)
        grad_norm, term = norm_back(h_rows[rows], gain(2), second.result(p))
        sum_ffn += column_sum(term)
        total = cot[rows].astype(jnp.float32) + grad_norm
        dh[rows] = total
        grad_u, term = norm_back(u_rows[rows], gain(1), total)
        sum_attn += column_sum(term)
        du_own[rows] = grad_u.astype(jnp.bfloat16)
        bring.over_x(p).start()
    terms[1:2, :] = sum_attn
    terms[2:3, :] = sum_ffn
    bring.near_own().start()
    du_all[at.t] = du_own[...]
    second.finish()
    dctx = s["dctx"]

    def back_ctx(t):
        dctx[t] = dot(du_all[t], wo[...]).astype(jnp.bfloat16)

    back_ctx(at.t)
    bring.near_own().wait_recv()
    back_ctx(at.t_mate)
    bring.pass_on()
    pump(2)
    back_ctx(at.t_side)
    bring.all_here()
    back_ctx(at.t_side_mate)

    def weight_grad(target, left, right):
        value = contract_rows(
            left[...].reshape(n_tensor * size, width), right[...].reshape(n_tensor * size, head)
        )
        target[...] = value.astype(jnp.bfloat16)

    weight_grad(wo_part, du_all, ctx)
    sums.start(c_wo)
    pump(2)
    dq_low, dk_low, dv_low, dv, dk = (s[n] for n in ("dq_low", "dk_low", "dv_low", "dv", "dk"))

    def attend_back(t):
        scores = contract_cols(q_rot[t], k_rot[...]) * factor
        probs = jnp.where(allowed_pairs(t, scores.shape), jnp.exp(scores - lse[t]), 0.0)
        grad_probs = contract_cols(dctx[t], v_all[...])
        delta = jnp.sum(probs * grad_probs, axis=-1, keepdims=True)
        grad_scores = (probs * (grad_probs - delta) * factor).astype(jnp.bfloat16)
        grad_q = dot(grad_scores, k_rot[...])
        low, term = norm_back(q_raw[t], q_gain, turn(grad_q, cosine[t], -sine[t]))
        dq_low[t] = low.astype(jnp.bfloat16)
        return (
            contract_rows(probs.astype(jnp.bfloat16), dctx[t]),
            contract_rows(grad_scores, q_rot[t]),
            column_sum(term),
        )

    add_v, add_k, sum_q = attend_back(0)
    dv[...] = add_v
    dk[...] = add_k
    for t in range(1, n_tensor):
        add_v, add_k, more = attend_back(t)
        dv[...] += add_v
        dk[...] += add_k
        sum_q += more
    sum_k = jnp.zeros((1, head), jnp.float32)
    for t in range(n_tensor):
        rows = pl.ds(t * size, size)
        low, term = norm_back(k_raw[t], k_gain, turn(dk[rows], cosine[t], -sine[t]))
        dk_low[t] = low.astype(jnp.bfloat16)
        sum_k += column_sum(term)
        dv_low[t] = dv[rows].astype(jnp.bfloat16)
    terms[4:5, :head] = sum_q
    terms[5:6, :head] = sum_k
    pump(2)

    def back_in(t):
        parts4[t] = (
            contract_cols(dq_low[t], wq[...])
            + contract_cols(dk_low[t], kv_all[0])
            + contract_cols(dv_low[t], kv_all[1])
        ).astype(jnp.bfloat16)

    held4, come4 = s["held4"], s["come4"]
    back = Scatter4(at, pieces, parts4, held4, come4, s["s2ms"], s["s2mr"], s["s2fs"], s["s2fr"])
    back_in(at.t_side_mate)
    back.near(1).start()
    back_in(at.t_side)
    back.send_side()
    back_in(at.t_mate)
    back.near(0).start()
    back_in(at.t)
    weight_grad(kv_part.at[0], a_all, dk_low)
    weight_grad(kv_part.at[1], a_all, dv_low)
    ks, kr = s["ks"], s["kr"]
    mate_kv = send_to(at.mate, kv_part.at[1 - at.core], kv_held, ks.at[0], kr.at[0])
    mate_kv.start()
    weight_grad(wq_part, a_all, dq_low)
    sums.start(c_wq)
    mate_kv.wait()

    def pair_up(rows):
        kv_held[rows] = add_up(kv_part[at.core, rows], kv_held[rows]).astype(jnp.bfloat16)

    by_rows(kv_held.shape[0], pair_up)
    sums.start(c_kv)
    pump(1)
    back.near(0).wait_recv()
    sum_in = jnp.zeros((1, width), jnp.float32)
    for p, piece in enumerate(pieces):
        rows = pl.ds(*piece)
        back.far(p).wait_recv()
        total = add_up(parts4[at.t, rows], held4[0, rows]) + come4[rows].astype(jnp.float32)
        grad_norm, term = norm_back(hidden[rows].astype(jnp.float32), gain(0), total)
        s["hidden_out"][rows] = dh[rows] + grad_norm
        sum_in += column_sum(term)
    terms[0:1, :] = sum_in

    pool_t, pool_r, pool_z = s["pool_t"], s["pool_r"], s["pool_z"]
    pool_t[at.t] = terms[...].astype(jnp.bfloat16)
    over_t = [
        send_to(where, pool_t.at[at.t], pool_t.at[at.t], s["ts"].at[j], s["tr"].at[j])
        for j, where in enumerate(others)
    ]
    for copy in over_t:
        copy.start()
    pump(1)
    for copy in over_t:
        copy.wait()
    total = pool_t[0].astype(jnp.float32)
    for t in range(1, n_tensor):
        total = total + pool_t[t].astype(jnp.float32)
    pool_r[at.rest] = total.astype(jnp.bfloat16)
    over_r = [
        send_to(at.rest_at[r], pool_r.at[at.rest], pool_r.at[at.rest], s["us"].at[r], s["ur"].at[r])
        for r in range(1, at.n_rest)
    ]
    for copy in over_r:
        copy.start()
    pump(len(steps))
    for copy in over_r:
        copy.wait()
    total = pool_r[0].astype(jnp.float32)
    for r in range(1, at.n_rest):
        total = total + pool_r[r].astype(jnp.float32)
    pool_z[at.line] = total.astype(jnp.bfloat16)
    over_z = [
        send_to(at.line_at[k], pool_z.at[at.line], pool_z.at[at.line], s["vs"].at[k], s["vr"].at[k])
        for k in (1, 2, 3)
    ]
    for copy in over_z:
        copy.start()
    for c in (c_wo, c_wq, c_kv):
        for k in sums.turns:
            sums.add(c, k)
    for c in range(n_ffn):
        sums.arrive(c)

        def put_all(low_first, own=ffn_in.at[c, 0, 0], far=ffn_far.at[c], target=s["ffn_out"].at[c]):
            def put(rows):
                same = add_up(own[rows], far[1, rows])
                cross = add_up(far[0, rows], far[2, rows])
                low, high = (same, cross) if low_first else (cross, same)
                target[rows, :wide] = low
                target[rows, wide:] = high[:, : target.shape[-1] - wide]

            by_rows(own.shape[0], put)

        @pl.when(at.half == 0)
        def _(put_all=put_all):
            put_all(True)

        @pl.when(at.half == 1)
        def _(put_all=put_all):
            put_all(False)

    for copy in over_z:
        copy.wait()
    s["gains_out"][...] = add_up(pool_z[0], pool_z[1]) + add_up(pool_z[2], pool_z[3])

    def whole(c):
        sums.arrive(c)
        far = sums.distant[c]
        return add_up(sums.landed[c][0, 0], far[0]) + add_up(far[1], far[2])

    s["wo_out"][...] = whole(c_wo)
    s["wq_out"][...] = whole(c_wq)
    kv_pool, kv_out = s["kv_pool"], s["kv_out"]
    kv_pool[0] = whole(c_kv).astype(jnp.bfloat16)
    kv_side = send_to(at.side, kv_pool.at[0], kv_pool.at[1], ks.at[1], kr.at[1])
    kv_side.start()
    kv_side.wait()
    kv_out[at.core] = add_up(kv_pool[0], kv_pool[1])
    give = send_to(at.mate, kv_out.at[at.core], kv_out.at[at.core], ks.at[2], kr.at[2])
    give.start()
    give.wait()
    for c in range(n_ffn + 3):
        sums.finish(c)
    bring.finish()
    back.finish()


def layer(n_dp, hidden, cot, gain_rows, wq, wo, kv, cosine, sine, seg_ids, ffn, columns, ident):
    size, width = hidden.shape
    n_tensor = seg_ids.shape[0] // size
    dr, wide = ffn.shape[2:]
    n_rest = n_dp // 4
    head = wq.shape[1]
    pieces = row_pieces(size, 10)
    count = len(pieces)
    tokens = n_tensor * size
    blocked = (n_tensor, size)
    gain_block = gain_rows.shape

    def out(*dims, kind=jnp.float32):
        return jax.ShapeDtypeStruct(dims, kind)

    def low(*dims):
        return pltpu.VMEM(dims, jnp.bfloat16)

    def full(*dims):
        return pltpu.VMEM(dims, jnp.float32)

    def dma(*dims):
        return pltpu.SemaphoreType.DMA(dims)

    inputs = dict(
        hidden=hidden, cot=cot, gains=gain_rows, wq=wq, wo=wo, kv=kv,
        cosine=cosine.reshape(*blocked, -1), sine=sine.reshape(*blocked, -1),
        seg_col=seg_ids.reshape(*blocked, 1), seg_row=seg_ids.reshape(1, -1), ffn=ffn,
    )
    outputs = dict(
        out_rows=out(size, width, kind=jnp.bfloat16), hidden_out=out(size, width),
        gains_out=out(SUBLANES, width), wq_out=out(dr, head), wo_out=out(dr, head),
        kv_out=out(2, dr, head), ffn_out=out(3, dr, columns),
    )
    scratch = dict(
        gains_all=low(n_dp, *gain_block), kv_all=low(2, width, head), wq_all=low(width, head),
        wo_all=low(width, head), ffn_all=low(3, width, wide),
        wide_gains=full(gain_block[0], width), head_gains=full(gain_block[0], head),
        a_own=low(size, width), a_all=low(*blocked, width), q_raw=full(*blocked, head),
        k_raw=full(*blocked, head), q_rot=low(*blocked, head), k_rot=low(tokens, head),
        v_all=low(tokens, head), lse=full(*blocked, 1), ctx=low(*blocked, head),
        u_rows=full(size, width), h_rows=full(size, width),
        held4=low(2, size, width), come4=low(size, width),
        c_own=low(size, width), c_all=low(2, *blocked, width),
        fm=low(2 * tokens, wide), fa=low(2 * tokens, wide), fb=low(2 * tokens, wide),
        parts8=low(2, *blocked, width), held8=low(4, size, width), come8=low(2, size, width),
        last8=low(size, width), df_own=low(size, width), df_all=low(2, *blocked, width),
        dwd=low(width, wide), ffn_in=low(3, 4, n_rest - 1, dr, wide), ffn_far=low(3, 3, dr, wide),
        dh=full(size, width), du_own=low(size, width), du_all=low(*blocked, width),
        dctx=low(*blocked, head), dv=full(tokens, head), dk=full(tokens, head),
        dq_low=low(*blocked, head), dk_low=low(*blocked, head), dv_low=low(*blocked, head),
        wq_part=low(width, head), wo_part=low(width, head), kv_part=low(2, width, head),
        kv_held=low(width, head), wq_in=low(4, n_rest - 1, dr, head),
        wo_in=low(4, n_rest - 1, dr, head), kv_in=low(4, n_rest - 1, dr, head),
        wq_far=low(3, dr, head), wo_far=low(3, dr, head), kv_far=low(3, dr, head),
        kv_pool=low(2, dr, head), terms=full(SUBLANES, width), pool_t=low(n_tensor, SUBLANES, width),
        pool_r=low(n_rest, SUBLANES, width), pool_z=low(4, SUBLANES, width),
        own_sem=dma(7), lzs=dma(7, 4), lzr=dma(7, 4), lrs=dma(7, 4, n_rest), lrr=dma(7, 4, n_rest),
        rs=dma(6, 4, n_rest), rr=dma(6, 4, n_rest), zs=dma(6, 4), zr=dma(6, 4),
        ks=dma(4), kr=dma(4), ts=dma(3), tr=dma(3), us=dma(n_rest), ur=dma(n_rest), vs=dma(4), vr=dma(4),
    )
    for i in "12":
        for n in ("xs", "xr"):
            scratch[f"g{i}{n}"] = dma(count)
        for n in ("ms", "mr"):
            scratch[f"g{i}{n}"] = dma(count + 1)
            scratch[f"s{i}{n}"] = dma(2)
            scratch[f"e{i}{n}"] = dma(4)
            scratch[f"m{i}{n[1]}"] = dma(4, count)
        for n in ("fs", "fr"):
            scratch[f"s{i}{n}"] = dma(count)
            scratch[f"e{i}{n}"] = dma(2, count)
            scratch[f"e{i}l{n[1]}"] = dma(count)
            for a in "xzd":
                scratch[f"{a}{i}{n[1]}"] = dma(count)
    vmem = pl.BlockSpec(memory_space=pltpu.VMEM)
    names = (*inputs, *outputs, *scratch)
    return pl.pallas_call(
        functools.partial(layer_body, n_dp, pieces, names),
        out_shape=list(outputs.values()),
        in_specs=[vmem] * (len(inputs) - 1) + [pl.BlockSpec(memory_space=pl.ANY)],
        out_specs=[vmem] * len(outputs),
        scratch_shapes=list(scratch.values()),
        compiler_params=pltpu.CompilerParams(
            collective_id=ident, has_side_effects=True, vmem_limit_bytes=LAYER_VMEM
        ),
        name="layer",
    )(*inputs.values())


def pack_gains(blocks, width):
    n = blocks[0].shape[0]
    rows = [jnp.pad(block, ((0, 0), (0, width - block.shape[1]))) for block in blocks]
    packed = jnp.stack(rows, axis=1)
    return jnp.pad(packed, ((0, 0), (0, SUBLANES - len(blocks)), (0, 0)))


def stepwise(
    n_dp, hidden, cotangent, gains, gain_rows, w_query, w_output, w_kv, cosine, sine_table,
    segment_ids, ffn, columns,
):
    n_tensor = segment_ids.shape[0] // hidden.shape[0]
    wide = ffn.shape[-1]
    gains_all, wq_all, wo_all, kv_all = attention_weights(
        n_dp, gain_rows, w_query, w_output, w_kv, 0
    )
    full_in_gain, full_attn_gain, full_ffn_gain, full_out_gain, full_qgain, full_kgain = (
        gains_all[:, row, : gain.shape[0]].reshape(-1).astype(jnp.float32)
        for row, gain in enumerate(gains)
    )
    full_query, full_output = (block.reshape(-1, block.shape[-1]) for block in (wq_all, wo_all))
    full_key, full_value = (kv_all[i].reshape(-1, kv_all.shape[-1]) for i in range(2))
    wide_gains = jnp.stack([full_in_gain, full_attn_gain, full_ffn_gain, full_out_gain])
    head_gains = jnp.stack([full_qgain, full_kgain])
    (
        normed_in, query_raw, key_raw, query_rot, key_rot, value_rows, log_total, context,
        attn_rows, residual, ffn_in, ffn_all,
    ) = forward(
        n_dp,
        hidden,
        wide_gains,
        head_gains,
        full_query, full_key, full_value, full_output, cosine, sine_table, segment_ids, ffn, 1,
    )
    ffn_in = ffn_in.reshape(-1, ffn_in.shape[-1])
    full_gate, full_up, full_down = (ffn_all[i].reshape(-1, wide) for i in range(3))
    gate_pre = jnp.dot(ffn_in, full_gate, preferred_element_type=jnp.float32)
    up_pre = jnp.dot(ffn_in, full_up, preferred_element_type=jnp.float32)
    gelu_values, gelu_back = jax.vjp(gelu_tanh, gate_pre)
    mixed = (gelu_values * up_pre).astype(jnp.bfloat16)
    down_part = contract_cols(mixed, full_down)
    down_rows = scatter8(
        n_dp, down_part.astype(jnp.bfloat16).reshape(2, n_tensor, -1, down_part.shape[-1]), 4
    )
    output = (residual + apply_norm(down_rows, full_out_gain)).astype(jnp.bfloat16)
    cot_f = cotangent.astype(jnp.float32)
    grad_down, term_out = norm_back(down_rows, full_out_gain, cot_f)
    down_all = gather8(n_dp, grad_down.astype(jnp.bfloat16), 5).reshape(-1, grad_down.shape[-1])
    grad_wd = contract_rows(down_all, mixed)
    grad_mixed = jnp.dot(down_all, full_down, preferred_element_type=jnp.float32)
    gate_low = gelu_back(grad_mixed * up_pre)[0].astype(jnp.bfloat16)
    up_low = (grad_mixed * gelu_values).astype(jnp.bfloat16)
    grad_wg = contract_rows(ffn_in, gate_low)
    grad_wu = contract_rows(ffn_in, up_low)
    ffn_part = contract_cols(gate_low, full_gate) + contract_cols(up_low, full_up)
    ffn_back = scatter8(
        n_dp, ffn_part.astype(jnp.bfloat16).reshape(2, n_tensor, -1, ffn_part.shape[-1]), 6
    )
    grad_hidden, gain_sums, own_query, own_output, own_kv, own_ffn_weights = backward(
        n_dp, hidden, cotangent, ffn_back, residual, attn_rows,
        jnp.sum(term_out, axis=0, keepdims=True), wide_gains, head_gains,
        full_query, full_key, full_value, full_output, cosine, sine_table, segment_ids,
        normed_in, query_raw, key_raw, query_rot, key_rot, value_rows, log_total, context,
        jnp.stack(
            [
                grad.astype(jnp.bfloat16).reshape(n_dp, -1, grad.shape[-1])
                for grad in (grad_wd, grad_wg, grad_wu)
            ]
        ),
        columns,
        9,
    )
    return output, grad_hidden, gain_sums, own_query, own_output, own_kv, own_ffn_weights


def local(
    n_dp,
    n_tensor,
    hidden,
    in_gain,
    w_query,
    w_key,
    w_value,
    query_gain,
    key_gain,
    w_output,
    attn_gain,
    ffn_gain,
    w_gate,
    w_up,
    w_down,
    out_gain,
    cotangent,
    segment_ids,
    positions,
):
    gains = (in_gain, attn_gain, ffn_gain, out_gain, query_gain, key_gain)
    width = -(-max(gain.shape[0] for gain in gains) // LANES) * LANES
    gain_rows = pack_gains([gain[None] for gain in gains], width)[0]
    columns = w_gate.shape[1]
    wide = -(-columns // (2 * LANES)) * LANES
    ffn = jnp.stack([w_gate, w_up, w_down.T])
    ffn = jnp.pad(ffn, ((0, 0), (0, 0), (0, 2 * wide - columns)))
    ffn = jnp.stack([ffn[:, :, :wide], ffn[:, :, wide:]])
    cosine, sine_table = rotary_tables(positions, HD)
    w_kv = jnp.stack([w_key, w_value])
    if w_query.shape[0] % SUBLANES == 0:
        output, grad_hidden, gain_sums, own_query, own_output, own_kv, own_ffn_weights = layer(
            n_dp, hidden, cotangent, gain_rows, w_query, w_output.T, w_kv, cosine, sine_table,
            segment_ids, ffn, columns, 0,
        )
    else:
        output, grad_hidden, gain_sums, own_query, own_output, own_kv, own_ffn_weights = stepwise(
            n_dp, hidden, cotangent, gains, gain_rows, w_query, w_output.T, w_kv, cosine, sine_table,
            segment_ids, ffn, columns,
        )
    place = lax.axis_index("dp")
    own_in, own_attn, own_ffn, own_out, own_q, own_k = (
        lax.dynamic_slice(gain_sums[row], (place * gain.shape[0],), gain.shape)
        for row, gain in enumerate(gains)
    )
    return (
        output,
        grad_hidden,
        own_in,
        own_query,
        own_kv[0],
        own_kv[1],
        own_q,
        own_k,
        own_output.T,
        own_attn,
        own_ffn,
        own_ffn_weights[1],
        own_ffn_weights[2],
        own_ffn_weights[0].T,
        own_out,
    )


def solution(mesh):
    placed = (
        P(("dp", "tensor"), None),
        P("dp"),
        P("dp", "tensor"),
        P("dp", None),
        P("dp", None),
        P("dp"),
        P("dp"),
        P("tensor", "dp"),
        P("dp"),
        P("dp"),
        P("dp", "tensor"),
        P("dp", "tensor"),
        P("tensor", "dp"),
        P("dp"),
        P(("dp", "tensor"), None),
        P("dp"),
        P("dp"),
    )
    return jax.shard_map(
        functools.partial(local, mesh.shape["dp"], mesh.shape["tensor"]),
        mesh=mesh,
        in_specs=placed,
        out_specs=(
            P(("dp", "tensor"), None),
            P(("dp", "tensor"), None),
            P("dp"),
            P("dp", "tensor"),
            P("dp", None),
            P("dp", None),
            P("dp"),
            P("dp"),
            P("tensor", "dp"),
            P("dp"),
            P("dp"),
            P("dp", "tensor"),
            P("dp", "tensor"),
            P("tensor", "dp"),
            P("dp"),
        ),
        check_vma=False,
    )
```

```python
import functools
import math
import types

import jax
import jax.numpy as jnp
from jax import lax
from jax.experimental import pallas as pl
from jax.experimental.pallas import tpu as pltpu
from jax.sharding import PartitionSpec as P

HD = 256
WINDOW = 512


EPSILON = 1e-06
ROPE_BASE = 10000.0


def rms_scale(values):
    return lax.rsqrt(jnp.mean(values * values, axis=-1, keepdims=True) + EPSILON)


def apply_norm(values, gain_vec):
    return values * rms_scale(values) * gain_vec.astype(jnp.float32)


def norm_back(values, gain_vec, upstream):
    factor = rms_scale(values)
    unit_rows = values * factor
    scaled = upstream * gain_vec.astype(jnp.float32)
    grad_values = factor * (
        scaled - unit_rows * jnp.mean(scaled * unit_rows, axis=-1, keepdims=True)
    )
    return (grad_values, upstream * unit_rows)


def rotary_frequency(width):
    steps_half = jnp.arange(width // 2, dtype=jnp.float32)
    return ROPE_BASE ** (-2.0 * steps_half / width)


def rotary_tables(token_pos, width):
    angles = token_pos.astype(jnp.float32)[:, None] * rotary_frequency(width)[None, :]
    return (jnp.cos(angles), jnp.sin(angles))


def gelu_tanh(values):
    return jax.nn.gelu(values, approximate=True)


def contract_rows(left, right):
    return lax.dot_general(
        left, right, (((0,), (0,)), ((), ())), preferred_element_type=jnp.float32
    )


def contract_cols(left, right):
    return lax.dot_general(
        left, right, (((1,), (1,)), ((), ())), preferred_element_type=jnp.float32
    )


MESH = pl.DeviceIdType.MESH
LANES = 128
SUBLANES = 16
MIB = 1024 * 1024
LAYER_VMEM = 63 * MIB
GELU_SCALE = (2.0 / math.pi) ** 0.5
GELU_CUBE = 0.044715


def send_to(where, src, dst, send, recv):
    return pltpu.make_async_remote_copy(
        src_ref=src,
        dst_ref=dst,
        send_sem=send,
        recv_sem=recv,
        device_id=where,
        device_id_type=MESH,
    )


def meet(partners):
    barrier = pltpu.get_barrier_semaphore()
    for where in partners:
        pl.semaphore_signal(barrier, inc=1, device_id=where, device_id_type=MESH)
    pl.semaphore_wait(barrier, len(partners))


class Spot:
    def __init__(self, n_dp):
        self.n_rest = n_dp // 4
        self.dp = lax.axis_index("dp")
        self.t = lax.axis_index("tensor")
        self.x = self.t // 2
        self.core = self.t - 2 * self.x
        self.line = self.dp // self.n_rest
        self.rest = self.dp - self.line * self.n_rest
        self.half = self.line % 2
        high = self.line // 2
        self.lines = [
            self.line,
            2 * high + 1 - self.half,
            2 * (1 - high) + self.half,
            2 * (1 - high) + 1 - self.half,
        ]
        self.line_dp = [line * self.n_rest + self.rest for line in self.lines]
        self.line_at = [{"dp": dp} for dp in self.line_dp]
        self.rests = [(self.rest + r) % self.n_rest for r in range(self.n_rest)]
        self.rest_at = [{"dp": self.line * self.n_rest + rest} for rest in self.rests]
        self.from_rest = [
            (self.rest + self.n_rest - r) % self.n_rest for r in range(self.n_rest)
        ]
        self.t_mate = 2 * self.x + 1 - self.core
        self.t_side = 2 * (1 - self.x) + self.core
        self.t_side_mate = 2 * (1 - self.x) + 1 - self.core
        self.mate = {"tensor": self.t_mate}
        self.side = {"tensor": self.t_side}
        self.pair = self.line_at[1]


def row_pieces(rows, wanted):
    cuts = wanted if rows % (wanted * SUBLANES) == 0 else 1
    size = rows // cuts
    return [(cut * size, size) for cut in range(cuts)]


def gather8_body(n_dp, pieces, mine, full, own_sem, xs, xr, zs, zr, ds, dr, ms, mr):
    at = Spot(n_dp)
    meet([at.mate, at.side, at.pair])
    half, other = at.half, 1 - at.half

    def cut(ref, p):
        return ref.at[pl.ds(*pieces[p])]

    def over_x(p):
        return send_to(at.side, cut(mine, p), cut(full.at[half, at.t], p), xs.at[p], xr.at[p])

    def over_z(p):
        return send_to(at.pair, cut(mine, p), cut(full.at[half, at.t], p), zs.at[p], zr.at[p])

    def onward(p):
        if p % 2 == 0:
            block = cut(full.at[half, at.t_side], p)
            return send_to(at.pair, block, block, ds.at[p], dr.at[p])
        block = cut(full.at[other, at.t], p)
        return send_to(at.side, block, block, ds.at[p], dr.at[p])

    def near(j, p):
        place = cut(full.at[(half, half, other, other)[j], (at.t, at.t_side, at.t, at.t_side)[j]], p)
        source = cut(mine, p) if j == 0 else place
        return send_to(at.mate, source, place, ms.at[j, p], mr.at[j, p])

    count = len(pieces)
    for p in range(count):
        over_x(p).start()
        over_z(p).start()
    own = pltpu.make_async_copy(mine, full.at[half, at.t], own_sem)
    own.start()
    for p in range(count):
        near(0, p).start()
    for p in range(count):
        over_x(p).wait_recv()
        if p % 2 == 0:
            onward(p).start()
        near(1, p).start()
        over_z(p).wait_recv()
        if p % 2 == 1:
            onward(p).start()
        near(2, p).start()
    for p in range(count):
        onward(p).wait_recv()
        near(3, p).start()
    own.wait()
    for p in range(count):
        over_x(p).wait_send()
        over_z(p).wait_send()
        onward(p).wait_send()
        for j in range(4):
            near(j, p).wait()


def gather8(n_dp, block, ident):
    pieces = row_pieces(block.shape[0], 10)
    count = len(pieces)
    one = pltpu.SemaphoreType.DMA((count,))
    four = pltpu.SemaphoreType.DMA((4, count))
    return pl.pallas_call(
        functools.partial(gather8_body, n_dp, pieces),
        out_shape=jax.ShapeDtypeStruct((2, 4, *block.shape), block.dtype),
        in_specs=[pl.BlockSpec(memory_space=pltpu.VMEM)],
        out_specs=pl.BlockSpec(memory_space=pl.ANY),
        scratch_shapes=[pltpu.SemaphoreType.DMA, one, one, one, one, one, one, four, four],
        compiler_params=pltpu.CompilerParams(collective_id=ident, has_side_effects=True),
        name=f"gather8_{ident}",
    )(block)


def add_up(left, right):
    return left.astype(jnp.float32) + right.astype(jnp.float32)


def scatter8_body(
    n_dp, pieces, parts, out, held, come, last, ms, mr, fs, fr, ls, lr
):
    at = Spot(n_dp)
    meet([at.mate, at.side, at.pair])
    half, other = at.half, 1 - at.half
    halves = (half, half, other, other)
    mine_t = (at.t, at.t_side, at.t, at.t_side)
    mate_t = (at.t_mate, at.t_side_mate, at.t_mate, at.t_side_mate)
    count = len(pieces)

    def near(k, p):
        rows = pl.ds(*pieces[p])
        return send_to(
            at.mate, parts.at[halves[k], mate_t[k], rows], held.at[k, rows], ms.at[k, p], mr.at[k, p]
        )

    def first(j, p):
        rows = pl.ds(*pieces[p])
        if p % 2 == 0:
            return send_to(at.side, held.at[(1, 3)[j], rows], come.at[j, rows], fs.at[j, p], fr.at[j, p])
        return send_to(at.pair, held.at[(2, 3)[j], rows], come.at[j, rows], fs.at[j, p], fr.at[j, p])

    def second(p):
        rows = pl.ds(*pieces[p])
        if p % 2 == 0:
            return send_to(at.pair, held.at[2, rows], last.at[rows], ls.at[p], lr.at[p])
        return send_to(at.side, held.at[1, rows], last.at[rows], ls.at[p], lr.at[p])

    for p in range(count):
        for k in (3, 1, 2, 0):
            near(k, p).start()
    for p in range(count):
        rows = pl.ds(*pieces[p])
        for k in (3, 1, 2, 0):
            near(k, p).wait_recv()
            held[k, rows] = add_up(parts[halves[k], mine_t[k], rows], held[k, rows]).astype(jnp.bfloat16)
        first(1, p).start()
        first(0, p).start()
    for p in range(count):
        rows = pl.ds(*pieces[p])
        keep = 2 if p % 2 == 0 else 1
        first(1, p).wait_recv()
        held[keep, rows] = add_up(held[keep, rows], come[1, rows]).astype(jnp.bfloat16)
        second(p).start()
        first(0, p).wait_recv()
        out[rows] = add_up(held[0, rows], come[0, rows])
    for p in range(count):
        rows = pl.ds(*pieces[p])
        second(p).wait_recv()
        out[rows] = out[rows] + last[rows].astype(jnp.float32)
    for p in range(count):
        for k in range(4):
            near(k, p).wait_send()
        for j in range(2):
            first(j, p).wait_send()
        second(p).wait_send()


def scatter8(n_dp, parts, ident):
    rows, width = parts.shape[2:]
    pieces = row_pieces(rows, 10)
    count = len(pieces)

    def sems(*shape):
        return pltpu.SemaphoreType.DMA((*shape, count))

    return pl.pallas_call(
        functools.partial(scatter8_body, n_dp, pieces),
        out_shape=jax.ShapeDtypeStruct((rows, width), jnp.float32),
        in_specs=[pl.BlockSpec(memory_space=pltpu.VMEM)],
        out_specs=pl.BlockSpec(memory_space=pltpu.VMEM),
        scratch_shapes=[
            pltpu.VMEM((4, rows, width), jnp.bfloat16),
            pltpu.VMEM((2, rows, width), jnp.bfloat16),
            pltpu.VMEM((rows, width), jnp.bfloat16),
            sems(4), sems(4), sems(2), sems(2), sems(), sems(),
        ],
        compiler_params=pltpu.CompilerParams(
            collective_id=ident, has_side_effects=True, vmem_limit_bytes=40 * MIB
        ),
        name=f"scatter8_{ident}",
    )(parts)


def weights_body(
    n_dp, gains, wq, wo, kv, gains_all, wq_all, wo_all, kv_all, own_sem, zs, zr, rs, rr, ks, kr
):
    at = Spot(n_dp)
    meet([at.mate] + at.line_at[1:] + at.rest_at[1:])

    def source(c):
        return kv.at[at.core] if c == 3 else (gains, wq, wo)[c]

    def place(c, dp):
        return kv_all.at[at.core, dp] if c == 3 else (gains_all, wq_all, wo_all)[c].at[dp]

    def along(c, k):
        return send_to(at.line_at[k], source(c), place(c, at.dp), zs.at[c, k], zr.at[c, k])

    def across(c, k, r):
        spot = place(c, at.line_dp[k])
        return send_to(
            at.rest_at[r], source(c) if k == 0 else spot, spot, rs.at[c, k, r], rr.at[c, k, r]
        )

    order = (0, 3, 1, 2)
    for c in order:
        for k in (1, 2, 3):
            along(c, k).start()
        for r in range(1, at.n_rest):
            across(c, 0, r).start()
    own = [pltpu.make_async_copy(source(c), place(c, at.dp), own_sem.at[c]) for c in order]
    for copy in own:
        copy.start()
    for c in order:
        for k in (1, 2, 3):
            along(c, k).wait_recv()
            for r in range(1, at.n_rest):
                across(c, k, r).start()
    for copy in own:
        copy.wait()
    share = send_to(at.mate, kv_all.at[at.core], kv_all.at[at.core], ks, kr)
    for c in (3, 0, 1, 2):
        for k in range(4):
            for r in range(1, at.n_rest):
                across(c, k, r).wait()
            if k:
                along(c, k).wait_send()
        if c == 3:
            share.start()
    share.wait()


def attention_weights(n_dp, gains, wq, wo, kv, ident):
    line = pltpu.SemaphoreType.DMA((4, 4))
    rest = pltpu.SemaphoreType.DMA((4, 4, n_dp // 4))
    any_space = pl.BlockSpec(memory_space=pl.ANY)

    def shape(*dims):
        return jax.ShapeDtypeStruct(dims, jnp.bfloat16)

    return pl.pallas_call(
        functools.partial(weights_body, n_dp),
        out_shape=[
            shape(n_dp, *gains.shape), shape(n_dp, *wq.shape), shape(n_dp, *wo.shape),
            shape(2, n_dp, *kv.shape[1:]),
        ],
        in_specs=[pl.BlockSpec(memory_space=pltpu.VMEM)] * 4,
        out_specs=[any_space] * 4,
        scratch_shapes=[
            pltpu.SemaphoreType.DMA((4,)), line, line, rest, rest,
            pltpu.SemaphoreType.DMA, pltpu.SemaphoreType.DMA,
        ],
        compiler_params=pltpu.CompilerParams(collective_id=ident, has_side_effects=True),
        name="attention_weights",
    )(gains, wq, wo, kv)


class Background:
    def __init__(self, at, ffn, ffn_all, own_sem, zs, zr, rs, rr):
        self.at, self.ffn, self.ffn_all = at, ffn, ffn_all
        self.own_sem, self.zs, self.zr, self.rs, self.rr = own_sem, zs, zr, rs, rr
        self.halves = (at.half, 1 - at.half, at.half, 1 - at.half)

    def along(self, c, k):
        at = self.at
        return send_to(
            at.line_at[k], self.ffn.at[self.halves[k], c], self.ffn_all.at[c, at.dp],
            self.zs.at[c, k], self.zr.at[c, k],
        )

    def across(self, c, k, r):
        at = self.at
        spot = self.ffn_all.at[c, at.line_dp[k]]
        source = self.ffn.at[at.half, c] if k == 0 else spot
        return send_to(at.rest_at[r], source, spot, self.rs.at[c, k, r], self.rr.at[c, k, r])

    def own(self, c):
        at = self.at
        return pltpu.make_async_copy(
            self.ffn.at[at.half, c], self.ffn_all.at[c, at.dp], self.own_sem.at[c]
        )

    def launch(self, c):
        for k in (2, 3, 1):
            self.along(c, k).start()
        for r in range(1, self.at.n_rest):
            self.across(c, 0, r).start()
        self.own(c).start()

    def forward(self, c, ks=(2, 3, 1)):
        for k in ks:
            self.along(c, k).wait_recv()
            for r in range(1, self.at.n_rest):
                self.across(c, k, r).start()

    def finish(self, c):
        self.own(c).wait()
        for k in range(4):
            for r in range(1, self.at.n_rest):
                self.across(c, k, r).wait()
            if k:
                self.along(c, k).wait_send()


def dot(left, right):
    return jnp.dot(left, right, preferred_element_type=jnp.float32)


def turn(values, cosine, sine_table):
    half_width = values.shape[-1] // 2
    first_half = values[:, :half_width]
    second = values[:, half_width:]
    return jnp.concatenate(
        [first_half * cosine - second * sine_table, second * cosine + first_half * sine_table],
        axis=-1,
    )


class Gather4:
    def __init__(self, at, pieces, mine, full, xs, xr, ms, mr):
        self.at, self.pieces, self.mine, self.full = at, pieces, mine, full
        self.xs, self.xr, self.ms, self.mr = xs, xr, ms, mr

    def over_x(self, p):
        rows, at = pl.ds(*self.pieces[p]), self.at
        return send_to(
            at.side, self.mine.at[rows], self.full.at[at.t, rows], self.xs.at[p], self.xr.at[p]
        )

    def near(self, p):
        rows, at = pl.ds(*self.pieces[p]), self.at
        block = self.full.at[at.t_side, rows]
        return send_to(at.mate, block, block, self.ms.at[p], self.mr.at[p])

    def near_own(self):
        at, p = self.at, len(self.pieces)
        return send_to(at.mate, self.mine, self.full.at[at.t], self.ms.at[p], self.mr.at[p])

    def start(self):
        for p in range(len(self.pieces)):
            self.over_x(p).start()
        self.near_own().start()

    def pass_on(self):
        for p in range(len(self.pieces)):
            self.over_x(p).wait_recv()
            self.near(p).start()

    def all_here(self):
        for p in range(len(self.pieces)):
            self.near(p).wait_recv()

    def finish(self):
        self.near_own().wait_send()
        for p in range(len(self.pieces)):
            self.over_x(p).wait_send()
            self.near(p).wait_send()


class Scatter4:
    def __init__(self, at, pieces, parts, held, come, ms, mr, fs, fr):
        self.at, self.pieces, self.parts, self.held, self.come = at, pieces, parts, held, come
        self.ms, self.mr, self.fs, self.fr = ms, mr, fs, fr
        self.mate_t = (at.t_mate, at.t_side_mate)

    def near(self, k):
        return send_to(
            self.at.mate, self.parts.at[self.mate_t[k]], self.held.at[k], self.ms.at[k], self.mr.at[k]
        )

    def far(self, p):
        rows = pl.ds(*self.pieces[p])
        return send_to(
            self.at.side, self.held.at[1, rows], self.come.at[rows], self.fs.at[p], self.fr.at[p]
        )

    def send_side(self):
        self.near(1).wait_recv()
        for p, piece in enumerate(self.pieces):
            rows = pl.ds(*piece)
            self.held[1, rows] = add_up(self.parts[self.at.t_side, rows], self.held[1, rows]).astype(
                jnp.bfloat16
            )
            self.far(p).start()

    def result(self, out):
        self.near(0).wait_recv()
        for p, piece in enumerate(self.pieces):
            rows = pl.ds(*piece)
            self.far(p).wait_recv()
            out[rows] = add_up(self.parts[self.at.t, rows], self.held[0, rows]) + self.come[
                rows
            ].astype(jnp.float32)

    def finish(self):
        for k in range(2):
            self.near(k).wait_send()
        for p in range(len(self.pieces)):
            self.far(p).wait_send()


class Gather8:
    def __init__(self, at, pieces, mine, full, xs, xr, zs, zr, ds, dr, ms, mr):
        self.at, self.pieces, self.mine, self.full = at, pieces, mine, full
        self.xs, self.xr, self.zs, self.zr = xs, xr, zs, zr
        self.ds, self.dr, self.ms, self.mr = ds, dr, ms, mr

    def spot(self, z, t, p):
        return self.full.at[z, t, pl.ds(*self.pieces[p])]

    def over_x(self, p):
        at = self.at
        return send_to(
            at.side, self.mine.at[pl.ds(*self.pieces[p])], self.spot(at.half, at.t, p),
            self.xs.at[p], self.xr.at[p],
        )

    def over_z(self, p):
        at = self.at
        return send_to(
            at.pair, self.mine.at[pl.ds(*self.pieces[p])], self.spot(at.half, at.t, p),
            self.zs.at[p], self.zr.at[p],
        )

    def onward(self, p):
        at = self.at
        if p % 2 == 0:
            block = self.spot(at.half, at.t_side, p)
            return send_to(at.pair, block, block, self.ds.at[p], self.dr.at[p])
        block = self.spot(1 - at.half, at.t, p)
        return send_to(at.side, block, block, self.ds.at[p], self.dr.at[p])

    def near(self, j, p):
        at = self.at
        z = (at.half, at.half, 1 - at.half, 1 - at.half)[j]
        place = self.spot(z, (at.t, at.t_side, at.t, at.t_side)[j], p)
        source = self.mine.at[pl.ds(*self.pieces[p])] if j == 0 else place
        return send_to(at.mate, source, place, self.ms.at[j, p], self.mr.at[j, p])

    def start(self, p):
        self.over_x(p).start()
        self.over_z(p).start()
        self.near(0, p).start()

    def pass_on(self):
        for p in range(len(self.pieces)):
            self.over_x(p).wait_recv()
            if p % 2 == 0:
                self.onward(p).start()
            self.near(1, p).start()
            self.over_z(p).wait_recv()
            if p % 2 == 1:
                self.onward(p).start()
            self.near(2, p).start()

    def pass_x(self):
        for p in range(len(self.pieces)):
            self.over_x(p).wait_recv()
            if p % 2 == 0:
                self.onward(p).start()
            self.near(1, p).start()

    def pass_z(self):
        for p in range(len(self.pieces)):
            self.over_z(p).wait_recv()
            if p % 2 == 1:
                self.onward(p).start()
            self.near(2, p).start()

    def pass_last(self):
        for p in range(len(self.pieces)):
            self.onward(p).wait_recv()
            self.near(3, p).start()

    def here(self, j):
        for p in range(len(self.pieces)):
            self.near(j, p).wait_recv()

    def finish(self):
        for p in range(len(self.pieces)):
            self.over_x(p).wait_send()
            self.over_z(p).wait_send()
            self.onward(p).wait_send()
            for j in range(4):
                self.near(j, p).wait_send()


def forward_body(
    n_dp, pieces,
    hidden, gains, head_gains, wq, wk, wv, wo, cosine, sine, seg_col, seg_row, ffn,
    a_all, q_raw, k_raw, q_rot, k_rot, v_all, lse, ctx, u_out, h_out, c_all, ffn_all,
    a_own, c_own, parts, held, come,
    own_sem, bzs, bzr, brs, brr, gxs, gxr, gms, gmr, sms, smr, sfs, sfr,
    xs, xr, zs, zr, ds, dr, ms, mr,
):
    at = Spot(n_dp)
    meet([at.mate, at.side] + at.line_at[1:] + at.rest_at[1:])
    load = Background(at, ffn, ffn_all, own_sem, bzs, bzr, brs, brr)
    count = ffn.shape[1]
    size = hidden.shape[0]
    load.launch(0)
    if count > 1:
        load.launch(1)

    def gain(row):
        return gains[row : row + 1, :]

    bring = Gather4(at, pieces, a_own, a_all, gxs, gxr, gms, gmr)
    for piece in pieces:
        rows = pl.ds(*piece)
        a_own[rows] = apply_norm(hidden[rows].astype(jnp.float32), gain(0)).astype(jnp.bfloat16)
    bring.start()
    a_all[at.t] = a_own[...]

    def project(t):
        rows = pl.ds(pl.multiple_of(t * size, SUBLANES), size)
        a = a_all[t]
        q = dot(a, wq[...])
        q_raw[t] = q
        q_rot[t] = turn(apply_norm(q, head_gains[0:1, :]), cosine[t], sine[t]).astype(jnp.bfloat16)
        k = dot(a, wk[...])
        k_raw[t] = k
        k_rot[rows] = turn(apply_norm(k, head_gains[1:2, :]), cosine[t], sine[t]).astype(
            jnp.bfloat16
        )
        v_all[rows] = dot(a, wv[...]).astype(jnp.bfloat16)

    project(at.t)
    bring.near_own().wait_recv()
    project(at.t_mate)
    bring.pass_on()
    project(at.t_side)
    bring.all_here()
    project(at.t_side_mate)

    def attend(t):
        scores = contract_cols(q_rot[t], k_rot[...]) * HD ** (-0.5)
        row = lax.broadcasted_iota(jnp.int32, scores.shape, 0) + t * size
        behind = row - lax.broadcasted_iota(jnp.int32, scores.shape, 1)
        allowed = (seg_col[t] == seg_row[...]) & (behind >= 0) & (behind < WINDOW)
        weights = jnp.where(allowed, jnp.exp(scores), 0.0)
        total = jnp.sum(weights, axis=-1, keepdims=True)
        lse[t] = jnp.log(total)
        mixed = dot((weights / total).astype(jnp.bfloat16), v_all[...]).astype(jnp.bfloat16)
        ctx[t] = mixed
        parts[t] = contract_cols(mixed, wo[...]).astype(jnp.bfloat16)

    back = Scatter4(at, pieces, parts, held, come, sms, smr, sfs, sfr)
    attend(at.t_side_mate)
    back.near(1).start()
    attend(at.t_side)
    back.send_side()
    attend(at.t_mate)
    back.near(0).start()
    attend(at.t)
    load.forward(0)
    back.result(u_out)
    spread = Gather8(at, pieces, c_own, c_all, xs, xr, zs, zr, ds, dr, ms, mr)
    for p, piece in enumerate(pieces):
        rows = pl.ds(*piece)
        total = hidden[rows].astype(jnp.float32) + apply_norm(u_out[rows], gain(1))
        h_out[rows] = total
        c_own[rows] = apply_norm(total, gain(2)).astype(jnp.bfloat16)
        spread.start(p)
    for c in range(2, count):
        load.launch(c)
    c_all[at.half, at.t] = c_own[...]
    if count > 1:
        load.forward(1)
    spread.pass_on()
    spread.pass_last()
    for c in range(2, count):
        load.forward(c)
    for k in range(4):
        spread.here(k)
    bring.finish()
    back.finish()
    spread.finish()
    for c in range(count):
        load.finish(c)


def forward(n_dp, hidden, gains, head_gains, wq, wk, wv, wo, cosine, sine, seg_ids, ffn, ident):
    size, width = hidden.shape
    n_tensor = seg_ids.shape[0] // size
    parts = ffn.shape[1]
    pieces = row_pieces(size, 10)
    count = len(pieces)
    head = wq.shape[1]
    vmem = pl.BlockSpec(memory_space=pltpu.VMEM)
    any_space = pl.BlockSpec(memory_space=pl.ANY)

    def low(*dims):
        return jax.ShapeDtypeStruct(dims, jnp.bfloat16)

    def full(*dims):
        return jax.ShapeDtypeStruct(dims, jnp.float32)

    def dma(*dims):
        return pltpu.SemaphoreType.DMA(dims)

    line, rest = dma(parts, 4), dma(parts, 4, n_dp // 4)
    blocked = (n_tensor, size)
    return pl.pallas_call(
        functools.partial(forward_body, n_dp, pieces),
        out_shape=[
            low(*blocked, width), full(*blocked, head), full(*blocked, wk.shape[1]),
            low(*blocked, head), low(n_tensor * size, wk.shape[1]), low(n_tensor * size, wv.shape[1]),
            full(*blocked, 1), low(*blocked, head), full(size, width), full(size, width),
            low(2, *blocked, width), low(parts, n_dp, *ffn.shape[2:]),
        ],
        in_specs=[vmem] * 11 + [any_space],
        out_specs=[vmem] * 11 + [any_space],
        scratch_shapes=[
            pltpu.VMEM((size, width), jnp.bfloat16), pltpu.VMEM((size, width), jnp.bfloat16),
            pltpu.VMEM((*blocked, width), jnp.bfloat16), pltpu.VMEM((2, size, width), jnp.bfloat16),
            pltpu.VMEM((size, width), jnp.bfloat16),
            dma(parts), line, line, rest, rest,
            dma(count), dma(count), dma(count + 1), dma(count + 1),
            dma(2), dma(2), dma(count), dma(count),
            dma(count), dma(count), dma(count), dma(count), dma(count), dma(count),
            dma(4, count), dma(4, count),
        ],
        compiler_params=pltpu.CompilerParams(
            collective_id=ident, has_side_effects=True, vmem_limit_bytes=56 * MIB
        ),
        name="forward",
    )(
        hidden, gains, head_gains, wq, wk, wv, wo,
        cosine.reshape(*blocked, -1), sine.reshape(*blocked, -1),
        seg_ids.reshape(*blocked, 1), seg_ids.reshape(1, -1), ffn,
    )


def by_rows(rows, body):
    step = SUBLANES if rows % SUBLANES == 0 else rows
    if step == rows:
        body(slice(None))
        return

    def one(i, carry):
        body(pl.ds(pl.multiple_of(i * step, step), step))
        return carry

    lax.fori_loop(0, rows // step, one, 0)


class Sums:
    def __init__(self, at, blocks, owns, landed, distant, rs, rr, zs, zr):
        self.at, self.blocks, self.owns, self.landed, self.distant = at, blocks, owns, landed, distant
        self.rs, self.rr, self.zs, self.zr = rs, rr, zs, zr
        self.turns = (2, 3, 1, 0)

    def across(self, c, k, r):
        at = self.at
        target = at.lines[k] * at.n_rest + at.rests[r]
        return send_to(
            at.rest_at[r], self.blocks[c](target), self.landed[c].at[k, r - 1],
            self.rs.at[c, k, r], self.rr.at[c, k, r],
        )

    def along(self, c, k):
        return send_to(
            self.at.line_at[k], self.landed[c].at[k, 0], self.distant[c].at[k - 1],
            self.zs.at[c, k], self.zr.at[c, k],
        )

    def start(self, c):
        for k in self.turns:
            for r in range(1, self.at.n_rest):
                self.across(c, k, r).start()

    def add(self, c, k):
        at, come = self.at, self.landed[c]
        for r in range(1, at.n_rest):
            self.across(c, k, r).wait_recv()
        own = self.owns[c](k)

        def one(rows):
            total = own[rows].astype(jnp.float32)
            for r in range(1, at.n_rest):
                total = total + come[k, r - 1, rows].astype(jnp.float32)
            come[k, 0, rows] = total.astype(jnp.bfloat16)

        by_rows(come.shape[2], one)
        if k:
            self.along(c, k).start()

    def arrive(self, c):
        for k in (1, 2, 3):
            self.along(c, k).wait_recv()

    def finish(self, c):
        for k in self.turns:
            for r in range(1, self.at.n_rest):
                self.across(c, k, r).wait_send()
            if k:
                self.along(c, k).wait_send()


def backward_body(
    n_dp, pieces,
    hidden, cot, back_rows, h_rows, u_rows, term_out, gains, head_gains, wq, wk, wv, wo,
    cosine, sine, seg_col, seg_row, a_all, q_raw, k_raw, q_rot, k_rot, v_all, lse, ctx, ffn,
    hidden_out, gains_out, wq_out, wo_out, kv_out, ffn_out,
    dh, du_own, du_all, parts, held, come, dctx, dv, dk, dq_low, dk_low, dv_low, wide,
    wq_part, wo_part, kv_part, kv_held, ffn_own, wq_in, wo_in, kv_in, ffn_in,
    wq_far, wo_far, kv_far, ffn_far, kv_pool, terms, pool_t, pool_r, pool_z,
    own_sem, rs, rr, zs, zr, ks, kr, gxs, gxr, gms, gmr, sms, smr, sfs, sfr, ts, tr, us, ur, vs, vr,
):
    at = Spot(n_dp)
    others = [at.mate, at.side, {"tensor": at.t_side_mate}]
    meet(others + at.line_at[1:] + at.rest_at[1:])
    n_ffn = ffn.shape[0]
    size = hidden.shape[0]
    c_wo, c_wq, c_kv = n_ffn, n_ffn + 1, n_ffn + 2
    factor = HD ** (-0.5)

    def of_ffn(c):
        return lambda dp: ffn.at[c, dp]

    def own_ffn(c):
        return lambda k: ffn_own.at[c, k]

    def of(ref):
        return lambda dp: ref.at[dp]

    def own(ref):
        return lambda k: ref.at[at.line_dp[k]]

    sums = Sums(
        at,
        [of_ffn(c) for c in range(n_ffn)] + [of(wo_part), of(wq_part), of(kv_held)],
        [own_ffn(c) for c in range(n_ffn)] + [own(wo_part), own(wq_part), own(kv_held)],
        [ffn_in.at[c] for c in range(n_ffn)] + [wo_in, wq_in, kv_in],
        [ffn_far.at[c] for c in range(n_ffn)] + [wo_far, wq_far, kv_far],
        rs, rr, zs, zr,
    )
    for c in range(n_ffn):
        sums.start(c)
    keep = [
        pltpu.make_async_copy(ffn.at[c, at.line_dp[k]], ffn_own.at[c, k], own_sem.at[c, k])
        for c in range(n_ffn)
        for k in range(4)
    ]
    for copy in keep:
        copy.start()
    steps = [(c, k) for c in range(n_ffn) for k in sums.turns]

    def pump(count):
        for _ in range(count):
            if steps:
                sums.add(*steps.pop(0))

    def gain(row):
        return gains[row : row + 1, :]

    def column_sum(values):
        return jnp.sum(values, axis=0, keepdims=True)

    width = hidden.shape[1]
    head = q_raw.shape[-1]
    terms[...] = jnp.zeros_like(terms)
    terms[3:4, :] = term_out[...]
    bring = Gather4(at, pieces, du_own, du_all, gxs, gxr, gms, gmr)
    sum_ffn = jnp.zeros((1, width), jnp.float32)
    sum_attn = jnp.zeros((1, width), jnp.float32)
    for p, piece in enumerate(pieces):
        rows = pl.ds(*piece)
        grad_norm, term = norm_back(h_rows[rows], gain(2), back_rows[rows])
        sum_ffn += column_sum(term)
        total = cot[rows].astype(jnp.float32) + grad_norm
        dh[rows] = total
        grad_u, term = norm_back(u_rows[rows], gain(1), total)
        sum_attn += column_sum(term)
        du_own[rows] = grad_u.astype(jnp.bfloat16)
        bring.over_x(p).start()
    terms[1:2, :] = sum_attn
    terms[2:3, :] = sum_ffn
    bring.near_own().start()
    du_all[at.t] = du_own[...]
    for copy in keep:
        copy.wait()

    def back_ctx(t):
        dctx[t] = dot(du_all[t], wo[...]).astype(jnp.bfloat16)

    back_ctx(at.t)
    bring.near_own().wait_recv()
    back_ctx(at.t_mate)
    bring.pass_on()
    back_ctx(at.t_side)
    bring.all_here()
    back_ctx(at.t_side_mate)
    n_tensor = du_all.shape[0]
    dr = wo_part.shape[1]

    def weight_grad(out, left, right):
        total = contract_rows(left[0], right[0])
        for t in range(1, n_tensor):
            total = total + contract_rows(left[t], right[t])
        wide[...] = total
        for i in range(n_dp):
            out[i] = wide[i * dr : (i + 1) * dr].astype(jnp.bfloat16)

    weight_grad(wo_part, du_all, ctx)
    sums.start(c_wo)
    pump(3)

    def attend_back(t):
        scores = contract_cols(q_rot[t], k_rot[...]) * factor
        row = lax.broadcasted_iota(jnp.int32, scores.shape, 0) + t * size
        behind = row - lax.broadcasted_iota(jnp.int32, scores.shape, 1)
        allowed = (seg_col[t] == seg_row[...]) & (behind >= 0) & (behind < WINDOW)
        probs = jnp.where(allowed, jnp.exp(scores - lse[t]), 0.0)
        grad_probs = contract_cols(dctx[t], v_all[...])
        delta = jnp.sum(probs * grad_probs, axis=-1, keepdims=True)
        grad_scores = (probs * (grad_probs - delta) * factor).astype(jnp.bfloat16)
        grad_q = dot(grad_scores, k_rot[...])
        low, term = norm_back(q_raw[t], head_gains[0:1, :], turn(grad_q, cosine[t], -sine[t]))
        dq_low[t] = low.astype(jnp.bfloat16)
        return (
            contract_rows(probs.astype(jnp.bfloat16), dctx[t]),
            contract_rows(grad_scores, q_rot[t]),
            column_sum(term),
        )

    add_v, add_k, sum_q = attend_back(0)
    dv[...] = add_v
    dk[...] = add_k
    for t in range(1, n_tensor):
        add_v, add_k, more = attend_back(t)
        dv[...] += add_v
        dk[...] += add_k
        sum_q += more
    sum_k = jnp.zeros((1, head), jnp.float32)
    for t in range(n_tensor):
        rows = pl.ds(t * size, size)
        low, term = norm_back(k_raw[t], head_gains[1:2, :], turn(dk[rows], cosine[t], -sine[t]))
        dk_low[t] = low.astype(jnp.bfloat16)
        sum_k += column_sum(term)
        dv_low[t] = dv[rows].astype(jnp.bfloat16)
    terms[4:5, :head] = sum_q
    terms[5:6, :head] = sum_k
    pump(2)

    def back_in(t):
        parts[t] = (
            contract_cols(dq_low[t], wq[...])
            + contract_cols(dk_low[t], wk[...])
            + contract_cols(dv_low[t], wv[...])
        ).astype(jnp.bfloat16)

    back = Scatter4(at, pieces, parts, held, come, sms, smr, sfs, sfr)
    back_in(at.t_side_mate)
    back.near(1).start()
    back_in(at.t_side)
    back.send_side()
    back_in(at.t_mate)
    back.near(0).start()
    back_in(at.t)
    weight_grad(kv_part.at[0], a_all, dk_low)
    weight_grad(kv_part.at[1], a_all, dv_low)
    mate_kv = send_to(at.mate, kv_part.at[1 - at.core], kv_held, ks.at[0], kr.at[0])
    mate_kv.start()
    weight_grad(wq_part, a_all, dq_low)
    sums.start(c_wq)
    mate_kv.wait()

    def pair_up(dp, carry):
        def add(rows):
            kv_held[dp, rows] = add_up(kv_part[at.core, dp, rows], kv_held[dp, rows]).astype(
                jnp.bfloat16
            )

        by_rows(kv_held.shape[1], add)
        return carry

    lax.fori_loop(0, n_dp, pair_up, 0)
    sums.start(c_kv)
    pump(1)
    back.near(0).wait_recv()
    sum_in = jnp.zeros((1, width), jnp.float32)
    for p, piece in enumerate(pieces):
        rows = pl.ds(*piece)
        back.far(p).wait_recv()
        total = add_up(parts[at.t, rows], held[0, rows]) + come[rows].astype(jnp.float32)
        grad_norm, term = norm_back(hidden[rows].astype(jnp.float32), gain(0), total)
        hidden_out[rows] = dh[rows] + grad_norm
        sum_in += column_sum(term)
    terms[0:1, :] = sum_in

    pool_t[at.t] = terms[...].astype(jnp.bfloat16)
    over_t = [
        send_to(where, pool_t.at[at.t], pool_t.at[at.t], ts.at[j], tr.at[j])
        for j, where in enumerate(others)
    ]
    for copy in over_t:
        copy.start()
    pump(2)
    for copy in over_t:
        copy.wait()
    total = pool_t[0].astype(jnp.float32)
    for t in range(1, n_tensor):
        total = total + pool_t[t].astype(jnp.float32)
    pool_r[at.rest] = total.astype(jnp.bfloat16)
    over_r = [
        send_to(at.rest_at[r], pool_r.at[at.rest], pool_r.at[at.rest], us.at[r], ur.at[r])
        for r in range(1, at.n_rest)
    ]
    for copy in over_r:
        copy.start()
    pump(len(steps))
    for copy in over_r:
        copy.wait()
    total = pool_r[0].astype(jnp.float32)
    for r in range(1, at.n_rest):
        total = total + pool_r[r].astype(jnp.float32)
    pool_z[at.line] = total.astype(jnp.bfloat16)
    over_z = [
        send_to(at.line_at[k], pool_z.at[at.line], pool_z.at[at.line], vs.at[k], vr.at[k])
        for k in (1, 2, 3)
    ]
    for copy in over_z:
        copy.start()
    for c in (c_wo, c_wq, c_kv):
        for k in sums.turns:
            sums.add(c, k)
    half_width = ffn.shape[-1]
    for c in range(n_ffn):
        sums.arrive(c)

        def finish(first, own=ffn_in.at[c, 0, 0], far=ffn_far.at[c], target=ffn_out.at[c]):
            def put(rows):
                same = add_up(own[rows], far[1, rows])
                cross = add_up(far[0, rows], far[2, rows])
                low, high = (same, cross) if first else (cross, same)
                target[rows, :half_width] = low
                target[rows, half_width:] = high[:, : target.shape[-1] - half_width]

            by_rows(own.shape[0], put)

        @pl.when(at.half == 0)
        def _(finish=finish):
            finish(True)

        @pl.when(at.half == 1)
        def _(finish=finish):
            finish(False)

    for copy in over_z:
        copy.wait()
    gains_out[...] = add_up(pool_z[0], pool_z[1]) + add_up(pool_z[2], pool_z[3])
    sums.arrive(c_wo)
    wo_out[...] = add_up(wo_in[0, 0], wo_far[0]) + add_up(wo_far[1], wo_far[2])
    sums.arrive(c_wq)
    wq_out[...] = add_up(wq_in[0, 0], wq_far[0]) + add_up(wq_far[1], wq_far[2])
    sums.arrive(c_kv)
    kv_pool[0] = (add_up(kv_in[0, 0], kv_far[0]) + add_up(kv_far[1], kv_far[2])).astype(jnp.bfloat16)
    kv_side = send_to(at.side, kv_pool.at[0], kv_pool.at[1], ks.at[1], kr.at[1])
    kv_side.start()
    kv_side.wait()
    kv_out[at.core] = add_up(kv_pool[0], kv_pool[1])
    give = send_to(at.mate, kv_out.at[at.core], kv_out.at[at.core], ks.at[2], kr.at[2])
    give.start()
    give.wait()
    for c in range(n_ffn + 3):
        sums.finish(c)
    bring.finish()
    back.finish()


def backward(
    n_dp, hidden, cot, back_rows, h_rows, u_rows, term_out, gains, head_gains, wq, wk, wv, wo,
    cosine, sine, seg_ids, a_all, q_raw, k_raw, q_rot, k_rot, v_all, lse, ctx, ffn, columns, ident,
):
    size, width = hidden.shape
    n_tensor = seg_ids.shape[0] // size
    n_ffn, _, dr, half_width = ffn.shape
    n_rest = n_dp // 4
    head = wq.shape[1]
    pieces = row_pieces(size, 10)
    count = len(pieces)
    vmem = pl.BlockSpec(memory_space=pltpu.VMEM)
    blocked = (n_tensor, size)

    def out(*dims):
        return jax.ShapeDtypeStruct(dims, jnp.float32)

    def low(*dims):
        return pltpu.VMEM(dims, jnp.bfloat16)

    def full(*dims):
        return pltpu.VMEM(dims, jnp.float32)

    def dma(*dims):
        return pltpu.SemaphoreType.DMA(dims)

    total = n_ffn + 3
    rows16 = -(-6 // SUBLANES) * SUBLANES
    return pl.pallas_call(
        functools.partial(backward_body, n_dp, pieces),
        out_shape=[
            out(size, width), out(rows16, width), out(dr, head), out(dr, head), out(2, dr, head),
            out(n_ffn, dr, columns),
        ],
        in_specs=[vmem] * 24 + [pl.BlockSpec(memory_space=pl.ANY)],
        out_specs=[vmem] * 6,
        scratch_shapes=[
            full(size, width), low(size, width), low(*blocked, width), low(*blocked, width),
            low(2, size, width), low(size, width), low(*blocked, head),
            full(n_tensor * size, head), full(n_tensor * size, head),
            low(*blocked, head), low(*blocked, head), low(*blocked, head), full(width, head),
            low(n_dp, dr, head), low(n_dp, dr, head), low(2, n_dp, dr, head), low(n_dp, dr, head),
            low(n_ffn, 4, dr, half_width),
            low(4, n_rest - 1, dr, head), low(4, n_rest - 1, dr, head), low(4, n_rest - 1, dr, head),
            low(n_ffn, 4, n_rest - 1, dr, half_width),
            low(3, dr, head), low(3, dr, head), low(3, dr, head), low(n_ffn, 3, dr, half_width),
            low(2, dr, head), full(rows16, width), low(n_tensor, rows16, width),
            low(n_rest, rows16, width), low(4, rows16, width),
            dma(n_ffn, 4), dma(total, 4, n_rest), dma(total, 4, n_rest), dma(total, 4), dma(total, 4),
            dma(3), dma(3), dma(count), dma(count), dma(count + 1), dma(count + 1),
            dma(2), dma(2), dma(count), dma(count),
            dma(3), dma(3), dma(n_rest), dma(n_rest), dma(4), dma(4),
        ],
        compiler_params=pltpu.CompilerParams(
            collective_id=ident, has_side_effects=True, vmem_limit_bytes=60 * MIB
        ),
        name="backward",
    )(
        hidden, cot, back_rows, h_rows, u_rows, term_out, gains, head_gains, wq, wk, wv, wo,
        cosine.reshape(*blocked, -1), sine.reshape(*blocked, -1),
        seg_ids.reshape(*blocked, 1), seg_ids.reshape(1, -1),
        a_all, q_raw, k_raw, q_rot, k_rot, v_all, lse, ctx, ffn,
    )


class Spread:
    def __init__(self, at, source, place, own_sem, zs, zr, rs, rr):
        self.at, self.source, self.place = at, source, place
        self.own_sem, self.zs, self.zr, self.rs, self.rr = own_sem, zs, zr, rs, rr

    def along(self, c, k):
        at = self.at
        return send_to(
            at.line_at[k], self.source(c, k), self.place(c, at.dp), self.zs.at[c, k], self.zr.at[c, k]
        )

    def across(self, c, k, r):
        at = self.at
        spot = self.place(c, at.line_dp[k])
        source = self.source(c, 0) if k == 0 else spot
        return send_to(at.rest_at[r], source, spot, self.rs.at[c, k, r], self.rr.at[c, k, r])

    def own(self, c):
        return pltpu.make_async_copy(
            self.source(c, 0), self.place(c, self.at.dp), self.own_sem.at[c]
        )

    def launch(self, c):
        inner = (self.at.line + 1) // 2 == 1

        @pl.when(inner)
        def _():
            for k in (3, 1, 2):
                self.along(c, k).start()

        @pl.when(jnp.logical_not(inner))
        def _():
            for k in (1, 2, 3):
                self.along(c, k).start()

        for r in range(1, self.at.n_rest):
            self.across(c, 0, r).start()
        self.own(c).start()

    def forward(self, c):
        for k in (1, 3, 2):
            self.along(c, k).wait_recv()
            for r in range(1, self.at.n_rest):
                self.across(c, k, r).start()

    def arrived(self, c):
        self.own(c).wait()
        for k in range(4):
            for r in range(1, self.at.n_rest):
                self.across(c, k, r).wait_recv()

    def finish(self, c):
        for k in range(4):
            for r in range(1, self.at.n_rest):
                self.across(c, k, r).wait_send()
            if k:
                self.along(c, k).wait_send()


class Scatter8:
    def __init__(self, at, pieces, parts, held, come, last, ms, mr, fs, fr, ls, lr):
        self.at, self.pieces, self.parts, self.held = at, pieces, parts, held
        self.come, self.last = come, last
        self.ms, self.mr, self.fs, self.fr, self.ls, self.lr = ms, mr, fs, fr, ls, lr
        half, other = at.half, 1 - at.half
        self.z = (half, half, other, other)
        self.x = (at.x, 1 - at.x, at.x, 1 - at.x)
        self.mine_t = (at.t, at.t_side, at.t, at.t_side)
        self.mate_t = (at.t_mate, at.t_side_mate, at.t_mate, at.t_side_mate)

    def near(self, k):
        return send_to(
            self.at.mate, self.parts.at[self.z[k], self.mate_t[k]], self.held.at[k],
            self.ms.at[k], self.mr.at[k],
        )

    def first(self, j, p):
        rows = pl.ds(*self.pieces[p])
        where, blocks = (self.at.side, (1, 3)) if p % 2 == 0 else (self.at.pair, (2, 3))
        return send_to(
            where, self.held.at[blocks[j], rows], self.come.at[j, rows],
            self.fs.at[j, p], self.fr.at[j, p],
        )

    def second(self, p):
        rows = pl.ds(*self.pieces[p])
        where, block = (self.at.pair, 2) if p % 2 == 0 else (self.at.side, 1)
        return send_to(
            where, self.held.at[block, rows], self.last.at[rows], self.ls.at[p], self.lr.at[p]
        )

    def combine(self, k):
        self.near(k).wait_recv()
        for p, piece in enumerate(self.pieces):
            rows = pl.ds(*piece)
            self.held[k, rows] = add_up(
                self.parts[self.z[k], self.mine_t[k], rows], self.held[k, rows]
            ).astype(jnp.bfloat16)
            if k == 3:
                self.first(1, p).start()
            elif k == 1 and p % 2 == 0 or k == 2 and p % 2 == 1:
                self.first(0, p).start()

    def relay(self):
        for p, piece in enumerate(self.pieces):
            rows = pl.ds(*piece)
            keep = 2 if p % 2 == 0 else 1
            self.first(1, p).wait_recv()
            self.held[keep, rows] = add_up(self.held[keep, rows], self.come[1, rows]).astype(
                jnp.bfloat16
            )
            self.second(p).start()

    def result(self, p):
        rows = pl.ds(*self.pieces[p])
        self.first(0, p).wait_recv()
        self.second(p).wait_recv()
        return add_up(self.held[0, rows], self.come[0, rows]) + self.last[rows].astype(jnp.float32)

    def finish(self):
        for k in range(4):
            self.near(k).wait_send()
        for p in range(len(self.pieces)):
            self.first(0, p).wait_send()
            self.first(1, p).wait_send()
            self.second(p).wait_send()


GAINS, KV, WQ, WO, GATE, UP, DOWN = range(7)


def layer_body(n_dp, pieces, names, *refs):
    s = types.SimpleNamespace(**dict(zip(names, refs, strict=True)))
    hidden, cot, ffn = s.hidden, s.cot, s.ffn
    cosine, sine, seg_col = s.cosine, s.sine, s.seg_col
    at = Spot(n_dp)
    others = [at.mate, at.side, {"tensor": at.t_side_mate}]
    meet(others + at.line_at[1:] + at.rest_at[1:])
    halves = (at.half, 1 - at.half, at.half, 1 - at.half)
    size, width = hidden.shape
    dr, wide = ffn.shape[2:]
    n_tensor, _, head = s.q_raw.shape
    factor = HD ** (-0.5)
    a_all, q_raw, k_raw, q_rot, k_rot = (s.a_all, s.q_raw, s.k_raw, s.q_rot, s.k_rot)
    v_all, lse, ctx, u_rows, h_rows = (s.v_all, s.lse, s.ctx, s.u_rows, s.h_rows)
    kv_all, wq, wo, ffn_all = s.kv_all, s.wq_all, s.wo_all, s.ffn_all

    def rows_of(dp):
        return pl.ds(pl.multiple_of(dp * dr, SUBLANES), dr)

    def source(c, k):
        if c == KV:
            return s.kv.at[at.core]
        if c < GATE:
            return {GAINS: s.gains, WQ: s.wq, WO: s.wo}[c]
        return ffn.at[halves[k], c - GATE]

    def place(c, dp):
        if c == GAINS:
            return s.gains_all.at[dp]
        if c == KV:
            return kv_all.at[at.core, rows_of(dp)]
        if c < GATE:
            return (wq if c == WQ else wo).at[rows_of(dp)]
        return ffn_all.at[c - GATE, rows_of(dp)]

    load = Spread(at, source, place, s.own_sem, s.lzs, s.lzr, s.lrs, s.lrr)
    gain_refs = [s.in_gain, s.attn_gain, s.ffn_gain, s.out_gain, s.query_gain, s.key_gain]
    packed = s.packed
    packed[...] = jnp.zeros_like(packed)
    for i, ref in enumerate(gain_refs):
        packed[i : i + 1, : ref.shape[1]] = ref[...].astype(jnp.float32)
    s.gains[...] = packed[...].astype(jnp.bfloat16)
    for c in (GAINS, KV, WQ, WO, GATE):
        load.launch(c)
    seg_row = s.seg_row[...].astype(jnp.float32)
    pos_row = s.pos_row[...].astype(jnp.float32)
    for t in range(n_tensor):
        shape = (size, seg_row.shape[1])
        row = lax.broadcasted_iota(jnp.int32, shape, 0) + t * size
        here = row == lax.broadcasted_iota(jnp.int32, shape, 1)
        seg_col[t] = jnp.sum(jnp.where(here, seg_row, 0.0), axis=1, keepdims=True)
        column = jnp.sum(jnp.where(here, pos_row, 0.0), axis=1, keepdims=True)
        angles = column * s.frequency[...]
        cosine[t] = jnp.cos(angles)
        sine[t] = jnp.sin(angles)

    load.forward(GAINS)
    load.arrived(GAINS)
    gains, head_gains = s.wide_gains, s.head_gains
    g_width, g_head = width // n_dp, head // n_dp
    for i in range(n_dp):
        block = s.gains_all[i].astype(jnp.float32)
        gains[:, i * g_width : (i + 1) * g_width] = block[:, :g_width]
        head_gains[:, i * g_head : (i + 1) * g_head] = block[:, :g_head]

    def gain(row):
        return gains[row : row + 1, :]

    q_gain, k_gain = head_gains[4:5, :], head_gains[5:6, :]

    def column_sum(values):
        return jnp.sum(values, axis=0, keepdims=True)

    bring = Gather4(at, pieces, s.a_own, a_all, s.g1xs, s.g1xr, s.g1ms, s.g1mr)
    for piece in pieces:
        rows = pl.ds(*piece)
        s.a_own[rows] = apply_norm(hidden[rows].astype(jnp.float32), gain(0)).astype(jnp.bfloat16)
    bring.start()
    a_all[at.t] = s.a_own[...]
    bring.pass_on()
    load.forward(KV)
    load.forward(WQ)
    load.launch(UP)
    bring.near_own().wait_recv()
    bring.all_here()
    load.arrived(KV)
    share = send_to(at.mate, kv_all.at[at.core], kv_all.at[at.core], s.ks.at[3], s.kr.at[3])
    share.start()
    load.forward(WO)

    def project_q(t):
        q = dot(a_all[t], wq[...])
        q_raw[t] = q
        q_rot[t] = turn(apply_norm(q, q_gain), cosine[t], sine[t]).astype(jnp.bfloat16)

    def project_kv(t):
        rows = pl.ds(t * size, size)
        k = dot(a_all[t], kv_all[0])
        k_raw[t] = k
        k_rot[rows] = turn(apply_norm(k, k_gain), cosine[t], sine[t]).astype(jnp.bfloat16)
        v_all[rows] = dot(a_all[t], kv_all[1]).astype(jnp.bfloat16)

    share.wait()
    for t in range(n_tensor):
        project_kv(t)
    load.arrived(WQ)
    for t in range(n_tensor):
        project_q(t)
    load.arrived(WO)

    def allowed_pairs(t, shape):
        row = lax.broadcasted_iota(jnp.int32, shape, 0) + t * size
        behind = row - lax.broadcasted_iota(jnp.int32, shape, 1)
        return (seg_col[t] == seg_row) & (behind >= 0) & (behind < WINDOW)

    parts8 = s.parts8
    parts4 = parts8.at[0]

    def attend(t):
        scores = contract_cols(q_rot[t], k_rot[...]) * factor
        weights = jnp.where(allowed_pairs(t, scores.shape), jnp.exp(scores), 0.0)
        total = jnp.sum(weights, axis=-1, keepdims=True)
        lse[t] = jnp.log(total)
        mixed = dot((weights / total).astype(jnp.bfloat16), v_all[...]).astype(jnp.bfloat16)
        ctx[t] = mixed
        parts4[t] = contract_cols(mixed, wo[...]).astype(jnp.bfloat16)

    back = Scatter4(
        at, pieces, parts4, s.held4, s.come4, s.s1ms, s.s1mr, s.s1fs, s.s1fr
    )
    attend(at.t_side_mate)
    back.near(1).start()
    attend(at.t_side)
    back.send_side()
    attend(at.t_mate)
    back.near(0).start()
    attend(at.t)
    load.launch(DOWN)
    load.forward(GATE)
    back.result(u_rows)
    spread = Gather8(
        at, pieces, s.c_own, s.c_all,
        s.x1s, s.x1r, s.z1s, s.z1r, s.d1s, s.d1r, s.m1s, s.m1r,
    )
    for p, piece in enumerate(pieces):
        rows = pl.ds(*piece)
        total = hidden[rows].astype(jnp.float32) + apply_norm(u_rows[rows], gain(1))
        h_rows[rows] = total
        s.c_own[rows] = apply_norm(total, gain(2)).astype(jnp.bfloat16)
        spread.start(p)
    c_all = s.c_all
    c_all[at.half, at.t] = s.c_own[...]
    spread.pass_x()
    load.forward(UP)
    spread.pass_z()
    spread.pass_last()
    for k in range(4):
        spread.here(k)
    back.finish()
    bring.finish()
    load.arrived(GATE)
    load.arrived(UP)
    for c in (GAINS, KV, WQ, WO):
        load.finish(c)
    spread.finish()

    fm, fa, fb = s.fm, s.fa, s.fb
    double = 2 * size
    cuts = [(0, 4 * LANES), (4 * LANES, wide)] if wide > 4 * LANES else [(0, wide)]

    def hidden_units(j, carry):
        z = j // 2
        x = j - 2 * z
        rows = pl.ds(pl.multiple_of(j * double, SUBLANES), double)
        block = c_all[z, pl.ds(2 * x, 2)].reshape(double, width)
        for low, high in cuts:
            g = dot(block, ffn_all[0, :, low:high])
            r = dot(block, ffn_all[1, :, low:high])
            square = g * g
            bend = jnp.tanh(GELU_SCALE * g * (1.0 + GELU_CUBE * square))
            rise = 0.5 * (1.0 + bend)
            value = g * rise
            slope = rise + 0.5 * g * (1.0 - bend * bend) * (
                GELU_SCALE * (1.0 + 3.0 * GELU_CUBE * square)
            )
            fm[rows, low:high] = (value * r).astype(jnp.bfloat16)
            fa[rows, low:high] = (r * slope).astype(jnp.bfloat16)
            fb[rows, low:high] = value.astype(jnp.bfloat16)
        return carry

    lax.fori_loop(0, 4, hidden_units, 0)
    load.forward(DOWN)
    load.arrived(DOWN)

    held8, come8, last8 = s.held8, s.come8, s.last8
    order = (3, 1, 2, 0)

    def block_rows(scatter, k):
        first = (2 * scatter.z[k] + scatter.x[k]) * double
        return pl.ds(pl.multiple_of(first, SUBLANES), double)

    def sum8(scatter, part):
        before = None
        for k in order:
            value = part(block_rows(scatter, k)).astype(jnp.bfloat16)
            parts8[scatter.z[k], pl.ds(2 * scatter.x[k], 2)] = value.reshape(2, size, width)
            scatter.near(k).start()
            if before is not None:
                scatter.combine(before)
            before = k
        scatter.combine(before)

    first = Scatter8(
        at, pieces, parts8, held8, come8, last8,
        s.e1ms, s.e1mr, s.e1fs, s.e1fr, s.e1ls, s.e1lr,
    )
    sum8(first, lambda rows: contract_cols(fm[rows], ffn_all[2]))
    first.relay()
    df_own, df_all = s.df_own, s.df_all
    spread = Gather8(
        at, pieces, df_own, df_all,
        s.x2s, s.x2r, s.z2s, s.z2r, s.d2s, s.d2r, s.m2s, s.m2r,
    )
    terms = s.terms
    terms[...] = jnp.zeros_like(terms)
    sum_out = jnp.zeros((1, width), jnp.float32)
    for p, piece in enumerate(pieces):
        rows = pl.ds(*piece)
        down = first.result(p)
        s.out_rows[rows] = (h_rows[rows] + apply_norm(down, gain(3))).astype(jnp.bfloat16)
        grad, term = norm_back(down, gain(3), cot[rows].astype(jnp.float32))
        sum_out += column_sum(term)
        df_own[rows] = grad.astype(jnp.bfloat16)
        spread.start(p)
    terms[3:4, :] = sum_out
    df_all[at.half, at.t] = df_own[...]
    first.finish()
    load.finish(GATE)
    load.finish(UP)
    load.finish(DOWN)

    def units_back(k):
        rows = block_rows(first, k)
        block = df_all[first.z[k], pl.ds(2 * first.x[k], 2)].reshape(double, width)
        for low, high in cuts:
            dm = dot(block, ffn_all[2, :, low:high])
            fa[rows, low:high] = (dm * fa[rows, low:high].astype(jnp.float32)).astype(jnp.bfloat16)
            fb[rows, low:high] = (dm * fb[rows, low:high].astype(jnp.float32)).astype(jnp.bfloat16)

    spread.here(0)
    units_back(0)
    spread.pass_on()
    spread.here(1)
    units_back(1)
    spread.here(2)
    units_back(2)
    spread.pass_last()
    spread.here(3)

    dwd = s.dwd
    tile = width // 3 if width % (3 * LANES) == 0 else width

    def ffn_grad(target, left, right):
        def one(i, carry):
            cols = pl.ds(pl.multiple_of(i * tile, LANES), tile)
            block = left[:, :, :, cols].reshape(4 * double, tile)
            value = contract_rows(block, right[...]).astype(jnp.bfloat16)
            target[pl.ds(pl.multiple_of(i * tile, SUBLANES), tile)] = value
            return carry

        lax.fori_loop(0, width // tile, one, 0)

    def flat(ref):
        return lambda dp: ref.at[rows_of(dp)]

    def own_flat(ref):
        return lambda k: ref.at[rows_of(at.line_dp[k])]

    dwg, dwu = fm, ffn_all.at[2]
    wo_part, wq_part, kv_part, kv_held = (s.wo_part, s.wq_part, s.kv_part, s.kv_held)
    ffn_in, ffn_far = s.ffn_in, s.ffn_far
    moved = (dwd, dwg, dwu, wo_part, wq_part, kv_held)
    n_ffn = 3
    c_wo, c_wq, c_kv = 3, 4, 5
    sums = Sums(
        at, [flat(ref) for ref in moved], [own_flat(ref) for ref in moved],
        [ffn_in.at[c] for c in range(n_ffn)] + [s.wo_in, s.wq_in, s.kv_in],
        [ffn_far.at[c] for c in range(n_ffn)] + [s.wo_far, s.wq_far, s.kv_far],
        s.rs, s.rr, s.zs, s.zr,
    )
    steps = [(c, k) for c in range(n_ffn) for k in sums.turns]

    def pump(count):
        for _ in range(count):
            if steps:
                sums.add(*steps.pop(0))

    ffn_grad(dwd, df_all, fm)
    sums.start(0)
    units_back(3)
    second = Scatter8(
        at, pieces, parts8, held8, come8, last8,
        s.e2ms, s.e2mr, s.e2fs, s.e2fr, s.e2ls, s.e2lr,
    )
    sum8(
        second,
        lambda rows: contract_cols(fa[rows], ffn_all[0]) + contract_cols(fb[rows], ffn_all[1]),
    )
    ffn_grad(dwg, c_all, fa)
    sums.start(1)
    second.relay()
    pump(2)
    ffn_grad(dwu, c_all, fb)
    sums.start(2)
    pump(1)
    spread.finish()

    dh, du_own, du_all = s.dh, s.du_own, s.du_all
    bring = Gather4(at, pieces, du_own, du_all, s.g2xs, s.g2xr, s.g2ms, s.g2mr)
    sum_ffn = jnp.zeros((1, width), jnp.float32)
    sum_attn = jnp.zeros((1, width), jnp.float32)
    for p, piece in enumerate(pieces):
        rows = pl.ds(*piece)
        grad_norm, term = norm_back(h_rows[rows], gain(2), second.result(p))
        sum_ffn += column_sum(term)
        total = cot[rows].astype(jnp.float32) + grad_norm
        dh[rows] = total
        grad_u, term = norm_back(u_rows[rows], gain(1), total)
        sum_attn += column_sum(term)
        du_own[rows] = grad_u.astype(jnp.bfloat16)
        bring.over_x(p).start()
    terms[1:2, :] = sum_attn
    terms[2:3, :] = sum_ffn
    bring.near_own().start()
    du_all[at.t] = du_own[...]
    second.finish()
    dctx = s.dctx

    def back_ctx(t):
        dctx[t] = dot(du_all[t], wo[...]).astype(jnp.bfloat16)

    back_ctx(at.t)
    bring.near_own().wait_recv()
    back_ctx(at.t_mate)
    bring.pass_on()
    pump(2)
    back_ctx(at.t_side)
    bring.all_here()
    back_ctx(at.t_side_mate)

    def weight_grad(target, left, right):
        value = contract_rows(
            left[...].reshape(n_tensor * size, width), right[...].reshape(n_tensor * size, head)
        )
        target[...] = value.astype(jnp.bfloat16)

    weight_grad(wo_part, du_all, ctx)
    sums.start(c_wo)
    dq_low, dk_low, dv_low, dv, dk = (s.dq_low, s.dk_low, s.dv_low, s.dv, s.dk)

    def attend_back(t):
        scores = contract_cols(q_rot[t], k_rot[...]) * factor
        probs = jnp.where(allowed_pairs(t, scores.shape), jnp.exp(scores - lse[t]), 0.0)
        grad_probs = contract_cols(dctx[t], v_all[...])
        delta = jnp.sum(probs * grad_probs, axis=-1, keepdims=True)
        grad_scores = (probs * (grad_probs - delta) * factor).astype(jnp.bfloat16)
        grad_q = dot(grad_scores, k_rot[...])
        low, term = norm_back(q_raw[t], q_gain, turn(grad_q, cosine[t], -sine[t]))
        dq_low[t] = low.astype(jnp.bfloat16)
        return (
            contract_rows(probs.astype(jnp.bfloat16), dctx[t]),
            contract_rows(grad_scores, q_rot[t]),
            column_sum(term),
        )

    add_v, add_k, sum_q = attend_back(0)
    dv[...] = add_v
    dk[...] = add_k
    for t in range(1, n_tensor):
        add_v, add_k, more = attend_back(t)
        dv[...] += add_v
        dk[...] += add_k
        sum_q += more
    sum_k = jnp.zeros((1, head), jnp.float32)
    for t in range(n_tensor):
        rows = pl.ds(t * size, size)
        low, term = norm_back(k_raw[t], k_gain, turn(dk[rows], cosine[t], -sine[t]))
        dk_low[t] = low.astype(jnp.bfloat16)
        sum_k += column_sum(term)
        dv_low[t] = dv[rows].astype(jnp.bfloat16)
    terms[4:5, :head] = sum_q
    terms[5:6, :head] = sum_k
    pump(1)

    def back_in(t):
        parts4[t] = (
            contract_cols(dq_low[t], wq[...])
            + contract_cols(dk_low[t], kv_all[0])
            + contract_cols(dv_low[t], kv_all[1])
        ).astype(jnp.bfloat16)

    held4, come4 = s.held4, s.come4
    back = Scatter4(at, pieces, parts4, held4, come4, s.s2ms, s.s2mr, s.s2fs, s.s2fr)
    back_in(at.t_side_mate)
    back.near(1).start()
    back_in(at.t_side)
    back.send_side()
    back_in(at.t_mate)
    back.near(0).start()
    back_in(at.t)
    pump(1)
    weight_grad(kv_part.at[0], a_all, dk_low)
    weight_grad(kv_part.at[1], a_all, dv_low)
    ks, kr = s.ks, s.kr
    mate_kv = send_to(at.mate, kv_part.at[1 - at.core], kv_held, ks.at[0], kr.at[0])
    mate_kv.start()
    weight_grad(wq_part, a_all, dq_low)
    sums.start(c_wq)
    mate_kv.wait()

    def pair_up(rows):
        kv_held[rows] = add_up(kv_part[at.core, rows], kv_held[rows]).astype(jnp.bfloat16)

    by_rows(kv_held.shape[0], pair_up)
    sums.start(c_kv)
    pump(1)
    back.near(0).wait_recv()
    sum_in = jnp.zeros((1, width), jnp.float32)
    for p, piece in enumerate(pieces):
        rows = pl.ds(*piece)
        back.far(p).wait_recv()
        total = add_up(parts4[at.t, rows], held4[0, rows]) + come4[rows].astype(jnp.float32)
        grad_norm, term = norm_back(hidden[rows].astype(jnp.float32), gain(0), total)
        s.hidden_out[rows] = dh[rows] + grad_norm
        sum_in += column_sum(term)
    terms[0:1, :] = sum_in

    pool_t, pool_r, pool_z = s.pool_t, s.pool_r, s.pool_z
    pool_t[at.t] = terms[...].astype(jnp.bfloat16)
    over_t = [
        send_to(where, pool_t.at[at.t], pool_t.at[at.t], s.ts.at[j], s.tr.at[j])
        for j, where in enumerate(others)
    ]
    for copy in over_t:
        copy.start()
    pump(1)
    for copy in over_t:
        copy.wait()
    total = pool_t[0].astype(jnp.float32)
    for t in range(1, n_tensor):
        total = total + pool_t[t].astype(jnp.float32)
    pool_r[at.rest] = total.astype(jnp.bfloat16)
    over_r = [
        send_to(at.rest_at[r], pool_r.at[at.rest], pool_r.at[at.rest], s.us.at[r], s.ur.at[r])
        for r in range(1, at.n_rest)
    ]
    for copy in over_r:
        copy.start()
    pump(len(steps))
    for copy in over_r:
        copy.wait()
    total = pool_r[0].astype(jnp.float32)
    for r in range(1, at.n_rest):
        total = total + pool_r[r].astype(jnp.float32)
    pool_z[at.line] = total.astype(jnp.bfloat16)
    over_z = [
        send_to(at.line_at[k], pool_z.at[at.line], pool_z.at[at.line], s.vs.at[k], s.vr.at[k])
        for k in (1, 2, 3)
    ]
    for copy in over_z:
        copy.start()
    for c in (c_wo, c_wq, c_kv):
        for k in sums.turns:
            sums.add(c, k)
    for c in range(n_ffn):
        sums.arrive(c)

        target = (s.gate_out, s.gate_out, s.up_out)[c]

        def put_all(low_first, own=ffn_in.at[c, 0, 0], far=ffn_far.at[c], target=target):
            def put(rows):
                same = add_up(own[rows], far[1, rows])
                cross = add_up(far[0, rows], far[2, rows])
                low, high = (same, cross) if low_first else (cross, same)
                target[rows, :wide] = low
                target[rows, wide:] = high[:, : target.shape[-1] - wide]

            by_rows(own.shape[0], put)

        @pl.when(at.half == 0)
        def _(put_all=put_all):
            put_all(True)

        @pl.when(at.half == 1)
        def _(put_all=put_all):
            put_all(False)

        if c == 0:
            s.down_out[...] = target[...].T

    for copy in over_z:
        copy.wait()
    s.gains_out[...] = add_up(pool_z[0], pool_z[1]) + add_up(pool_z[2], pool_z[3])

    def whole(c):
        sums.arrive(c)
        far = sums.distant[c]
        return add_up(sums.landed[c][0, 0], far[0]) + add_up(far[1], far[2])

    s.wo_out[...] = whole(c_wo).T
    s.wq_out[...] = whole(c_wq)
    kv_pool, kv_out = s.kv_pool, s.kv_out
    kv_pool[0] = whole(c_kv).astype(jnp.bfloat16)
    kv_side = send_to(at.side, kv_pool.at[0], kv_pool.at[1], ks.at[1], kr.at[1])
    kv_side.start()
    kv_side.wait()
    kv_out[at.core] = add_up(kv_pool[0], kv_pool[1])
    give = send_to(at.mate, kv_out.at[at.core], kv_out.at[at.core], ks.at[2], kr.at[2])
    give.start()
    give.wait()
    for c in range(n_ffn + 3):
        sums.finish(c)
    bring.finish()
    back.finish()


def layer(n_dp, hidden, cot, gains, wq, wo, kv, frequency, seg_ids, positions, ffn, columns, ident):
    size, width = hidden.shape
    n_tensor = seg_ids.shape[0] // size
    dr, wide = ffn.shape[2:]
    n_rest = n_dp // 4
    head = wq.shape[1]
    pieces = row_pieces(size, 5)
    count = len(pieces)
    tokens = n_tensor * size
    blocked = (n_tensor, size)
    wider = -(-max(gain.shape[0] for gain in gains) // LANES) * LANES
    gain_block = (SUBLANES, wider)
    assert wq.shape[1] == head

    def out(*dims, kind=jnp.float32):
        return jax.ShapeDtypeStruct(dims, kind)

    def low(*dims):
        return pltpu.VMEM(dims, jnp.bfloat16)

    def full(*dims):
        return pltpu.VMEM(dims, jnp.float32)

    def dma(*dims):
        return pltpu.SemaphoreType.DMA(dims)

    inputs = dict(
        in_gain=gains[0][None], attn_gain=gains[1][None], ffn_gain=gains[2][None],
        out_gain=gains[3][None], query_gain=gains[4][None], key_gain=gains[5][None],
        hidden=hidden, cot=cot, wq=wq, wo=wo, kv=kv, frequency=frequency,
        seg_row=seg_ids[None], pos_row=positions[None], ffn=ffn,
    )
    outputs = dict(
        out_rows=out(size, width, kind=jnp.bfloat16), hidden_out=out(size, width),
        gains_out=out(SUBLANES, width), wq_out=out(dr, head), wo_out=out(head, dr),
        kv_out=out(2, dr, head), gate_out=out(dr, columns), up_out=out(dr, columns),
        down_out=out(columns, dr),
    )
    scratch = dict(
        packed=full(*gain_block), gains=low(*gain_block),
        cosine=full(*blocked, head // 2), sine=full(*blocked, head // 2), seg_col=full(*blocked, 1),
        gains_all=low(n_dp, *gain_block), kv_all=low(2, width, head), wq_all=low(width, head),
        wo_all=low(width, head), ffn_all=low(3, width, wide),
        wide_gains=full(gain_block[0], width), head_gains=full(gain_block[0], head),
        a_own=low(size, width), a_all=low(*blocked, width), q_raw=full(*blocked, head),
        k_raw=full(*blocked, head), q_rot=low(*blocked, head), k_rot=low(tokens, head),
        v_all=low(tokens, head), lse=full(*blocked, 1), ctx=low(*blocked, head),
        u_rows=full(size, width), h_rows=full(size, width),
        held4=low(2, size, width), come4=low(size, width),
        c_own=low(size, width), c_all=low(2, *blocked, width),
        fm=low(2 * tokens, wide), fa=low(2 * tokens, wide), fb=low(2 * tokens, wide),
        parts8=low(2, *blocked, width), held8=low(4, size, width), come8=low(2, size, width),
        last8=low(size, width), df_own=low(size, width), df_all=low(2, *blocked, width),
        dwd=low(width, wide), ffn_in=low(3, 4, n_rest - 1, dr, wide), ffn_far=low(3, 3, dr, wide),
        dh=full(size, width), du_own=low(size, width), du_all=low(*blocked, width),
        dctx=low(*blocked, head), dv=full(tokens, head), dk=full(tokens, head),
        dq_low=low(*blocked, head), dk_low=low(*blocked, head), dv_low=low(*blocked, head),
        wq_part=low(width, head), wo_part=low(width, head), kv_part=low(2, width, head),
        kv_held=low(width, head), wq_in=low(4, n_rest - 1, dr, head),
        wo_in=low(4, n_rest - 1, dr, head), kv_in=low(4, n_rest - 1, dr, head),
        wq_far=low(3, dr, head), wo_far=low(3, dr, head), kv_far=low(3, dr, head),
        kv_pool=low(2, dr, head), terms=full(SUBLANES, width), pool_t=low(n_tensor, SUBLANES, width),
        pool_r=low(n_rest, SUBLANES, width), pool_z=low(4, SUBLANES, width),
        own_sem=dma(7), lzs=dma(7, 4), lzr=dma(7, 4), lrs=dma(7, 4, n_rest), lrr=dma(7, 4, n_rest),
        rs=dma(6, 4, n_rest), rr=dma(6, 4, n_rest), zs=dma(6, 4), zr=dma(6, 4),
        ks=dma(4), kr=dma(4), ts=dma(3), tr=dma(3), us=dma(n_rest), ur=dma(n_rest), vs=dma(4), vr=dma(4),
    )
    for i in "12":
        for n in ("xs", "xr"):
            scratch[f"g{i}{n}"] = dma(count)
        for n in ("ms", "mr"):
            scratch[f"g{i}{n}"] = dma(count + 1)
            scratch[f"s{i}{n}"] = dma(2)
            scratch[f"e{i}{n}"] = dma(4)
            scratch[f"m{i}{n[1]}"] = dma(4, count)
        for n in ("fs", "fr"):
            scratch[f"s{i}{n}"] = dma(count)
            scratch[f"e{i}{n}"] = dma(2, count)
            scratch[f"e{i}l{n[1]}"] = dma(count)
            for a in "xzd":
                scratch[f"{a}{i}{n[1]}"] = dma(count)
    vmem = pl.BlockSpec(memory_space=pltpu.VMEM)
    names = (*inputs, *outputs, *scratch)
    return pl.pallas_call(
        functools.partial(layer_body, n_dp, pieces, names),
        out_shape=list(outputs.values()),
        in_specs=[vmem] * (len(inputs) - 1) + [pl.BlockSpec(memory_space=pl.ANY)],
        out_specs=[vmem] * len(outputs),
        scratch_shapes=list(scratch.values()),
        compiler_params=pltpu.CompilerParams(
            collective_id=ident, has_side_effects=True, vmem_limit_bytes=LAYER_VMEM
        ),
        name="layer",
    )(*inputs.values())


def pack_gains(blocks, width):
    n = blocks[0].shape[0]
    rows = [jnp.pad(block, ((0, 0), (0, width - block.shape[1]))) for block in blocks]
    packed = jnp.stack(rows, axis=1)
    return jnp.pad(packed, ((0, 0), (0, SUBLANES - len(blocks)), (0, 0)))


def stepwise(
    n_dp, hidden, cotangent, gains, w_query, w_output, w_kv, cosine, sine_table, segment_ids, ffn,
    columns,
):
    n_tensor = segment_ids.shape[0] // hidden.shape[0]
    wide = ffn.shape[-1]
    width = -(-max(gain.shape[0] for gain in gains) // LANES) * LANES
    gain_rows = pack_gains([gain[None] for gain in gains], width)[0]
    gains_all, wq_all, wo_all, kv_all = attention_weights(
        n_dp, gain_rows, w_query, w_output, w_kv, 0
    )
    full_in_gain, full_attn_gain, full_ffn_gain, full_out_gain, full_qgain, full_kgain = (
        gains_all[:, row, : gain.shape[0]].reshape(-1).astype(jnp.float32)
        for row, gain in enumerate(gains)
    )
    full_query, full_output = (block.reshape(-1, block.shape[-1]) for block in (wq_all, wo_all))
    full_key, full_value = (kv_all[i].reshape(-1, kv_all.shape[-1]) for i in range(2))
    wide_gains = jnp.stack([full_in_gain, full_attn_gain, full_ffn_gain, full_out_gain])
    head_gains = jnp.stack([full_qgain, full_kgain])
    (
        normed_in, query_raw, key_raw, query_rot, key_rot, value_rows, log_total, context,
        attn_rows, residual, ffn_in, ffn_all,
    ) = forward(
        n_dp,
        hidden,
        wide_gains,
        head_gains,
        full_query, full_key, full_value, full_output, cosine, sine_table, segment_ids, ffn, 1,
    )
    ffn_in = ffn_in.reshape(-1, ffn_in.shape[-1])
    full_gate, full_up, full_down = (ffn_all[i].reshape(-1, wide) for i in range(3))
    gate_pre = jnp.dot(ffn_in, full_gate, preferred_element_type=jnp.float32)
    up_pre = jnp.dot(ffn_in, full_up, preferred_element_type=jnp.float32)
    gelu_values, gelu_back = jax.vjp(gelu_tanh, gate_pre)
    mixed = (gelu_values * up_pre).astype(jnp.bfloat16)
    down_part = contract_cols(mixed, full_down)
    down_rows = scatter8(
        n_dp, down_part.astype(jnp.bfloat16).reshape(2, n_tensor, -1, down_part.shape[-1]), 4
    )
    output = (residual + apply_norm(down_rows, full_out_gain)).astype(jnp.bfloat16)
    cot_f = cotangent.astype(jnp.float32)
    grad_down, term_out = norm_back(down_rows, full_out_gain, cot_f)
    down_all = gather8(n_dp, grad_down.astype(jnp.bfloat16), 5).reshape(-1, grad_down.shape[-1])
    grad_wd = contract_rows(down_all, mixed)
    grad_mixed = jnp.dot(down_all, full_down, preferred_element_type=jnp.float32)
    gate_low = gelu_back(grad_mixed * up_pre)[0].astype(jnp.bfloat16)
    up_low = (grad_mixed * gelu_values).astype(jnp.bfloat16)
    grad_wg = contract_rows(ffn_in, gate_low)
    grad_wu = contract_rows(ffn_in, up_low)
    ffn_part = contract_cols(gate_low, full_gate) + contract_cols(up_low, full_up)
    ffn_back = scatter8(
        n_dp, ffn_part.astype(jnp.bfloat16).reshape(2, n_tensor, -1, ffn_part.shape[-1]), 6
    )
    grad_hidden, gain_sums, own_query, own_output, own_kv, own_ffn_weights = backward(
        n_dp, hidden, cotangent, ffn_back, residual, attn_rows,
        jnp.sum(term_out, axis=0, keepdims=True), wide_gains, head_gains,
        full_query, full_key, full_value, full_output, cosine, sine_table, segment_ids,
        normed_in, query_raw, key_raw, query_rot, key_rot, value_rows, log_total, context,
        jnp.stack(
            [
                grad.astype(jnp.bfloat16).reshape(n_dp, -1, grad.shape[-1])
                for grad in (grad_wd, grad_wg, grad_wu)
            ]
        ),
        columns,
        9,
    )
    return output, grad_hidden, gain_sums, own_query, own_output, own_kv, own_ffn_weights


def local(
    n_dp,
    n_tensor,
    hidden,
    in_gain,
    w_query,
    w_key,
    w_value,
    query_gain,
    key_gain,
    w_output,
    attn_gain,
    ffn_gain,
    w_gate,
    w_up,
    w_down,
    out_gain,
    cotangent,
    segment_ids,
    positions,
):
    gains = (in_gain, attn_gain, ffn_gain, out_gain, query_gain, key_gain)
    columns = w_gate.shape[1]
    wide = -(-columns // (2 * LANES)) * LANES
    ffn = jnp.stack([w_gate, w_up, w_down.T])
    ffn = jnp.pad(ffn, ((0, 0), (0, 0), (0, 2 * wide - columns)))
    ffn = jnp.stack([ffn[:, :, :wide], ffn[:, :, wide:]])
    w_kv = jnp.stack([w_key, w_value])
    if w_query.shape[0] % SUBLANES == 0:
        (
            output, grad_hidden, gain_sums, own_query, own_output, own_kv, own_gate, own_up, own_down,
        ) = layer(
            n_dp, hidden, cotangent, gains, w_query, w_output.T, w_kv, rotary_frequency(HD)[None],
            segment_ids, positions, ffn, columns, 0,
        )
    else:
        cosine, sine_table = rotary_tables(positions, HD)
        output, grad_hidden, gain_sums, own_query, own_output, own_kv, own_ffn_weights = stepwise(
            n_dp, hidden, cotangent, gains, w_query, w_output.T, w_kv, cosine, sine_table,
            segment_ids, ffn, columns,
        )
        own_output = own_output.T
        own_gate, own_up, own_down = own_ffn_weights[1], own_ffn_weights[2], own_ffn_weights[0].T
    place = lax.axis_index("dp")
    own_in, own_attn, own_ffn, own_out, own_q, own_k = (
        lax.dynamic_slice(gain_sums[row], (place * gain.shape[0],), gain.shape)
        for row, gain in enumerate(gains)
    )
    return (
        output,
        grad_hidden,
        own_in,
        own_query,
        own_kv[0],
        own_kv[1],
        own_q,
        own_k,
        own_output,
        own_attn,
        own_ffn,
        own_gate,
        own_up,
        own_down,
        own_out,
    )


def solution(mesh):
    placed = (
        P(("dp", "tensor"), None),
        P("dp"),
        P("dp", "tensor"),
        P("dp", None),
        P("dp", None),
        P("dp"),
        P("dp"),
        P("tensor", "dp"),
        P("dp"),
        P("dp"),
        P("dp", "tensor"),
        P("dp", "tensor"),
        P("tensor", "dp"),
        P("dp"),
        P(("dp", "tensor"), None),
        P("dp"),
        P("dp"),
    )
    return jax.shard_map(
        functools.partial(local, mesh.shape["dp"], mesh.shape["tensor"]),
        mesh=mesh,
        in_specs=placed,
        out_specs=(
            P(("dp", "tensor"), None),
            P(("dp", "tensor"), None),
            P("dp"),
            P("dp", "tensor"),
            P("dp", None),
            P("dp", None),
            P("dp"),
            P("dp"),
            P("tensor", "dp"),
            P("dp"),
            P("dp"),
            P("dp", "tensor"),
            P("dp", "tensor"),
            P("tensor", "dp"),
            P("dp"),
        ),
        check_vma=False,
    )
```

```python
import functools
import math
import types

import jax
import jax.numpy as jnp
from jax import lax
from jax.experimental import pallas as pl
from jax.experimental.pallas import tpu as pltpu
from jax.sharding import PartitionSpec as P

HD = 256
WINDOW = 512


EPSILON = 1e-06
ROPE_BASE = 10000.0


def rms_scale(values):
    return lax.rsqrt(jnp.mean(values * values, axis=-1, keepdims=True) + EPSILON)


def apply_norm(values, gain_vec):
    return values * rms_scale(values) * gain_vec.astype(jnp.float32)


def norm_back(values, gain_vec, upstream):
    factor = rms_scale(values)
    unit_rows = values * factor
    scaled = upstream * gain_vec.astype(jnp.float32)
    grad_values = factor * (
        scaled - unit_rows * jnp.mean(scaled * unit_rows, axis=-1, keepdims=True)
    )
    return (grad_values, upstream * unit_rows)


def rotary_frequency(width):
    steps_half = jnp.arange(width // 2, dtype=jnp.float32)
    return ROPE_BASE ** (-2.0 * steps_half / width)


def rotary_tables(token_pos, width):
    angles = token_pos.astype(jnp.float32)[:, None] * rotary_frequency(width)[None, :]
    return (jnp.cos(angles), jnp.sin(angles))


def gelu_tanh(values):
    return jax.nn.gelu(values, approximate=True)


def contract_rows(left, right):
    return lax.dot_general(
        left, right, (((0,), (0,)), ((), ())), preferred_element_type=jnp.float32
    )


def contract_cols(left, right):
    return lax.dot_general(
        left, right, (((1,), (1,)), ((), ())), preferred_element_type=jnp.float32
    )


MESH = pl.DeviceIdType.MESH
LANES = 128
SUBLANES = 16
MIB = 1024 * 1024
LAYER_VMEM = 63 * MIB
GELU_SCALE = (2.0 / math.pi) ** 0.5
GELU_CUBE = 0.044715


def send_to(where, src, dst, send, recv):
    return pltpu.make_async_remote_copy(
        src_ref=src,
        dst_ref=dst,
        send_sem=send,
        recv_sem=recv,
        device_id=where,
        device_id_type=MESH,
    )


def meet(partners):
    barrier = pltpu.get_barrier_semaphore()
    for where in partners:
        pl.semaphore_signal(barrier, inc=1, device_id=where, device_id_type=MESH)
    pl.semaphore_wait(barrier, len(partners))


class Spot:
    def __init__(self, n_dp):
        self.n_rest = n_dp // 4
        self.dp = lax.axis_index("dp")
        self.t = lax.axis_index("tensor")
        self.x = self.t // 2
        self.core = self.t - 2 * self.x
        self.line = self.dp // self.n_rest
        self.rest = self.dp - self.line * self.n_rest
        self.half = self.line % 2
        high = self.line // 2
        self.lines = [
            self.line,
            2 * high + 1 - self.half,
            2 * (1 - high) + self.half,
            2 * (1 - high) + 1 - self.half,
        ]
        self.line_dp = [line * self.n_rest + self.rest for line in self.lines]
        self.line_at = [{"dp": dp} for dp in self.line_dp]
        self.rests = [(self.rest + r) % self.n_rest for r in range(self.n_rest)]
        self.rest_at = [{"dp": self.line * self.n_rest + rest} for rest in self.rests]
        self.from_rest = [
            (self.rest + self.n_rest - r) % self.n_rest for r in range(self.n_rest)
        ]
        self.t_mate = 2 * self.x + 1 - self.core
        self.t_side = 2 * (1 - self.x) + self.core
        self.t_side_mate = 2 * (1 - self.x) + 1 - self.core
        self.mate = {"tensor": self.t_mate}
        self.side = {"tensor": self.t_side}
        self.pair = self.line_at[1]


def row_pieces(rows, wanted):
    cuts = wanted if rows % (wanted * SUBLANES) == 0 else 1
    size = rows // cuts
    return [(cut * size, size) for cut in range(cuts)]


def gather8_body(n_dp, pieces, mine, full, own_sem, xs, xr, zs, zr, ds, dr, ms, mr):
    at = Spot(n_dp)
    meet([at.mate, at.side, at.pair])
    half, other = at.half, 1 - at.half

    def cut(ref, p):
        return ref.at[pl.ds(*pieces[p])]

    def over_x(p):
        return send_to(at.side, cut(mine, p), cut(full.at[half, at.t], p), xs.at[p], xr.at[p])

    def over_z(p):
        return send_to(at.pair, cut(mine, p), cut(full.at[half, at.t], p), zs.at[p], zr.at[p])

    def onward(p):
        if p % 2 == 0:
            block = cut(full.at[half, at.t_side], p)
            return send_to(at.pair, block, block, ds.at[p], dr.at[p])
        block = cut(full.at[other, at.t], p)
        return send_to(at.side, block, block, ds.at[p], dr.at[p])

    def near(j, p):
        place = cut(full.at[(half, half, other, other)[j], (at.t, at.t_side, at.t, at.t_side)[j]], p)
        source = cut(mine, p) if j == 0 else place
        return send_to(at.mate, source, place, ms.at[j, p], mr.at[j, p])

    count = len(pieces)
    for p in range(count):
        over_x(p).start()
        over_z(p).start()
    own = pltpu.make_async_copy(mine, full.at[half, at.t], own_sem)
    own.start()
    for p in range(count):
        near(0, p).start()
    for p in range(count):
        over_x(p).wait_recv()
        if p % 2 == 0:
            onward(p).start()
        near(1, p).start()
        over_z(p).wait_recv()
        if p % 2 == 1:
            onward(p).start()
        near(2, p).start()
    for p in range(count):
        onward(p).wait_recv()
        near(3, p).start()
    own.wait()
    for p in range(count):
        over_x(p).wait_send()
        over_z(p).wait_send()
        onward(p).wait_send()
        for j in range(4):
            near(j, p).wait()


def gather8(n_dp, block, ident):
    pieces = row_pieces(block.shape[0], 10)
    count = len(pieces)
    one = pltpu.SemaphoreType.DMA((count,))
    four = pltpu.SemaphoreType.DMA((4, count))
    return pl.pallas_call(
        functools.partial(gather8_body, n_dp, pieces),
        out_shape=jax.ShapeDtypeStruct((2, 4, *block.shape), block.dtype),
        in_specs=[pl.BlockSpec(memory_space=pltpu.VMEM)],
        out_specs=pl.BlockSpec(memory_space=pl.ANY),
        scratch_shapes=[pltpu.SemaphoreType.DMA, one, one, one, one, one, one, four, four],
        compiler_params=pltpu.CompilerParams(collective_id=ident, has_side_effects=True),
        name=f"gather8_{ident}",
    )(block)


def add_up(left, right):
    return left.astype(jnp.float32) + right.astype(jnp.float32)


def scatter8_body(
    n_dp, pieces, parts, out, held, come, last, ms, mr, fs, fr, ls, lr
):
    at = Spot(n_dp)
    meet([at.mate, at.side, at.pair])
    half, other = at.half, 1 - at.half
    halves = (half, half, other, other)
    mine_t = (at.t, at.t_side, at.t, at.t_side)
    mate_t = (at.t_mate, at.t_side_mate, at.t_mate, at.t_side_mate)
    count = len(pieces)

    def near(k, p):
        rows = pl.ds(*pieces[p])
        return send_to(
            at.mate, parts.at[halves[k], mate_t[k], rows], held.at[k, rows], ms.at[k, p], mr.at[k, p]
        )

    def first(j, p):
        rows = pl.ds(*pieces[p])
        if p % 2 == 0:
            return send_to(at.side, held.at[(1, 3)[j], rows], come.at[j, rows], fs.at[j, p], fr.at[j, p])
        return send_to(at.pair, held.at[(2, 3)[j], rows], come.at[j, rows], fs.at[j, p], fr.at[j, p])

    def second(p):
        rows = pl.ds(*pieces[p])
        if p % 2 == 0:
            return send_to(at.pair, held.at[2, rows], last.at[rows], ls.at[p], lr.at[p])
        return send_to(at.side, held.at[1, rows], last.at[rows], ls.at[p], lr.at[p])

    for p in range(count):
        for k in (3, 1, 2, 0):
            near(k, p).start()
    for p in range(count):
        rows = pl.ds(*pieces[p])
        for k in (3, 1, 2, 0):
            near(k, p).wait_recv()
            held[k, rows] = add_up(parts[halves[k], mine_t[k], rows], held[k, rows]).astype(jnp.bfloat16)
        first(1, p).start()
        first(0, p).start()
    for p in range(count):
        rows = pl.ds(*pieces[p])
        keep = 2 if p % 2 == 0 else 1
        first(1, p).wait_recv()
        held[keep, rows] = add_up(held[keep, rows], come[1, rows]).astype(jnp.bfloat16)
        second(p).start()
        first(0, p).wait_recv()
        out[rows] = add_up(held[0, rows], come[0, rows])
    for p in range(count):
        rows = pl.ds(*pieces[p])
        second(p).wait_recv()
        out[rows] = out[rows] + last[rows].astype(jnp.float32)
    for p in range(count):
        for k in range(4):
            near(k, p).wait_send()
        for j in range(2):
            first(j, p).wait_send()
        second(p).wait_send()


def scatter8(n_dp, parts, ident):
    rows, width = parts.shape[2:]
    pieces = row_pieces(rows, 10)
    count = len(pieces)

    def sems(*shape):
        return pltpu.SemaphoreType.DMA((*shape, count))

    return pl.pallas_call(
        functools.partial(scatter8_body, n_dp, pieces),
        out_shape=jax.ShapeDtypeStruct((rows, width), jnp.float32),
        in_specs=[pl.BlockSpec(memory_space=pltpu.VMEM)],
        out_specs=pl.BlockSpec(memory_space=pltpu.VMEM),
        scratch_shapes=[
            pltpu.VMEM((4, rows, width), jnp.bfloat16),
            pltpu.VMEM((2, rows, width), jnp.bfloat16),
            pltpu.VMEM((rows, width), jnp.bfloat16),
            sems(4), sems(4), sems(2), sems(2), sems(), sems(),
        ],
        compiler_params=pltpu.CompilerParams(
            collective_id=ident, has_side_effects=True, vmem_limit_bytes=40 * MIB
        ),
        name=f"scatter8_{ident}",
    )(parts)


def weights_body(
    n_dp, gains, wq, wo, kv, gains_all, wq_all, wo_all, kv_all, own_sem, zs, zr, rs, rr, ks, kr
):
    at = Spot(n_dp)
    meet([at.mate] + at.line_at[1:] + at.rest_at[1:])

    def source(c):
        return kv.at[at.core] if c == 3 else (gains, wq, wo)[c]

    def place(c, dp):
        return kv_all.at[at.core, dp] if c == 3 else (gains_all, wq_all, wo_all)[c].at[dp]

    def along(c, k):
        return send_to(at.line_at[k], source(c), place(c, at.dp), zs.at[c, k], zr.at[c, k])

    def across(c, k, r):
        spot = place(c, at.line_dp[k])
        return send_to(
            at.rest_at[r], source(c) if k == 0 else spot, spot, rs.at[c, k, r], rr.at[c, k, r]
        )

    order = (0, 3, 1, 2)
    for c in order:
        for k in (1, 2, 3):
            along(c, k).start()
        for r in range(1, at.n_rest):
            across(c, 0, r).start()
    own = [pltpu.make_async_copy(source(c), place(c, at.dp), own_sem.at[c]) for c in order]
    for copy in own:
        copy.start()
    for c in order:
        for k in (1, 2, 3):
            along(c, k).wait_recv()
            for r in range(1, at.n_rest):
                across(c, k, r).start()
    for copy in own:
        copy.wait()
    share = send_to(at.mate, kv_all.at[at.core], kv_all.at[at.core], ks, kr)
    for c in (3, 0, 1, 2):
        for k in range(4):
            for r in range(1, at.n_rest):
                across(c, k, r).wait()
            if k:
                along(c, k).wait_send()
        if c == 3:
            share.start()
    share.wait()


def attention_weights(n_dp, gains, wq, wo, kv, ident):
    line = pltpu.SemaphoreType.DMA((4, 4))
    rest = pltpu.SemaphoreType.DMA((4, 4, n_dp // 4))
    any_space = pl.BlockSpec(memory_space=pl.ANY)

    def shape(*dims):
        return jax.ShapeDtypeStruct(dims, jnp.bfloat16)

    return pl.pallas_call(
        functools.partial(weights_body, n_dp),
        out_shape=[
            shape(n_dp, *gains.shape), shape(n_dp, *wq.shape), shape(n_dp, *wo.shape),
            shape(2, n_dp, *kv.shape[1:]),
        ],
        in_specs=[pl.BlockSpec(memory_space=pltpu.VMEM)] * 4,
        out_specs=[any_space] * 4,
        scratch_shapes=[
            pltpu.SemaphoreType.DMA((4,)), line, line, rest, rest,
            pltpu.SemaphoreType.DMA, pltpu.SemaphoreType.DMA,
        ],
        compiler_params=pltpu.CompilerParams(collective_id=ident, has_side_effects=True),
        name="attention_weights",
    )(gains, wq, wo, kv)


class Background:
    def __init__(self, at, ffn, ffn_all, own_sem, zs, zr, rs, rr):
        self.at, self.ffn, self.ffn_all = at, ffn, ffn_all
        self.own_sem, self.zs, self.zr, self.rs, self.rr = own_sem, zs, zr, rs, rr
        self.halves = (at.half, 1 - at.half, at.half, 1 - at.half)

    def along(self, c, k):
        at = self.at
        return send_to(
            at.line_at[k], self.ffn.at[self.halves[k], c], self.ffn_all.at[c, at.dp],
            self.zs.at[c, k], self.zr.at[c, k],
        )

    def across(self, c, k, r):
        at = self.at
        spot = self.ffn_all.at[c, at.line_dp[k]]
        source = self.ffn.at[at.half, c] if k == 0 else spot
        return send_to(at.rest_at[r], source, spot, self.rs.at[c, k, r], self.rr.at[c, k, r])

    def own(self, c):
        at = self.at
        return pltpu.make_async_copy(
            self.ffn.at[at.half, c], self.ffn_all.at[c, at.dp], self.own_sem.at[c]
        )

    def launch(self, c):
        for k in (2, 3, 1):
            self.along(c, k).start()
        for r in range(1, self.at.n_rest):
            self.across(c, 0, r).start()
        self.own(c).start()

    def forward(self, c, ks=(2, 3, 1)):
        for k in ks:
            self.along(c, k).wait_recv()
            for r in range(1, self.at.n_rest):
                self.across(c, k, r).start()

    def finish(self, c):
        self.own(c).wait()
        for k in range(4):
            for r in range(1, self.at.n_rest):
                self.across(c, k, r).wait()
            if k:
                self.along(c, k).wait_send()


def dot(left, right):
    return jnp.dot(left, right, preferred_element_type=jnp.float32)


def turn(values, cosine, sine_table):
    half_width = values.shape[-1] // 2
    first_half = values[:, :half_width]
    second = values[:, half_width:]
    return jnp.concatenate(
        [first_half * cosine - second * sine_table, second * cosine + first_half * sine_table],
        axis=-1,
    )


class Gather4:
    def __init__(self, at, pieces, mine, full, xs, xr, ms, mr):
        self.at, self.pieces, self.mine, self.full = at, pieces, mine, full
        self.xs, self.xr, self.ms, self.mr = xs, xr, ms, mr

    def over_x(self, p):
        rows, at = pl.ds(*self.pieces[p]), self.at
        return send_to(
            at.side, self.mine.at[rows], self.full.at[at.t, rows], self.xs.at[p], self.xr.at[p]
        )

    def near(self, p):
        rows, at = pl.ds(*self.pieces[p]), self.at
        block = self.full.at[at.t_side, rows]
        return send_to(at.mate, block, block, self.ms.at[p], self.mr.at[p])

    def near_own(self):
        at, p = self.at, len(self.pieces)
        return send_to(at.mate, self.mine, self.full.at[at.t], self.ms.at[p], self.mr.at[p])

    def start(self):
        for p in range(len(self.pieces)):
            self.over_x(p).start()
        self.near_own().start()

    def pass_on(self):
        for p in range(len(self.pieces)):
            self.over_x(p).wait_recv()
            self.near(p).start()

    def all_here(self):
        for p in range(len(self.pieces)):
            self.near(p).wait_recv()

    def finish(self):
        self.near_own().wait_send()
        for p in range(len(self.pieces)):
            self.over_x(p).wait_send()
            self.near(p).wait_send()


class Scatter4:
    def __init__(self, at, pieces, parts, held, come, ms, mr, fs, fr):
        self.at, self.pieces, self.parts, self.held, self.come = at, pieces, parts, held, come
        self.ms, self.mr, self.fs, self.fr = ms, mr, fs, fr
        self.mate_t = (at.t_mate, at.t_side_mate)

    def near(self, k):
        return send_to(
            self.at.mate, self.parts.at[self.mate_t[k]], self.held.at[k], self.ms.at[k], self.mr.at[k]
        )

    def far(self, p):
        rows = pl.ds(*self.pieces[p])
        return send_to(
            self.at.side, self.held.at[1, rows], self.come.at[rows], self.fs.at[p], self.fr.at[p]
        )

    def send_side(self):
        self.near(1).wait_recv()
        for p, piece in enumerate(self.pieces):
            rows = pl.ds(*piece)
            self.held[1, rows] = add_up(self.parts[self.at.t_side, rows], self.held[1, rows]).astype(
                jnp.bfloat16
            )
            self.far(p).start()

    def result(self, out):
        self.near(0).wait_recv()
        for p, piece in enumerate(self.pieces):
            rows = pl.ds(*piece)
            self.far(p).wait_recv()
            out[rows] = add_up(self.parts[self.at.t, rows], self.held[0, rows]) + self.come[
                rows
            ].astype(jnp.float32)

    def finish(self):
        for k in range(2):
            self.near(k).wait_send()
        for p in range(len(self.pieces)):
            self.far(p).wait_send()


class Gather8:
    def __init__(self, at, pieces, mine, full, xs, xr, zs, zr, ds, dr, ms, mr):
        self.at, self.pieces, self.mine, self.full = at, pieces, mine, full
        self.xs, self.xr, self.zs, self.zr = xs, xr, zs, zr
        self.ds, self.dr, self.ms, self.mr = ds, dr, ms, mr

    def spot(self, z, t, p):
        return self.full.at[z, t, pl.ds(*self.pieces[p])]

    def over_x(self, p):
        at = self.at
        return send_to(
            at.side, self.mine.at[pl.ds(*self.pieces[p])], self.spot(at.half, at.t, p),
            self.xs.at[p], self.xr.at[p],
        )

    def over_z(self, p):
        at = self.at
        return send_to(
            at.pair, self.mine.at[pl.ds(*self.pieces[p])], self.spot(at.half, at.t, p),
            self.zs.at[p], self.zr.at[p],
        )

    def onward(self, p):
        at = self.at
        if p % 2 == 0:
            block = self.spot(at.half, at.t_side, p)
            return send_to(at.pair, block, block, self.ds.at[p], self.dr.at[p])
        block = self.spot(1 - at.half, at.t, p)
        return send_to(at.side, block, block, self.ds.at[p], self.dr.at[p])

    def near(self, j, p):
        at = self.at
        z = (at.half, at.half, 1 - at.half, 1 - at.half)[j]
        place = self.spot(z, (at.t, at.t_side, at.t, at.t_side)[j], p)
        source = self.mine.at[pl.ds(*self.pieces[p])] if j == 0 else place
        return send_to(at.mate, source, place, self.ms.at[j, p], self.mr.at[j, p])

    def start(self, p):
        self.over_x(p).start()
        self.over_z(p).start()
        self.near(0, p).start()

    def pass_on(self):
        for p in range(len(self.pieces)):
            self.over_x(p).wait_recv()
            if p % 2 == 0:
                self.onward(p).start()
            self.near(1, p).start()
            self.over_z(p).wait_recv()
            if p % 2 == 1:
                self.onward(p).start()
            self.near(2, p).start()

    def pass_x(self):
        for p in range(len(self.pieces)):
            self.over_x(p).wait_recv()
            if p % 2 == 0:
                self.onward(p).start()
            self.near(1, p).start()

    def pass_z(self):
        for p in range(len(self.pieces)):
            self.over_z(p).wait_recv()
            if p % 2 == 1:
                self.onward(p).start()
            self.near(2, p).start()

    def pass_last(self):
        for p in range(len(self.pieces)):
            self.onward(p).wait_recv()
            self.near(3, p).start()

    def here(self, j):
        for p in range(len(self.pieces)):
            self.near(j, p).wait_recv()

    def finish(self):
        for p in range(len(self.pieces)):
            self.over_x(p).wait_send()
            self.over_z(p).wait_send()
            self.onward(p).wait_send()
            for j in range(4):
                self.near(j, p).wait_send()


def forward_body(
    n_dp, pieces,
    hidden, gains, head_gains, wq, wk, wv, wo, cosine, sine, seg_col, seg_row, ffn,
    a_all, q_raw, k_raw, q_rot, k_rot, v_all, lse, ctx, u_out, h_out, c_all, ffn_all,
    a_own, c_own, parts, held, come,
    own_sem, bzs, bzr, brs, brr, gxs, gxr, gms, gmr, sms, smr, sfs, sfr,
    xs, xr, zs, zr, ds, dr, ms, mr,
):
    at = Spot(n_dp)
    meet([at.mate, at.side] + at.line_at[1:] + at.rest_at[1:])
    load = Background(at, ffn, ffn_all, own_sem, bzs, bzr, brs, brr)
    count = ffn.shape[1]
    size = hidden.shape[0]
    load.launch(0)
    if count > 1:
        load.launch(1)

    def gain(row):
        return gains[row : row + 1, :]

    bring = Gather4(at, pieces, a_own, a_all, gxs, gxr, gms, gmr)
    for piece in pieces:
        rows = pl.ds(*piece)
        a_own[rows] = apply_norm(hidden[rows].astype(jnp.float32), gain(0)).astype(jnp.bfloat16)
    bring.start()
    a_all[at.t] = a_own[...]

    def project(t):
        rows = pl.ds(pl.multiple_of(t * size, SUBLANES), size)
        a = a_all[t]
        q = dot(a, wq[...])
        q_raw[t] = q
        q_rot[t] = turn(apply_norm(q, head_gains[0:1, :]), cosine[t], sine[t]).astype(jnp.bfloat16)
        k = dot(a, wk[...])
        k_raw[t] = k
        k_rot[rows] = turn(apply_norm(k, head_gains[1:2, :]), cosine[t], sine[t]).astype(
            jnp.bfloat16
        )
        v_all[rows] = dot(a, wv[...]).astype(jnp.bfloat16)

    project(at.t)
    bring.near_own().wait_recv()
    project(at.t_mate)
    bring.pass_on()
    project(at.t_side)
    bring.all_here()
    project(at.t_side_mate)

    def attend(t):
        scores = contract_cols(q_rot[t], k_rot[...]) * HD ** (-0.5)
        row = lax.broadcasted_iota(jnp.int32, scores.shape, 0) + t * size
        behind = row - lax.broadcasted_iota(jnp.int32, scores.shape, 1)
        allowed = (seg_col[t] == seg_row[...]) & (behind >= 0) & (behind < WINDOW)
        weights = jnp.where(allowed, jnp.exp(scores), 0.0)
        total = jnp.sum(weights, axis=-1, keepdims=True)
        lse[t] = jnp.log(total)
        mixed = dot((weights / total).astype(jnp.bfloat16), v_all[...]).astype(jnp.bfloat16)
        ctx[t] = mixed
        parts[t] = contract_cols(mixed, wo[...]).astype(jnp.bfloat16)

    back = Scatter4(at, pieces, parts, held, come, sms, smr, sfs, sfr)
    attend(at.t_side_mate)
    back.near(1).start()
    attend(at.t_side)
    back.send_side()
    attend(at.t_mate)
    back.near(0).start()
    attend(at.t)
    load.forward(0)
    back.result(u_out)
    spread = Gather8(at, pieces, c_own, c_all, xs, xr, zs, zr, ds, dr, ms, mr)
    for p, piece in enumerate(pieces):
        rows = pl.ds(*piece)
        total = hidden[rows].astype(jnp.float32) + apply_norm(u_out[rows], gain(1))
        h_out[rows] = total
        c_own[rows] = apply_norm(total, gain(2)).astype(jnp.bfloat16)
        spread.start(p)
    for c in range(2, count):
        load.launch(c)
    c_all[at.half, at.t] = c_own[...]
    if count > 1:
        load.forward(1)
    spread.pass_on()
    spread.pass_last()
    for c in range(2, count):
        load.forward(c)
    for k in range(4):
        spread.here(k)
    bring.finish()
    back.finish()
    spread.finish()
    for c in range(count):
        load.finish(c)


def forward(n_dp, hidden, gains, head_gains, wq, wk, wv, wo, cosine, sine, seg_ids, ffn, ident):
    size, width = hidden.shape
    n_tensor = seg_ids.shape[0] // size
    parts = ffn.shape[1]
    pieces = row_pieces(size, 10)
    count = len(pieces)
    head = wq.shape[1]
    vmem = pl.BlockSpec(memory_space=pltpu.VMEM)
    any_space = pl.BlockSpec(memory_space=pl.ANY)

    def low(*dims):
        return jax.ShapeDtypeStruct(dims, jnp.bfloat16)

    def full(*dims):
        return jax.ShapeDtypeStruct(dims, jnp.float32)

    def dma(*dims):
        return pltpu.SemaphoreType.DMA(dims)

    line, rest = dma(parts, 4), dma(parts, 4, n_dp // 4)
    blocked = (n_tensor, size)
    return pl.pallas_call(
        functools.partial(forward_body, n_dp, pieces),
        out_shape=[
            low(*blocked, width), full(*blocked, head), full(*blocked, wk.shape[1]),
            low(*blocked, head), low(n_tensor * size, wk.shape[1]), low(n_tensor * size, wv.shape[1]),
            full(*blocked, 1), low(*blocked, head), full(size, width), full(size, width),
            low(2, *blocked, width), low(parts, n_dp, *ffn.shape[2:]),
        ],
        in_specs=[vmem] * 11 + [any_space],
        out_specs=[vmem] * 11 + [any_space],
        scratch_shapes=[
            pltpu.VMEM((size, width), jnp.bfloat16), pltpu.VMEM((size, width), jnp.bfloat16),
            pltpu.VMEM((*blocked, width), jnp.bfloat16), pltpu.VMEM((2, size, width), jnp.bfloat16),
            pltpu.VMEM((size, width), jnp.bfloat16),
            dma(parts), line, line, rest, rest,
            dma(count), dma(count), dma(count + 1), dma(count + 1),
            dma(2), dma(2), dma(count), dma(count),
            dma(count), dma(count), dma(count), dma(count), dma(count), dma(count),
            dma(4, count), dma(4, count),
        ],
        compiler_params=pltpu.CompilerParams(
            collective_id=ident, has_side_effects=True, vmem_limit_bytes=56 * MIB
        ),
        name="forward",
    )(
        hidden, gains, head_gains, wq, wk, wv, wo,
        cosine.reshape(*blocked, -1), sine.reshape(*blocked, -1),
        seg_ids.reshape(*blocked, 1), seg_ids.reshape(1, -1), ffn,
    )


def by_rows(rows, body):
    step = SUBLANES if rows % SUBLANES == 0 else rows
    if step == rows:
        body(slice(None))
        return

    def one(i, carry):
        body(pl.ds(pl.multiple_of(i * step, step), step))
        return carry

    lax.fori_loop(0, rows // step, one, 0)


class Sums:
    def __init__(self, at, blocks, owns, landed, distant, rs, rr, zs, zr):
        self.at, self.blocks, self.owns, self.landed, self.distant = at, blocks, owns, landed, distant
        self.rs, self.rr, self.zs, self.zr = rs, rr, zs, zr
        self.turns = (2, 3, 1, 0)

    def across(self, c, k, r):
        at = self.at
        target = at.lines[k] * at.n_rest + at.rests[r]
        return send_to(
            at.rest_at[r], self.blocks[c](target), self.landed[c].at[k, r - 1],
            self.rs.at[c, k, r], self.rr.at[c, k, r],
        )

    def along(self, c, k):
        return send_to(
            self.at.line_at[k], self.landed[c].at[k, 0], self.distant[c].at[k - 1],
            self.zs.at[c, k], self.zr.at[c, k],
        )

    def start(self, c):
        for k in self.turns:
            for r in range(1, self.at.n_rest):
                self.across(c, k, r).start()

    def add(self, c, k):
        at, come = self.at, self.landed[c]
        for r in range(1, at.n_rest):
            self.across(c, k, r).wait_recv()
        own = self.owns[c](k)

        def one(rows):
            total = own[rows].astype(jnp.float32)
            for r in range(1, at.n_rest):
                total = total + come[k, r - 1, rows].astype(jnp.float32)
            come[k, 0, rows] = total.astype(jnp.bfloat16)

        by_rows(come.shape[2], one)
        if k:
            self.along(c, k).start()

    def arrive(self, c):
        for k in (1, 2, 3):
            self.along(c, k).wait_recv()

    def finish(self, c):
        for k in self.turns:
            for r in range(1, self.at.n_rest):
                self.across(c, k, r).wait_send()
            if k:
                self.along(c, k).wait_send()


def backward_body(
    n_dp, pieces,
    hidden, cot, back_rows, h_rows, u_rows, term_out, gains, head_gains, wq, wk, wv, wo,
    cosine, sine, seg_col, seg_row, a_all, q_raw, k_raw, q_rot, k_rot, v_all, lse, ctx, ffn,
    hidden_out, gains_out, wq_out, wo_out, kv_out, ffn_out,
    dh, du_own, du_all, parts, held, come, dctx, dv, dk, dq_low, dk_low, dv_low, wide,
    wq_part, wo_part, kv_part, kv_held, ffn_own, wq_in, wo_in, kv_in, ffn_in,
    wq_far, wo_far, kv_far, ffn_far, kv_pool, terms, pool_t, pool_r, pool_z,
    own_sem, rs, rr, zs, zr, ks, kr, gxs, gxr, gms, gmr, sms, smr, sfs, sfr, ts, tr, us, ur, vs, vr,
):
    at = Spot(n_dp)
    others = [at.mate, at.side, {"tensor": at.t_side_mate}]
    meet(others + at.line_at[1:] + at.rest_at[1:])
    n_ffn = ffn.shape[0]
    size = hidden.shape[0]
    c_wo, c_wq, c_kv = n_ffn, n_ffn + 1, n_ffn + 2
    factor = HD ** (-0.5)

    def of_ffn(c):
        return lambda dp: ffn.at[c, dp]

    def own_ffn(c):
        return lambda k: ffn_own.at[c, k]

    def of(ref):
        return lambda dp: ref.at[dp]

    def own(ref):
        return lambda k: ref.at[at.line_dp[k]]

    sums = Sums(
        at,
        [of_ffn(c) for c in range(n_ffn)] + [of(wo_part), of(wq_part), of(kv_held)],
        [own_ffn(c) for c in range(n_ffn)] + [own(wo_part), own(wq_part), own(kv_held)],
        [ffn_in.at[c] for c in range(n_ffn)] + [wo_in, wq_in, kv_in],
        [ffn_far.at[c] for c in range(n_ffn)] + [wo_far, wq_far, kv_far],
        rs, rr, zs, zr,
    )
    for c in range(n_ffn):
        sums.start(c)
    keep = [
        pltpu.make_async_copy(ffn.at[c, at.line_dp[k]], ffn_own.at[c, k], own_sem.at[c, k])
        for c in range(n_ffn)
        for k in range(4)
    ]
    for copy in keep:
        copy.start()
    steps = [(c, k) for c in range(n_ffn) for k in sums.turns]

    def pump(count):
        for _ in range(count):
            if steps:
                sums.add(*steps.pop(0))

    def gain(row):
        return gains[row : row + 1, :]

    def column_sum(values):
        return jnp.sum(values, axis=0, keepdims=True)

    width = hidden.shape[1]
    head = q_raw.shape[-1]
    terms[...] = jnp.zeros_like(terms)
    terms[3:4, :] = term_out[...]
    bring = Gather4(at, pieces, du_own, du_all, gxs, gxr, gms, gmr)
    sum_ffn = jnp.zeros((1, width), jnp.float32)
    sum_attn = jnp.zeros((1, width), jnp.float32)
    for p, piece in enumerate(pieces):
        rows = pl.ds(*piece)
        grad_norm, term = norm_back(h_rows[rows], gain(2), back_rows[rows])
        sum_ffn += column_sum(term)
        total = cot[rows].astype(jnp.float32) + grad_norm
        dh[rows] = total
        grad_u, term = norm_back(u_rows[rows], gain(1), total)
        sum_attn += column_sum(term)
        du_own[rows] = grad_u.astype(jnp.bfloat16)
        bring.over_x(p).start()
    terms[1:2, :] = sum_attn
    terms[2:3, :] = sum_ffn
    bring.near_own().start()
    du_all[at.t] = du_own[...]
    for copy in keep:
        copy.wait()

    def back_ctx(t):
        dctx[t] = dot(du_all[t], wo[...]).astype(jnp.bfloat16)

    back_ctx(at.t)
    bring.near_own().wait_recv()
    back_ctx(at.t_mate)
    bring.pass_on()
    back_ctx(at.t_side)
    bring.all_here()
    back_ctx(at.t_side_mate)
    n_tensor = du_all.shape[0]
    dr = wo_part.shape[1]

    def weight_grad(out, left, right):
        total = contract_rows(left[0], right[0])
        for t in range(1, n_tensor):
            total = total + contract_rows(left[t], right[t])
        wide[...] = total
        for i in range(n_dp):
            out[i] = wide[i * dr : (i + 1) * dr].astype(jnp.bfloat16)

    weight_grad(wo_part, du_all, ctx)
    sums.start(c_wo)
    pump(3)

    def attend_back(t):
        scores = contract_cols(q_rot[t], k_rot[...]) * factor
        row = lax.broadcasted_iota(jnp.int32, scores.shape, 0) + t * size
        behind = row - lax.broadcasted_iota(jnp.int32, scores.shape, 1)
        allowed = (seg_col[t] == seg_row[...]) & (behind >= 0) & (behind < WINDOW)
        probs = jnp.where(allowed, jnp.exp(scores - lse[t]), 0.0)
        grad_probs = contract_cols(dctx[t], v_all[...])
        delta = jnp.sum(probs * grad_probs, axis=-1, keepdims=True)
        grad_scores = (probs * (grad_probs - delta) * factor).astype(jnp.bfloat16)
        grad_q = dot(grad_scores, k_rot[...])
        low, term = norm_back(q_raw[t], head_gains[0:1, :], turn(grad_q, cosine[t], -sine[t]))
        dq_low[t] = low.astype(jnp.bfloat16)
        return (
            contract_rows(probs.astype(jnp.bfloat16), dctx[t]),
            contract_rows(grad_scores, q_rot[t]),
            column_sum(term),
        )

    add_v, add_k, sum_q = attend_back(0)
    dv[...] = add_v
    dk[...] = add_k
    for t in range(1, n_tensor):
        add_v, add_k, more = attend_back(t)
        dv[...] += add_v
        dk[...] += add_k
        sum_q += more
    sum_k = jnp.zeros((1, head), jnp.float32)
    for t in range(n_tensor):
        rows = pl.ds(t * size, size)
        low, term = norm_back(k_raw[t], head_gains[1:2, :], turn(dk[rows], cosine[t], -sine[t]))
        dk_low[t] = low.astype(jnp.bfloat16)
        sum_k += column_sum(term)
        dv_low[t] = dv[rows].astype(jnp.bfloat16)
    terms[4:5, :head] = sum_q
    terms[5:6, :head] = sum_k
    pump(2)

    def back_in(t):
        parts[t] = (
            contract_cols(dq_low[t], wq[...])
            + contract_cols(dk_low[t], wk[...])
            + contract_cols(dv_low[t], wv[...])
        ).astype(jnp.bfloat16)

    back = Scatter4(at, pieces, parts, held, come, sms, smr, sfs, sfr)
    back_in(at.t_side_mate)
    back.near(1).start()
    back_in(at.t_side)
    back.send_side()
    back_in(at.t_mate)
    back.near(0).start()
    back_in(at.t)
    weight_grad(kv_part.at[0], a_all, dk_low)
    weight_grad(kv_part.at[1], a_all, dv_low)
    mate_kv = send_to(at.mate, kv_part.at[1 - at.core], kv_held, ks.at[0], kr.at[0])
    mate_kv.start()
    weight_grad(wq_part, a_all, dq_low)
    sums.start(c_wq)
    mate_kv.wait()

    def pair_up(dp, carry):
        def add(rows):
            kv_held[dp, rows] = add_up(kv_part[at.core, dp, rows], kv_held[dp, rows]).astype(
                jnp.bfloat16
            )

        by_rows(kv_held.shape[1], add)
        return carry

    lax.fori_loop(0, n_dp, pair_up, 0)
    sums.start(c_kv)
    pump(1)
    back.near(0).wait_recv()
    sum_in = jnp.zeros((1, width), jnp.float32)
    for p, piece in enumerate(pieces):
        rows = pl.ds(*piece)
        back.far(p).wait_recv()
        total = add_up(parts[at.t, rows], held[0, rows]) + come[rows].astype(jnp.float32)
        grad_norm, term = norm_back(hidden[rows].astype(jnp.float32), gain(0), total)
        hidden_out[rows] = dh[rows] + grad_norm
        sum_in += column_sum(term)
    terms[0:1, :] = sum_in

    pool_t[at.t] = terms[...].astype(jnp.bfloat16)
    over_t = [
        send_to(where, pool_t.at[at.t], pool_t.at[at.t], ts.at[j], tr.at[j])
        for j, where in enumerate(others)
    ]
    for copy in over_t:
        copy.start()
    pump(2)
    for copy in over_t:
        copy.wait()
    total = pool_t[0].astype(jnp.float32)
    for t in range(1, n_tensor):
        total = total + pool_t[t].astype(jnp.float32)
    pool_r[at.rest] = total.astype(jnp.bfloat16)
    over_r = [
        send_to(at.rest_at[r], pool_r.at[at.rest], pool_r.at[at.rest], us.at[r], ur.at[r])
        for r in range(1, at.n_rest)
    ]
    for copy in over_r:
        copy.start()
    pump(len(steps))
    for copy in over_r:
        copy.wait()
    total = pool_r[0].astype(jnp.float32)
    for r in range(1, at.n_rest):
        total = total + pool_r[r].astype(jnp.float32)
    pool_z[at.line] = total.astype(jnp.bfloat16)
    over_z = [
        send_to(at.line_at[k], pool_z.at[at.line], pool_z.at[at.line], vs.at[k], vr.at[k])
        for k in (1, 2, 3)
    ]
    for copy in over_z:
        copy.start()
    for c in (c_wo, c_wq, c_kv):
        for k in sums.turns:
            sums.add(c, k)
    half_width = ffn.shape[-1]
    for c in range(n_ffn):
        sums.arrive(c)

        def finish(first, own=ffn_in.at[c, 0, 0], far=ffn_far.at[c], target=ffn_out.at[c]):
            def put(rows):
                same = add_up(own[rows], far[1, rows])
                cross = add_up(far[0, rows], far[2, rows])
                low, high = (same, cross) if first else (cross, same)
                target[rows, :half_width] = low
                target[rows, half_width:] = high[:, : target.shape[-1] - half_width]

            by_rows(own.shape[0], put)

        @pl.when(at.half == 0)
        def _(finish=finish):
            finish(True)

        @pl.when(at.half == 1)
        def _(finish=finish):
            finish(False)

    for copy in over_z:
        copy.wait()
    gains_out[...] = add_up(pool_z[0], pool_z[1]) + add_up(pool_z[2], pool_z[3])
    sums.arrive(c_wo)
    wo_out[...] = add_up(wo_in[0, 0], wo_far[0]) + add_up(wo_far[1], wo_far[2])
    sums.arrive(c_wq)
    wq_out[...] = add_up(wq_in[0, 0], wq_far[0]) + add_up(wq_far[1], wq_far[2])
    sums.arrive(c_kv)
    kv_pool[0] = (add_up(kv_in[0, 0], kv_far[0]) + add_up(kv_far[1], kv_far[2])).astype(jnp.bfloat16)
    kv_side = send_to(at.side, kv_pool.at[0], kv_pool.at[1], ks.at[1], kr.at[1])
    kv_side.start()
    kv_side.wait()
    kv_out[at.core] = add_up(kv_pool[0], kv_pool[1])
    give = send_to(at.mate, kv_out.at[at.core], kv_out.at[at.core], ks.at[2], kr.at[2])
    give.start()
    give.wait()
    for c in range(n_ffn + 3):
        sums.finish(c)
    bring.finish()
    back.finish()


def backward(
    n_dp, hidden, cot, back_rows, h_rows, u_rows, term_out, gains, head_gains, wq, wk, wv, wo,
    cosine, sine, seg_ids, a_all, q_raw, k_raw, q_rot, k_rot, v_all, lse, ctx, ffn, columns, ident,
):
    size, width = hidden.shape
    n_tensor = seg_ids.shape[0] // size
    n_ffn, _, dr, half_width = ffn.shape
    n_rest = n_dp // 4
    head = wq.shape[1]
    pieces = row_pieces(size, 10)
    count = len(pieces)
    vmem = pl.BlockSpec(memory_space=pltpu.VMEM)
    blocked = (n_tensor, size)

    def out(*dims):
        return jax.ShapeDtypeStruct(dims, jnp.float32)

    def low(*dims):
        return pltpu.VMEM(dims, jnp.bfloat16)

    def full(*dims):
        return pltpu.VMEM(dims, jnp.float32)

    def dma(*dims):
        return pltpu.SemaphoreType.DMA(dims)

    total = n_ffn + 3
    rows16 = -(-6 // SUBLANES) * SUBLANES
    return pl.pallas_call(
        functools.partial(backward_body, n_dp, pieces),
        out_shape=[
            out(size, width), out(rows16, width), out(dr, head), out(dr, head), out(2, dr, head),
            out(n_ffn, dr, columns),
        ],
        in_specs=[vmem] * 24 + [pl.BlockSpec(memory_space=pl.ANY)],
        out_specs=[vmem] * 6,
        scratch_shapes=[
            full(size, width), low(size, width), low(*blocked, width), low(*blocked, width),
            low(2, size, width), low(size, width), low(*blocked, head),
            full(n_tensor * size, head), full(n_tensor * size, head),
            low(*blocked, head), low(*blocked, head), low(*blocked, head), full(width, head),
            low(n_dp, dr, head), low(n_dp, dr, head), low(2, n_dp, dr, head), low(n_dp, dr, head),
            low(n_ffn, 4, dr, half_width),
            low(4, n_rest - 1, dr, head), low(4, n_rest - 1, dr, head), low(4, n_rest - 1, dr, head),
            low(n_ffn, 4, n_rest - 1, dr, half_width),
            low(3, dr, head), low(3, dr, head), low(3, dr, head), low(n_ffn, 3, dr, half_width),
            low(2, dr, head), full(rows16, width), low(n_tensor, rows16, width),
            low(n_rest, rows16, width), low(4, rows16, width),
            dma(n_ffn, 4), dma(total, 4, n_rest), dma(total, 4, n_rest), dma(total, 4), dma(total, 4),
            dma(3), dma(3), dma(count), dma(count), dma(count + 1), dma(count + 1),
            dma(2), dma(2), dma(count), dma(count),
            dma(3), dma(3), dma(n_rest), dma(n_rest), dma(4), dma(4),
        ],
        compiler_params=pltpu.CompilerParams(
            collective_id=ident, has_side_effects=True, vmem_limit_bytes=60 * MIB
        ),
        name="backward",
    )(
        hidden, cot, back_rows, h_rows, u_rows, term_out, gains, head_gains, wq, wk, wv, wo,
        cosine.reshape(*blocked, -1), sine.reshape(*blocked, -1),
        seg_ids.reshape(*blocked, 1), seg_ids.reshape(1, -1),
        a_all, q_raw, k_raw, q_rot, k_rot, v_all, lse, ctx, ffn,
    )


class Spread:
    def __init__(self, at, source, place, own_sem, zs, zr, rs, rr):
        self.at, self.source, self.place = at, source, place
        self.own_sem, self.zs, self.zr, self.rs, self.rr = own_sem, zs, zr, rs, rr

    def along(self, c, k):
        at = self.at
        return send_to(
            at.line_at[k], self.source(c, k), self.place(c, at.dp), self.zs.at[c, k], self.zr.at[c, k]
        )

    def across(self, c, k, r):
        at = self.at
        spot = self.place(c, at.line_dp[k])
        source = self.source(c, 0) if k == 0 else spot
        return send_to(at.rest_at[r], source, spot, self.rs.at[c, k, r], self.rr.at[c, k, r])

    def own(self, c):
        return pltpu.make_async_copy(
            self.source(c, 0), self.place(c, self.at.dp), self.own_sem.at[c]
        )

    def launch(self, c):
        inner = (self.at.line + 1) // 2 == 1

        @pl.when(inner)
        def _():
            for k in (3, 1, 2):
                self.along(c, k).start()

        @pl.when(jnp.logical_not(inner))
        def _():
            for k in (1, 2, 3):
                self.along(c, k).start()

        for r in range(1, self.at.n_rest):
            self.across(c, 0, r).start()
        self.own(c).start()

    def forward(self, c):
        for k in (1, 3, 2):
            self.along(c, k).wait_recv()
            for r in range(1, self.at.n_rest):
                self.across(c, k, r).start()

    def arrived(self, c):
        self.own(c).wait()
        for k in range(4):
            for r in range(1, self.at.n_rest):
                self.across(c, k, r).wait_recv()

    def finish(self, c):
        for k in range(4):
            for r in range(1, self.at.n_rest):
                self.across(c, k, r).wait_send()
            if k:
                self.along(c, k).wait_send()


class Scatter8:
    def __init__(self, at, pieces, parts, held, come, last, ms, mr, fs, fr, ls, lr):
        self.at, self.pieces, self.parts, self.held = at, pieces, parts, held
        self.come, self.last = come, last
        self.ms, self.mr, self.fs, self.fr, self.ls, self.lr = ms, mr, fs, fr, ls, lr
        half, other = at.half, 1 - at.half
        self.z = (half, half, other, other)
        self.x = (at.x, 1 - at.x, at.x, 1 - at.x)
        self.mine_t = (at.t, at.t_side, at.t, at.t_side)
        self.mate_t = (at.t_mate, at.t_side_mate, at.t_mate, at.t_side_mate)

    def near(self, k):
        return send_to(
            self.at.mate, self.parts.at[self.z[k], self.mate_t[k]], self.held.at[k],
            self.ms.at[k], self.mr.at[k],
        )

    def first(self, j, p):
        rows = pl.ds(*self.pieces[p])
        where, blocks = (self.at.side, (1, 3)) if p % 2 == 0 else (self.at.pair, (2, 3))
        return send_to(
            where, self.held.at[blocks[j], rows], self.come.at[j, rows],
            self.fs.at[j, p], self.fr.at[j, p],
        )

    def second(self, p):
        rows = pl.ds(*self.pieces[p])
        where, block = (self.at.pair, 2) if p % 2 == 0 else (self.at.side, 1)
        return send_to(
            where, self.held.at[block, rows], self.last.at[rows], self.ls.at[p], self.lr.at[p]
        )

    def combine(self, k):
        self.near(k).wait_recv()
        for p, piece in enumerate(self.pieces):
            rows = pl.ds(*piece)
            self.held[k, rows] = add_up(
                self.parts[self.z[k], self.mine_t[k], rows], self.held[k, rows]
            ).astype(jnp.bfloat16)
            if k == 3:
                self.first(1, p).start()
            elif k == 1 and p % 2 == 0 or k == 2 and p % 2 == 1:
                self.first(0, p).start()

    def relay(self):
        for p, piece in enumerate(self.pieces):
            rows = pl.ds(*piece)
            keep = 2 if p % 2 == 0 else 1
            self.first(1, p).wait_recv()
            self.held[keep, rows] = add_up(self.held[keep, rows], self.come[1, rows]).astype(
                jnp.bfloat16
            )
            self.second(p).start()

    def result(self, p):
        rows = pl.ds(*self.pieces[p])
        self.first(0, p).wait_recv()
        self.second(p).wait_recv()
        return add_up(self.held[0, rows], self.come[0, rows]) + self.last[rows].astype(jnp.float32)

    def finish(self):
        for k in range(4):
            self.near(k).wait_send()
        for p in range(len(self.pieces)):
            self.first(0, p).wait_send()
            self.first(1, p).wait_send()
            self.second(p).wait_send()


GAINS, KV, WQ, WO, GATE, UP, DOWN = range(7)


def layer_body(n_dp, pieces, names, *refs):
    s = types.SimpleNamespace(**dict(zip(names, refs, strict=True)))
    hidden, cot, ffn = s.hidden, s.cot, s.ffn
    cosine, sine, seg_col = s.cosine, s.sine, s.seg_col
    at = Spot(n_dp)
    others = [at.mate, at.side, {"tensor": at.t_side_mate}]
    meet(others + at.line_at[1:] + at.rest_at[1:])
    halves = (at.half, 1 - at.half, at.half, 1 - at.half)
    size, width = hidden.shape
    dr, wide = ffn.shape[2:]
    n_tensor, _, head = s.q_raw.shape
    factor = HD ** (-0.5)
    a_all, q_raw, k_raw, q_rot, k_rot = (s.a_all, s.q_raw, s.k_raw, s.q_rot, s.k_rot)
    v_all, lse, ctx, u_rows, h_rows = (s.v_all, s.lse, s.ctx, s.u_rows, s.h_rows)
    kv_all, wq, wo, ffn_all = s.kv_all, s.wq_all, s.wo_all, s.ffn_all

    def rows_of(dp):
        return pl.ds(pl.multiple_of(dp * dr, SUBLANES), dr)

    def source(c, k):
        if c == KV:
            return s.kv.at[at.core]
        if c < GATE:
            return {GAINS: s.gains, WQ: s.wq, WO: s.wo}[c]
        return ffn.at[halves[k], c - GATE]

    def place(c, dp):
        if c == GAINS:
            return s.gains_all.at[dp]
        if c == KV:
            return kv_all.at[at.core, rows_of(dp)]
        if c < GATE:
            return (wq if c == WQ else wo).at[rows_of(dp)]
        return ffn_all.at[c - GATE, rows_of(dp)]

    load = Spread(at, source, place, s.own_sem, s.lzs, s.lzr, s.lrs, s.lrr)
    packed = s.packed
    packed[...] = jnp.zeros_like(packed)
    packed[:4, : s.gains_in.shape[1]] = s.gains_in[...].astype(jnp.float32)
    packed[4:6, : s.head_in.shape[1]] = s.head_in[...].astype(jnp.float32)
    s.kv[0] = s.w_key[...]
    s.kv[1] = s.w_value[...]
    s.gains[...] = packed[...].astype(jnp.bfloat16)
    for c in (GAINS, KV, WQ, WO, GATE):
        load.launch(c)
    seg_row = s.token_rows[0:1, :].astype(jnp.float32)
    pos_row = s.token_rows[1:2, :].astype(jnp.float32)
    for t in range(n_tensor):
        shape = (size, seg_row.shape[1])
        row = lax.broadcasted_iota(jnp.int32, shape, 0) + t * size
        here = row == lax.broadcasted_iota(jnp.int32, shape, 1)
        seg_col[t] = jnp.sum(jnp.where(here, seg_row, 0.0), axis=1, keepdims=True)
        column = jnp.sum(jnp.where(here, pos_row, 0.0), axis=1, keepdims=True)
        angles = column * s.frequency[...]
        cosine[t] = jnp.cos(angles)
        sine[t] = jnp.sin(angles)

    load.forward(GAINS)
    load.arrived(GAINS)
    gains, head_gains = s.wide_gains, s.head_gains
    g_width, g_head = width // n_dp, head // n_dp
    for i in range(n_dp):
        block = s.gains_all[i].astype(jnp.float32)
        gains[:, i * g_width : (i + 1) * g_width] = block[:, :g_width]
        head_gains[:, i * g_head : (i + 1) * g_head] = block[:, :g_head]

    def gain(row):
        return gains[row : row + 1, :]

    q_gain, k_gain = head_gains[4:5, :], head_gains[5:6, :]

    def column_sum(values):
        return jnp.sum(values, axis=0, keepdims=True)

    bring = Gather4(at, pieces, s.a_own, a_all, s.g1xs, s.g1xr, s.g1ms, s.g1mr)
    for piece in pieces:
        rows = pl.ds(*piece)
        s.a_own[rows] = apply_norm(hidden[rows].astype(jnp.float32), gain(0)).astype(jnp.bfloat16)
    bring.start()
    a_all[at.t] = s.a_own[...]
    bring.pass_on()
    load.forward(KV)
    load.forward(WQ)
    load.launch(UP)
    bring.near_own().wait_recv()
    bring.all_here()
    load.arrived(KV)
    share = send_to(at.mate, kv_all.at[at.core], kv_all.at[at.core], s.ks.at[3], s.kr.at[3])
    share.start()
    load.forward(WO)

    def project_q(t):
        q = dot(a_all[t], wq[...])
        q_raw[t] = q
        q_rot[t] = turn(apply_norm(q, q_gain), cosine[t], sine[t]).astype(jnp.bfloat16)

    def project_kv(t):
        rows = pl.ds(t * size, size)
        k = dot(a_all[t], kv_all[0])
        k_raw[t] = k
        k_rot[rows] = turn(apply_norm(k, k_gain), cosine[t], sine[t]).astype(jnp.bfloat16)
        v_all[rows] = dot(a_all[t], kv_all[1]).astype(jnp.bfloat16)

    share.wait()
    for t in range(n_tensor):
        project_kv(t)
    load.arrived(WQ)
    for t in range(n_tensor):
        project_q(t)
    load.arrived(WO)

    def allowed_pairs(t, shape):
        row = lax.broadcasted_iota(jnp.int32, shape, 0) + t * size
        behind = row - lax.broadcasted_iota(jnp.int32, shape, 1)
        return (seg_col[t] == seg_row) & (behind >= 0) & (behind < WINDOW)

    parts8 = s.parts8
    parts4 = parts8.at[0]

    def attend(t):
        scores = contract_cols(q_rot[t], k_rot[...]) * factor
        weights = jnp.where(allowed_pairs(t, scores.shape), jnp.exp(scores), 0.0)
        total = jnp.sum(weights, axis=-1, keepdims=True)
        lse[t] = jnp.log(total)
        mixed = dot((weights / total).astype(jnp.bfloat16), v_all[...]).astype(jnp.bfloat16)
        ctx[t] = mixed
        parts4[t] = contract_cols(mixed, wo[...]).astype(jnp.bfloat16)

    back = Scatter4(
        at, pieces, parts4, s.held4, s.come4, s.s1ms, s.s1mr, s.s1fs, s.s1fr
    )
    attend(at.t_side_mate)
    back.near(1).start()
    attend(at.t_side)
    back.send_side()
    attend(at.t_mate)
    back.near(0).start()
    attend(at.t)
    load.launch(DOWN)
    load.forward(GATE)
    back.result(u_rows)
    spread = Gather8(
        at, pieces, s.c_own, s.c_all,
        s.x1s, s.x1r, s.z1s, s.z1r, s.d1s, s.d1r, s.m1s, s.m1r,
    )
    for p, piece in enumerate(pieces):
        rows = pl.ds(*piece)
        total = hidden[rows].astype(jnp.float32) + apply_norm(u_rows[rows], gain(1))
        h_rows[rows] = total
        s.c_own[rows] = apply_norm(total, gain(2)).astype(jnp.bfloat16)
        spread.start(p)
    c_all = s.c_all
    c_all[at.half, at.t] = s.c_own[...]
    spread.pass_x()
    load.forward(UP)
    spread.pass_z()
    spread.pass_last()
    for k in range(4):
        spread.here(k)
    back.finish()
    bring.finish()
    load.arrived(GATE)
    load.arrived(UP)
    for c in (GAINS, KV, WQ, WO):
        load.finish(c)
    spread.finish()

    fm, fa, fb = s.fm, s.fa, s.fb
    double = 2 * size
    cuts = [(0, 4 * LANES), (4 * LANES, wide)] if wide > 4 * LANES else [(0, wide)]

    def hidden_units(j, carry):
        z = j // 2
        x = j - 2 * z
        rows = pl.ds(pl.multiple_of(j * double, SUBLANES), double)
        block = c_all[z, pl.ds(2 * x, 2)].reshape(double, width)
        for low, high in cuts:
            g = dot(block, ffn_all[0, :, low:high])
            r = dot(block, ffn_all[1, :, low:high])
            square = g * g
            bend = jnp.tanh(GELU_SCALE * g * (1.0 + GELU_CUBE * square))
            rise = 0.5 * (1.0 + bend)
            value = g * rise
            slope = rise + 0.5 * g * (1.0 - bend * bend) * (
                GELU_SCALE * (1.0 + 3.0 * GELU_CUBE * square)
            )
            fm[rows, low:high] = (value * r).astype(jnp.bfloat16)
            fa[rows, low:high] = (r * slope).astype(jnp.bfloat16)
            fb[rows, low:high] = value.astype(jnp.bfloat16)
        return carry

    lax.fori_loop(0, 4, hidden_units, 0)
    load.forward(DOWN)
    load.arrived(DOWN)

    held8, come8, last8 = s.held8, s.come8, s.last8
    order = (3, 1, 2, 0)

    def block_rows(scatter, k):
        first = (2 * scatter.z[k] + scatter.x[k]) * double
        return pl.ds(pl.multiple_of(first, SUBLANES), double)

    def sum8(scatter, part):
        before = None
        for k in order:
            value = part(block_rows(scatter, k)).astype(jnp.bfloat16)
            parts8[scatter.z[k], pl.ds(2 * scatter.x[k], 2)] = value.reshape(2, size, width)
            scatter.near(k).start()
            if before is not None:
                scatter.combine(before)
            before = k
        scatter.combine(before)

    first = Scatter8(
        at, pieces, parts8, held8, come8, last8,
        s.e1ms, s.e1mr, s.e1fs, s.e1fr, s.e1ls, s.e1lr,
    )
    sum8(first, lambda rows: contract_cols(fm[rows], ffn_all[2]))
    first.relay()
    df_own, df_all = s.df_own, s.df_all
    spread = Gather8(
        at, pieces, df_own, df_all,
        s.x2s, s.x2r, s.z2s, s.z2r, s.d2s, s.d2r, s.m2s, s.m2r,
    )
    terms = s.terms
    terms[...] = jnp.zeros_like(terms)
    sum_out = jnp.zeros((1, width), jnp.float32)
    for p, piece in enumerate(pieces):
        rows = pl.ds(*piece)
        down = first.result(p)
        s.out_rows[rows] = (h_rows[rows] + apply_norm(down, gain(3))).astype(jnp.bfloat16)
        grad, term = norm_back(down, gain(3), cot[rows].astype(jnp.float32))
        sum_out += column_sum(term)
        df_own[rows] = grad.astype(jnp.bfloat16)
        spread.start(p)
    terms[3:4, :] = sum_out
    df_all[at.half, at.t] = df_own[...]
    first.finish()
    load.finish(GATE)
    load.finish(UP)
    load.finish(DOWN)

    def units_back(k):
        rows = block_rows(first, k)
        block = df_all[first.z[k], pl.ds(2 * first.x[k], 2)].reshape(double, width)
        for low, high in cuts:
            dm = dot(block, ffn_all[2, :, low:high])
            fa[rows, low:high] = (dm * fa[rows, low:high].astype(jnp.float32)).astype(jnp.bfloat16)
            fb[rows, low:high] = (dm * fb[rows, low:high].astype(jnp.float32)).astype(jnp.bfloat16)

    spread.here(0)
    units_back(0)
    spread.pass_on()
    spread.here(1)
    units_back(1)
    spread.here(2)
    units_back(2)
    spread.pass_last()
    spread.here(3)

    dwd = s.dwd
    tile = width // 3 if width % (3 * LANES) == 0 else width

    def ffn_grad(target, left, right):
        def one(i, carry):
            cols = pl.ds(pl.multiple_of(i * tile, LANES), tile)
            block = left[:, :, :, cols].reshape(4 * double, tile)
            value = contract_rows(block, right[...]).astype(jnp.bfloat16)
            target[pl.ds(pl.multiple_of(i * tile, SUBLANES), tile)] = value
            return carry

        lax.fori_loop(0, width // tile, one, 0)

    def flat(ref):
        return lambda dp: ref.at[rows_of(dp)]

    def own_flat(ref):
        return lambda k: ref.at[rows_of(at.line_dp[k])]

    dwg, dwu = fm, ffn_all.at[2]
    wo_part, wq_part, kv_part, kv_held = (s.wo_part, s.wq_part, s.kv_part, s.kv_held)
    ffn_in, ffn_far = s.ffn_in, s.ffn_far
    moved = (dwd, dwg, dwu, wo_part, wq_part, kv_held)
    n_ffn = 3
    c_wo, c_wq, c_kv = 3, 4, 5
    sums = Sums(
        at, [flat(ref) for ref in moved], [own_flat(ref) for ref in moved],
        [ffn_in.at[c] for c in range(n_ffn)] + [s.wo_in, s.wq_in, s.kv_in],
        [ffn_far.at[c] for c in range(n_ffn)] + [s.wo_far, s.wq_far, s.kv_far],
        s.rs, s.rr, s.zs, s.zr,
    )
    steps = [(c, k) for c in range(n_ffn) for k in sums.turns]

    def pump(count):
        for _ in range(count):
            if steps:
                sums.add(*steps.pop(0))

    ffn_grad(dwd, df_all, fm)
    sums.start(0)
    units_back(3)
    second = Scatter8(
        at, pieces, parts8, held8, come8, last8,
        s.e2ms, s.e2mr, s.e2fs, s.e2fr, s.e2ls, s.e2lr,
    )
    sum8(
        second,
        lambda rows: contract_cols(fa[rows], ffn_all[0]) + contract_cols(fb[rows], ffn_all[1]),
    )
    ffn_grad(dwg, c_all, fa)
    sums.start(1)
    second.relay()
    pump(2)
    ffn_grad(dwu, c_all, fb)
    sums.start(2)
    pump(1)
    spread.finish()

    dh, du_own, du_all = s.dh, s.du_own, s.du_all
    bring = Gather4(at, pieces, du_own, du_all, s.g2xs, s.g2xr, s.g2ms, s.g2mr)
    sum_ffn = jnp.zeros((1, width), jnp.float32)
    sum_attn = jnp.zeros((1, width), jnp.float32)
    for p, piece in enumerate(pieces):
        rows = pl.ds(*piece)
        grad_norm, term = norm_back(h_rows[rows], gain(2), second.result(p))
        sum_ffn += column_sum(term)
        total = cot[rows].astype(jnp.float32) + grad_norm
        dh[rows] = total
        grad_u, term = norm_back(u_rows[rows], gain(1), total)
        sum_attn += column_sum(term)
        du_own[rows] = grad_u.astype(jnp.bfloat16)
        bring.over_x(p).start()
    terms[1:2, :] = sum_attn
    terms[2:3, :] = sum_ffn
    bring.near_own().start()
    du_all[at.t] = du_own[...]
    second.finish()
    dctx = s.dctx

    def back_ctx(t):
        dctx[t] = dot(du_all[t], wo[...]).astype(jnp.bfloat16)

    back_ctx(at.t)
    bring.near_own().wait_recv()
    back_ctx(at.t_mate)
    bring.pass_on()
    pump(2)
    back_ctx(at.t_side)
    bring.all_here()
    back_ctx(at.t_side_mate)

    def weight_grad(target, left, right):
        value = contract_rows(
            left[...].reshape(n_tensor * size, width), right[...].reshape(n_tensor * size, head)
        )
        target[...] = value.astype(jnp.bfloat16)

    weight_grad(wo_part, du_all, ctx)
    sums.start(c_wo)
    dq_low, dk_low, dv_low, dv, dk = (s.dq_low, s.dk_low, s.dv_low, s.dv, s.dk)

    def attend_back(t):
        scores = contract_cols(q_rot[t], k_rot[...]) * factor
        probs = jnp.where(allowed_pairs(t, scores.shape), jnp.exp(scores - lse[t]), 0.0)
        grad_probs = contract_cols(dctx[t], v_all[...])
        delta = jnp.sum(probs * grad_probs, axis=-1, keepdims=True)
        grad_scores = (probs * (grad_probs - delta) * factor).astype(jnp.bfloat16)
        grad_q = dot(grad_scores, k_rot[...])
        low, term = norm_back(q_raw[t], q_gain, turn(grad_q, cosine[t], -sine[t]))
        dq_low[t] = low.astype(jnp.bfloat16)
        return (
            contract_rows(probs.astype(jnp.bfloat16), dctx[t]),
            contract_rows(grad_scores, q_rot[t]),
            column_sum(term),
        )

    add_v, add_k, sum_q = attend_back(0)
    dv[...] = add_v
    dk[...] = add_k
    for t in range(1, n_tensor):
        add_v, add_k, more = attend_back(t)
        dv[...] += add_v
        dk[...] += add_k
        sum_q += more
    sum_k = jnp.zeros((1, head), jnp.float32)
    for t in range(n_tensor):
        rows = pl.ds(t * size, size)
        low, term = norm_back(k_raw[t], k_gain, turn(dk[rows], cosine[t], -sine[t]))
        dk_low[t] = low.astype(jnp.bfloat16)
        sum_k += column_sum(term)
        dv_low[t] = dv[rows].astype(jnp.bfloat16)
    terms[4:5, :head] = sum_q
    terms[5:6, :head] = sum_k
    pump(1)

    def back_in(t):
        parts4[t] = (
            contract_cols(dq_low[t], wq[...])
            + contract_cols(dk_low[t], kv_all[0])
            + contract_cols(dv_low[t], kv_all[1])
        ).astype(jnp.bfloat16)

    held4, come4 = s.held4, s.come4
    back = Scatter4(at, pieces, parts4, held4, come4, s.s2ms, s.s2mr, s.s2fs, s.s2fr)
    back_in(at.t_side_mate)
    back.near(1).start()
    back_in(at.t_side)
    back.send_side()
    back_in(at.t_mate)
    back.near(0).start()
    back_in(at.t)
    pump(1)
    weight_grad(kv_part.at[0], a_all, dk_low)
    weight_grad(kv_part.at[1], a_all, dv_low)
    ks, kr = s.ks, s.kr
    mate_kv = send_to(at.mate, kv_part.at[1 - at.core], kv_held, ks.at[0], kr.at[0])
    mate_kv.start()
    weight_grad(wq_part, a_all, dq_low)
    sums.start(c_wq)
    mate_kv.wait()

    def pair_up(rows):
        kv_held[rows] = add_up(kv_part[at.core, rows], kv_held[rows]).astype(jnp.bfloat16)

    by_rows(kv_held.shape[0], pair_up)
    sums.start(c_kv)
    pump(1)
    back.near(0).wait_recv()
    sum_in = jnp.zeros((1, width), jnp.float32)
    for p, piece in enumerate(pieces):
        rows = pl.ds(*piece)
        back.far(p).wait_recv()
        total = add_up(parts4[at.t, rows], held4[0, rows]) + come4[rows].astype(jnp.float32)
        grad_norm, term = norm_back(hidden[rows].astype(jnp.float32), gain(0), total)
        s.hidden_out[rows] = dh[rows] + grad_norm
        sum_in += column_sum(term)
    terms[0:1, :] = sum_in

    pool_t, pool_r, pool_z = s.pool_t, s.pool_r, s.pool_z
    pool_t[at.t] = terms[...].astype(jnp.bfloat16)
    over_t = [
        send_to(where, pool_t.at[at.t], pool_t.at[at.t], s.ts.at[j], s.tr.at[j])
        for j, where in enumerate(others)
    ]
    for copy in over_t:
        copy.start()
    pump(1)
    for copy in over_t:
        copy.wait()
    total = pool_t[0].astype(jnp.float32)
    for t in range(1, n_tensor):
        total = total + pool_t[t].astype(jnp.float32)
    pool_r[at.rest] = total.astype(jnp.bfloat16)
    over_r = [
        send_to(at.rest_at[r], pool_r.at[at.rest], pool_r.at[at.rest], s.us.at[r], s.ur.at[r])
        for r in range(1, at.n_rest)
    ]
    for copy in over_r:
        copy.start()
    pump(len(steps))
    for copy in over_r:
        copy.wait()
    total = pool_r[0].astype(jnp.float32)
    for r in range(1, at.n_rest):
        total = total + pool_r[r].astype(jnp.float32)
    pool_z[at.line] = total.astype(jnp.bfloat16)
    over_z = [
        send_to(at.line_at[k], pool_z.at[at.line], pool_z.at[at.line], s.vs.at[k], s.vr.at[k])
        for k in (1, 2, 3)
    ]
    for copy in over_z:
        copy.start()
    for c in (c_wo, c_wq, c_kv):
        for k in sums.turns:
            sums.add(c, k)
    for c in range(n_ffn):
        sums.arrive(c)

        target = (s.gate_out, s.gate_out, s.up_out)[c]

        def put_all(low_first, own=ffn_in.at[c, 0, 0], far=ffn_far.at[c], target=target):
            def put(rows):
                same = add_up(own[rows], far[1, rows])
                cross = add_up(far[0, rows], far[2, rows])
                low, high = (same, cross) if low_first else (cross, same)
                target[rows, :wide] = low
                target[rows, wide:] = high[:, : target.shape[-1] - wide]

            by_rows(own.shape[0], put)

        @pl.when(at.half == 0)
        def _(put_all=put_all):
            put_all(True)

        @pl.when(at.half == 1)
        def _(put_all=put_all):
            put_all(False)

        if c == 0:
            s.down_out[...] = target[...].T

    for copy in over_z:
        copy.wait()
    s.gains_out[...] = add_up(pool_z[0], pool_z[1]) + add_up(pool_z[2], pool_z[3])

    def whole(c):
        sums.arrive(c)
        far = sums.distant[c]
        return add_up(sums.landed[c][0, 0], far[0]) + add_up(far[1], far[2])

    s.wo_out[...] = whole(c_wo).T
    s.wq_out[...] = whole(c_wq)
    kv_pool, kv_out = s.kv_pool, s.kv_out
    kv_pool[0] = whole(c_kv).astype(jnp.bfloat16)
    kv_side = send_to(at.side, kv_pool.at[0], kv_pool.at[1], ks.at[1], kr.at[1])
    kv_side.start()
    kv_side.wait()
    kv_out[at.core] = add_up(kv_pool[0], kv_pool[1])
    give = send_to(at.mate, kv_out.at[at.core], kv_out.at[at.core], ks.at[2], kr.at[2])
    give.start()
    give.wait()
    for c in range(n_ffn + 3):
        sums.finish(c)
    bring.finish()
    back.finish()


def layer(
    n_dp, hidden, cot, gains, wq, wo, w_key, w_value, frequency, seg_ids, positions, ffn, columns, ident):
    size, width = hidden.shape
    n_tensor = seg_ids.shape[0] // size
    dr, wide = ffn.shape[2:]
    n_rest = n_dp // 4
    head = wq.shape[1]
    pieces = row_pieces(size, 5)
    count = len(pieces)
    tokens = n_tensor * size
    blocked = (n_tensor, size)
    wider = -(-max(gain.shape[0] for gain in gains) // LANES) * LANES
    gain_block = (SUBLANES, wider)
    assert wq.shape[1] == head

    def out(*dims, kind=jnp.float32):
        return jax.ShapeDtypeStruct(dims, kind)

    def low(*dims):
        return pltpu.VMEM(dims, jnp.bfloat16)

    def full(*dims):
        return pltpu.VMEM(dims, jnp.float32)

    def dma(*dims):
        return pltpu.SemaphoreType.DMA(dims)

    inputs = dict(
        gains_in=jnp.stack(gains[:4]), head_in=jnp.stack(gains[4:]),
        hidden=hidden, cot=cot, wq=wq, wo=wo, w_key=w_key, w_value=w_value, frequency=frequency,
        token_rows=jnp.stack([seg_ids, positions]), ffn=ffn,
    )
    outputs = dict(
        out_rows=out(size, width, kind=jnp.bfloat16), hidden_out=out(size, width),
        gains_out=out(SUBLANES, width), wq_out=out(dr, head), wo_out=out(head, dr),
        kv_out=out(2, dr, head), gate_out=out(dr, columns), up_out=out(dr, columns),
        down_out=out(columns, dr),
    )
    scratch = dict(
        packed=full(*gain_block), kv=low(2, *w_key.shape), gains=low(*gain_block),
        cosine=full(*blocked, head // 2), sine=full(*blocked, head // 2), seg_col=full(*blocked, 1),
        gains_all=low(n_dp, *gain_block), kv_all=low(2, width, head), wq_all=low(width, head),
        wo_all=low(width, head), ffn_all=low(3, width, wide),
        wide_gains=full(gain_block[0], width), head_gains=full(gain_block[0], head),
        a_own=low(size, width), a_all=low(*blocked, width), q_raw=full(*blocked, head),
        k_raw=full(*blocked, head), q_rot=low(*blocked, head), k_rot=low(tokens, head),
        v_all=low(tokens, head), lse=full(*blocked, 1), ctx=low(*blocked, head),
        u_rows=full(size, width), h_rows=full(size, width),
        held4=low(2, size, width), come4=low(size, width),
        c_own=low(size, width), c_all=low(2, *blocked, width),
        fm=low(2 * tokens, wide), fa=low(2 * tokens, wide), fb=low(2 * tokens, wide),
        parts8=low(2, *blocked, width), held8=low(4, size, width), come8=low(2, size, width),
        last8=low(size, width), df_own=low(size, width), df_all=low(2, *blocked, width),
        dwd=low(width, wide), ffn_in=low(3, 4, n_rest - 1, dr, wide), ffn_far=low(3, 3, dr, wide),
        dh=full(size, width), du_own=low(size, width), du_all=low(*blocked, width),
        dctx=low(*blocked, head), dv=full(tokens, head), dk=full(tokens, head),
        dq_low=low(*blocked, head), dk_low=low(*blocked, head), dv_low=low(*blocked, head),
        wq_part=low(width, head), wo_part=low(width, head), kv_part=low(2, width, head),
        kv_held=low(width, head), wq_in=low(4, n_rest - 1, dr, head),
        wo_in=low(4, n_rest - 1, dr, head), kv_in=low(4, n_rest - 1, dr, head),
        wq_far=low(3, dr, head), wo_far=low(3, dr, head), kv_far=low(3, dr, head),
        kv_pool=low(2, dr, head), terms=full(SUBLANES, width), pool_t=low(n_tensor, SUBLANES, width),
        pool_r=low(n_rest, SUBLANES, width), pool_z=low(4, SUBLANES, width),
        own_sem=dma(7), lzs=dma(7, 4), lzr=dma(7, 4), lrs=dma(7, 4, n_rest), lrr=dma(7, 4, n_rest),
        rs=dma(6, 4, n_rest), rr=dma(6, 4, n_rest), zs=dma(6, 4), zr=dma(6, 4),
        ks=dma(4), kr=dma(4), ts=dma(3), tr=dma(3), us=dma(n_rest), ur=dma(n_rest), vs=dma(4), vr=dma(4),
    )
    for i in "12":
        for n in ("xs", "xr"):
            scratch[f"g{i}{n}"] = dma(count)
        for n in ("ms", "mr"):
            scratch[f"g{i}{n}"] = dma(count + 1)
            scratch[f"s{i}{n}"] = dma(2)
            scratch[f"e{i}{n}"] = dma(4)
            scratch[f"m{i}{n[1]}"] = dma(4, count)
        for n in ("fs", "fr"):
            scratch[f"s{i}{n}"] = dma(count)
            scratch[f"e{i}{n}"] = dma(2, count)
            scratch[f"e{i}l{n[1]}"] = dma(count)
            for a in "xzd":
                scratch[f"{a}{i}{n[1]}"] = dma(count)
    vmem = pl.BlockSpec(memory_space=pltpu.VMEM)
    names = (*inputs, *outputs, *scratch)
    return pl.pallas_call(
        functools.partial(layer_body, n_dp, pieces, names),
        out_shape=list(outputs.values()),
        in_specs=[vmem] * (len(inputs) - 1) + [pl.BlockSpec(memory_space=pl.ANY)],
        out_specs=[vmem] * len(outputs),
        scratch_shapes=list(scratch.values()),
        compiler_params=pltpu.CompilerParams(
            collective_id=ident, has_side_effects=True, vmem_limit_bytes=LAYER_VMEM
        ),
        name="layer",
    )(*inputs.values())


def pack_gains(blocks, width):
    n = blocks[0].shape[0]
    rows = [jnp.pad(block, ((0, 0), (0, width - block.shape[1]))) for block in blocks]
    packed = jnp.stack(rows, axis=1)
    return jnp.pad(packed, ((0, 0), (0, SUBLANES - len(blocks)), (0, 0)))


def stepwise(
    n_dp, hidden, cotangent, gains, w_query, w_output, w_kv, cosine, sine_table, segment_ids, ffn,
    columns,
):
    n_tensor = segment_ids.shape[0] // hidden.shape[0]
    wide = ffn.shape[-1]
    width = -(-max(gain.shape[0] for gain in gains) // LANES) * LANES
    gain_rows = pack_gains([gain[None] for gain in gains], width)[0]
    gains_all, wq_all, wo_all, kv_all = attention_weights(
        n_dp, gain_rows, w_query, w_output, w_kv, 0
    )
    full_in_gain, full_attn_gain, full_ffn_gain, full_out_gain, full_qgain, full_kgain = (
        gains_all[:, row, : gain.shape[0]].reshape(-1).astype(jnp.float32)
        for row, gain in enumerate(gains)
    )
    full_query, full_output = (block.reshape(-1, block.shape[-1]) for block in (wq_all, wo_all))
    full_key, full_value = (kv_all[i].reshape(-1, kv_all.shape[-1]) for i in range(2))
    wide_gains = jnp.stack([full_in_gain, full_attn_gain, full_ffn_gain, full_out_gain])
    head_gains = jnp.stack([full_qgain, full_kgain])
    (
        normed_in, query_raw, key_raw, query_rot, key_rot, value_rows, log_total, context,
        attn_rows, residual, ffn_in, ffn_all,
    ) = forward(
        n_dp,
        hidden,
        wide_gains,
        head_gains,
        full_query, full_key, full_value, full_output, cosine, sine_table, segment_ids, ffn, 1,
    )
    ffn_in = ffn_in.reshape(-1, ffn_in.shape[-1])
    full_gate, full_up, full_down = (ffn_all[i].reshape(-1, wide) for i in range(3))
    gate_pre = jnp.dot(ffn_in, full_gate, preferred_element_type=jnp.float32)
    up_pre = jnp.dot(ffn_in, full_up, preferred_element_type=jnp.float32)
    gelu_values, gelu_back = jax.vjp(gelu_tanh, gate_pre)
    mixed = (gelu_values * up_pre).astype(jnp.bfloat16)
    down_part = contract_cols(mixed, full_down)
    down_rows = scatter8(
        n_dp, down_part.astype(jnp.bfloat16).reshape(2, n_tensor, -1, down_part.shape[-1]), 4
    )
    output = (residual + apply_norm(down_rows, full_out_gain)).astype(jnp.bfloat16)
    cot_f = cotangent.astype(jnp.float32)
    grad_down, term_out = norm_back(down_rows, full_out_gain, cot_f)
    down_all = gather8(n_dp, grad_down.astype(jnp.bfloat16), 5).reshape(-1, grad_down.shape[-1])
    grad_wd = contract_rows(down_all, mixed)
    grad_mixed = jnp.dot(down_all, full_down, preferred_element_type=jnp.float32)
    gate_low = gelu_back(grad_mixed * up_pre)[0].astype(jnp.bfloat16)
    up_low = (grad_mixed * gelu_values).astype(jnp.bfloat16)
    grad_wg = contract_rows(ffn_in, gate_low)
    grad_wu = contract_rows(ffn_in, up_low)
    ffn_part = contract_cols(gate_low, full_gate) + contract_cols(up_low, full_up)
    ffn_back = scatter8(
        n_dp, ffn_part.astype(jnp.bfloat16).reshape(2, n_tensor, -1, ffn_part.shape[-1]), 6
    )
    grad_hidden, gain_sums, own_query, own_output, own_kv, own_ffn_weights = backward(
        n_dp, hidden, cotangent, ffn_back, residual, attn_rows,
        jnp.sum(term_out, axis=0, keepdims=True), wide_gains, head_gains,
        full_query, full_key, full_value, full_output, cosine, sine_table, segment_ids,
        normed_in, query_raw, key_raw, query_rot, key_rot, value_rows, log_total, context,
        jnp.stack(
            [
                grad.astype(jnp.bfloat16).reshape(n_dp, -1, grad.shape[-1])
                for grad in (grad_wd, grad_wg, grad_wu)
            ]
        ),
        columns,
        9,
    )
    return output, grad_hidden, gain_sums, own_query, own_output, own_kv, own_ffn_weights


def local(
    n_dp,
    n_tensor,
    hidden,
    in_gain,
    w_query,
    w_key,
    w_value,
    query_gain,
    key_gain,
    w_output,
    attn_gain,
    ffn_gain,
    w_gate,
    w_up,
    w_down,
    out_gain,
    cotangent,
    segment_ids,
    positions,
):
    gains = (in_gain, attn_gain, ffn_gain, out_gain, query_gain, key_gain)
    columns = w_gate.shape[1]
    wide = -(-columns // (2 * LANES)) * LANES
    ffn = jnp.stack([w_gate, w_up, w_down.T])
    ffn = jnp.pad(ffn, ((0, 0), (0, 0), (0, 2 * wide - columns)))
    ffn = jnp.stack([ffn[:, :, :wide], ffn[:, :, wide:]])
    if w_query.shape[0] % SUBLANES == 0:
        (
            output, grad_hidden, gain_sums, own_query, own_output, own_kv, own_gate, own_up, own_down,
        ) = layer(
            n_dp, hidden, cotangent, gains, w_query, w_output.T, w_key, w_value, rotary_frequency(HD)[None],
            segment_ids, positions, ffn, columns, 0,
        )
    else:
        cosine, sine_table = rotary_tables(positions, HD)
        output, grad_hidden, gain_sums, own_query, own_output, own_kv, own_ffn_weights = stepwise(
            n_dp, hidden, cotangent, gains, w_query, w_output.T, jnp.stack([w_key, w_value]), cosine, sine_table,
            segment_ids, ffn, columns,
        )
        own_output = own_output.T
        own_gate, own_up, own_down = own_ffn_weights[1], own_ffn_weights[2], own_ffn_weights[0].T
    place = lax.axis_index("dp")
    own_in, own_attn, own_ffn, own_out, own_q, own_k = (
        lax.dynamic_slice(gain_sums[row], (place * gain.shape[0],), gain.shape)
        for row, gain in enumerate(gains)
    )
    return (
        output,
        grad_hidden,
        own_in,
        own_query,
        own_kv[0],
        own_kv[1],
        own_q,
        own_k,
        own_output,
        own_attn,
        own_ffn,
        own_gate,
        own_up,
        own_down,
        own_out,
    )


def solution(mesh):
    placed = (
        P(("dp", "tensor"), None),
        P("dp"),
        P("dp", "tensor"),
        P("dp", None),
        P("dp", None),
        P("dp"),
        P("dp"),
        P("tensor", "dp"),
        P("dp"),
        P("dp"),
        P("dp", "tensor"),
        P("dp", "tensor"),
        P("tensor", "dp"),
        P("dp"),
        P(("dp", "tensor"), None),
        P("dp"),
        P("dp"),
    )
    return jax.shard_map(
        functools.partial(local, mesh.shape["dp"], mesh.shape["tensor"]),
        mesh=mesh,
        in_specs=placed,
        out_specs=(
            P(("dp", "tensor"), None),
            P(("dp", "tensor"), None),
            P("dp"),
            P("dp", "tensor"),
            P("dp", None),
            P("dp", None),
            P("dp"),
            P("dp"),
            P("tensor", "dp"),
            P("dp"),
            P("dp"),
            P("dp", "tensor"),
            P("dp", "tensor"),
            P("tensor", "dp"),
            P("dp"),
        ),
        check_vma=False,
    )
```
